32 devices in a mesh: seg: 4 (over y, x), doc: 8 (over z, core).
Axes of the slice: x: 2, y: 2, z: 4, core: 2. Of those that a mesh axis runs over, the one named last changes fastest.
Arguments:
- tokens: bfloat16 [16, 512, 768], P('doc', 'seg'), may hold values from -6 to 6
- new_doc: int32 [16], P('doc'), may hold values from 0 to 1, as said below
- valid_len: int32 [16], P('doc'), may hold values from 1 to 512, as said below
- mem_init: bfloat16 [16, 768], replicated, may hold values from -6 to 6
- query_proj: bfloat16 [768, 768], replicated, may hold values from -0.21875 to 0.21875
- query_bias: float32 [768], replicated, may hold values from -3 to 3
- key_proj: bfloat16 [768, 768], replicated, may hold values from -0.21875 to 0.21875
- value_proj: bfloat16 [768, 768], replicated, may hold values from -0.21875 to 0.21875
- value_bias: float32 [768], replicated, may hold values from -3 to 3
- output_proj: bfloat16 [768, 768], replicated, may hold values from -1.75 to 1.75
- output_bias: float32 [768], replicated, may hold values from -2 to 2
- attn_gain: float32 [768], replicated, may hold values from 0.5 to 1.5
- attn_shift: float32 [768], replicated, may hold values from -2 to 2
- expand_proj: bfloat16 [768, 3072], replicated, may hold values from -0.21875 to 0.21875
- expand_bias: float32 [3072], replicated, may hold values from -2 to 2
- reduce_proj: bfloat16 [3072, 768], replicated, may hold values from -0.109375 to 0.109375
- reduce_bias: float32 [768], replicated, may hold values from -2 to 2
- final_gain: float32 [768], replicated, may hold values from 0.5 to 1.5
- final_shift: float32 [768], replicated, may hold values from -2 to 2
- d_out: bfloat16 [16, 512, 768], P('doc', 'seg'), may hold values from -6 to 6
Outputs:
- layer_out: bfloat16 [16, 512, 768], P('doc', 'seg')
- grad_tokens: bfloat16 [16, 512, 768], P('doc', 'seg')
- grad_mem: float32 [16, 768], P(None, ('seg', 'doc'))
- grad_query_proj: float32 [768, 768], P(('seg', 'doc'))
- grad_query_bias: float32 [768], P(('seg', 'doc'))
- grad_key_proj: float32 [768, 768], P(('seg', 'doc'))
- grad_value_proj: float32 [768, 768], P(('seg', 'doc'))
- grad_value_bias: float32 [768], P(('seg', 'doc'))
- grad_output_proj: float32 [768, 768], P(('seg', 'doc'))
- grad_output_bias: float32 [768], P(('seg', 'doc'))
- grad_attn_gain: float32 [768], P(('seg', 'doc'))
- grad_attn_shift: float32 [768], P(('seg', 'doc'))
- grad_expand_proj: float32 [768, 3072], P(('seg', 'doc'))
- grad_expand_bias: float32 [3072], P(('seg', 'doc'))
- grad_reduce_proj: float32 [3072, 768], P(('seg', 'doc'))
- grad_reduce_bias: float32 [768], P(('seg', 'doc'))
- grad_final_gain: float32 [768], P(('seg', 'doc'))
- grad_final_shift: float32 [768], P(('seg', 'doc'))
The draws below stay inside these ranges and needn't reach their ends.
Inputs may be any that keep to these rules, and one draw needn't show every extreme that they name: `new_doc`: the first of every 2 consecutive segments starts a document. `valid_len`: 512 for every segment that is not the last of its document.
All inputs are finite; a program needn't handle non-finite values.
Results may differ from the reference program's by a relative error of at most 0.02.
Values may be sent and summed in bfloat16 or wider, within the bound.
No kernel may reach another device: no remote copies, remote signals or barrier semaphores. Data moves between devices by JAX's collectives and lax.ppermute only.
A program may use at most 192 MiB of HBM per device.

```python
import jax
import jax.numpy as jnp
from jax import lax

D = 768
HEADS = 12
HEAD_DIM = 64
FF = 3072
MEM = 16
SEG_LEN = 512
SLOTS = 2
DOC_SLOTS = 16
N_DOC = 8


def plan_draw(key):
    coin_flips = jax.random.randint(jax.random.fold_in(key, 101), (DOC_SLOTS,), 0, 2)
    places = jnp.arange(DOC_SLOTS, dtype=jnp.int32)
    fresh_flags = jnp.where(places % SLOTS == 0, 1, coin_flips)
    fresh_flags = jnp.where(places == 1, 0, fresh_flags)
    following = jnp.concatenate([fresh_flags[1:], jnp.ones((1,), jnp.int32)])
    closing = (following == 1) | (places % SLOTS == SLOTS - 1)
    lengths = jax.random.randint(jax.random.fold_in(key, 202), (DOC_SLOTS,), 1, SEG_LEN + 1)
    valid_rows = jnp.where(closing, lengths, SEG_LEN)
    valid_rows = jnp.where(places == SLOTS - 1, 1, valid_rows)
    return (fresh_flags.astype(jnp.int32), valid_rows.astype(jnp.int32))


def draw_new_doc(key, part):
    return plan_draw(key)[0]


def draw_valid_len(key, part):
    return plan_draw(key)[1]


def block_levels(own_key, dims, cuts, low, top_value):
    def one(dim, parts):
        draws = jax.random.uniform(jax.random.fold_in(jax.random.fold_in(own_key, 6), dim), (parts,), jnp.float32, low / len(cuts), top_value / len(cuts))
        return jnp.repeat(jnp.exp(draws), dims[dim] // parts).reshape((-1,) + (1,) * (len(dims) - dim - 1))

    loudness = one(*cuts[0])
    for cut in cuts[1:]:
        loudness = loudness * one(*cut)
    return loudness


def bell_draw(stream_key, extent, width, bound, split=(), kind=jnp.bfloat16):
    gain = block_levels(stream_key, extent, split, -0.22, 0.18) if split else 1.0
    values = jax.random.normal(stream_key, extent, jnp.float32) * width * gain
    return jnp.minimum(jnp.maximum(values, -bound), bound).astype(kind)


def setup_inputs(seed: int = 0) -> dict:
    streams_of = jax.random.split(jax.random.key(seed), 21)
    tokens = bell_draw(streams_of[0], (DOC_SLOTS, SEG_LEN, D), 1.0, 6.0, ((0, 8), (1, 4)))
    new_doc = draw_new_doc(jax.random.fold_in(streams_of[20], 71), 0)
    valid_len = draw_valid_len(jax.random.fold_in(streams_of[20], 71), 0)
    mem_init = bell_draw(streams_of[3], (MEM, D), 1.0, 6.0)
    query_proj = bell_draw(streams_of[4], (D, D), D ** -0.5, 0.21875)
    query_bias = bell_draw(streams_of[5], (D,), 0.5, 3.0, (), jnp.float32)
    key_proj = bell_draw(streams_of[6], (D, D), D ** -0.5, 0.21875)
    value_proj = bell_draw(streams_of[7], (D, D), D ** -0.5, 0.21875)
    value_bias = bell_draw(streams_of[8], (D,), 0.5, 3.0, (), jnp.float32)
    output_proj = bell_draw(streams_of[9], (D, D), (D // 64) ** -0.5, 1.75)
    output_bias = bell_draw(streams_of[10], (D,), 0.3, 2.0, (), jnp.float32)
    attn_gain = jnp.clip(1.0 + 0.1 * jax.random.normal(streams_of[11], (D,), jnp.float32), 0.5, 1.5)
    attn_shift = bell_draw(streams_of[12], (D,), 0.3, 2.0, (), jnp.float32)
    expand_proj = bell_draw(streams_of[13], (D, FF), D ** -0.5, 0.21875)
    expand_bias = bell_draw(streams_of[14], (FF,), 0.3, 2.0, (), jnp.float32)
    reduce_proj = bell_draw(streams_of[15], (FF, D), FF ** -0.5, 0.109375)
    reduce_bias = bell_draw(streams_of[16], (D,), 0.3, 2.0, (), jnp.float32)
    final_gain = jnp.clip(1.0 + 0.1 * jax.random.normal(streams_of[17], (D,), jnp.float32), 0.5, 1.5)
    final_shift = bell_draw(streams_of[18], (D,), 0.3, 2.0, (), jnp.float32)
    d_out = bell_draw(streams_of[19], (DOC_SLOTS, SEG_LEN, D), 1.0, 6.0, ((0, 8), (1, 4)))
    return {"tokens": tokens, "new_doc": new_doc, "valid_len": valid_len, "mem_init": mem_init, "query_proj": query_proj, "query_bias": query_bias, "key_proj": key_proj, "value_proj": value_proj, "value_bias": value_bias, "output_proj": output_proj, "output_bias": output_bias, "attn_gain": attn_gain, "attn_shift": attn_shift, "expand_proj": expand_proj, "expand_bias": expand_bias, "reduce_proj": reduce_proj, "reduce_bias": reduce_bias, "final_gain": final_gain, "final_shift": final_shift, "d_out": d_out}


EPS = 1e-12
HIGH = lax.Precision.HIGHEST

@jax.custom_vjp
def low(v):
    return lax.optimization_barrier(v.astype(jnp.bfloat16)).astype(jnp.float32)

@jax.custom_vjp
def low_back(v):
    return v

def low_keep(v):
    return (low(v), None)

def low_pass(kept, grad):
    return (grad,)

def back_keep(v):
    return (v, None)

def back_low(kept, grad):
    return (low(grad),)
low.defvjp(low_keep, low_pass)
low_back.defvjp(back_keep, back_low)

def norm_rows(hidden, scale_vec, shift_vec):
    center = hidden - lax.optimization_barrier(jnp.mean(hidden, axis=-1, keepdims=True))
    spread = lax.optimization_barrier(jnp.mean(center * center, axis=-1, keepdims=True))
    return center * lax.rsqrt(spread + EPS) * scale_vec + shift_vec

def matmul_high(left, right):
    return jnp.einsum('...d,de->...e', left, right, precision=HIGH)

def layer_rows(slot_rows, key_mask, params):
    query_proj, query_bias, key_proj, value_proj, value_bias, output_proj, output_bias, attn_gain, attn_shift, expand_proj, expand_bias, reduce_proj, reduce_bias, final_gain, final_shift = params
    batch_size = slot_rows.shape[0]
    row_count = slot_rows.shape[1]
    rows_low = low(slot_rows)
    query_heads = low_back(low(matmul_high(rows_low, query_proj) + query_bias)).reshape(batch_size, row_count, HEADS, HEAD_DIM)
    key_heads = low_back(low(matmul_high(rows_low, key_proj))).reshape(batch_size, row_count, HEADS, HEAD_DIM)
    value_heads = low_back(low(matmul_high(rows_low, value_proj) + value_bias)).reshape(batch_size, row_count, HEADS, HEAD_DIM)
    scores = low_back(jnp.einsum('brhd,bkhd->bhrk', query_heads, key_heads, precision=HIGH) * 0.125)
    scores = jnp.where(key_mask[:, None, None, :], scores, -1e+30)
    attn_probs = low(jax.nn.softmax(scores, axis=-1))
    mixed = jnp.einsum('bhrk,bkhd->brhd', attn_probs, value_heads, precision=HIGH).reshape(batch_size, row_count, D)
    mixed = low_back(low(mixed))
    attn_out = low_back(matmul_high(mixed, output_proj) + output_bias)
    normed = norm_rows(slot_rows + attn_out, attn_gain, attn_shift)
    pre_active = low_back(matmul_high(low(normed), expand_proj) + expand_bias)
    active = low(jax.nn.gelu(pre_active, approximate=False))
    branch = low_back(matmul_high(active, reduce_proj) + reduce_bias)
    return norm_rows(normed + branch, final_gain, final_shift)

def forward_all(token_rows, memory_start, new_doc, valid_len, params):
    slot_tokens = token_rows.reshape(N_DOC, SLOTS, SEG_LEN, D).transpose(1, 0, 2, 3)
    fresh_slots = new_doc.reshape(N_DOC, SLOTS).T
    valid_slots = valid_len.reshape(N_DOC, SLOTS).T
    places = jnp.arange(SEG_LEN, dtype=jnp.int32)

    def step_slot(memory, inputs):
        tokens_now, fresh_now, valid_now = inputs
        start_mem = jnp.where((fresh_now == 1)[:, None, None], memory_start[None], memory)
        slot_rows = jnp.concatenate([start_mem, tokens_now, start_mem], axis=1)
        always_on = jnp.ones((N_DOC, MEM), dtype=bool)
        text_mask = places[None, :] < valid_now[:, None]
        key_mask = jnp.concatenate([always_on, text_mask, always_on], axis=1)
        result = layer_rows(slot_rows, key_mask, params)
        return (result[:, MEM + SEG_LEN:], result[:, MEM:MEM + SEG_LEN])
    start_carry = jnp.zeros((N_DOC, MEM, D), memory_start.dtype)
    _, outputs = lax.scan(jax.checkpoint(step_slot), start_carry, (slot_tokens, fresh_slots, valid_slots))
    return outputs.transpose(1, 0, 2, 3).reshape(DOC_SLOTS, SEG_LEN, D)

def reference(tokens, new_doc, valid_len, mem_init, query_proj, query_bias, key_proj, value_proj, value_bias, output_proj, output_bias, attn_gain, attn_shift, expand_proj, expand_bias, reduce_proj, reduce_bias, final_gain, final_shift, d_out):
    weights = (query_proj, query_bias, key_proj, value_proj, value_bias, output_proj, output_bias, attn_gain, attn_shift, expand_proj, expand_bias, reduce_proj, reduce_bias, final_gain, final_shift)
    weights = tuple((entry.astype(jnp.float32) for entry in weights))

    def run_layer(token_rows, memory_start, *params):
        return forward_all(token_rows, memory_start, new_doc, valid_len, params)
    output, pull_back = jax.vjp(run_layer, tokens.astype(jnp.float32), mem_init.astype(jnp.float32), *weights)
    grads = pull_back(d_out.astype(jnp.float32))
    return (output.astype(jnp.bfloat16), grads[0].astype(jnp.bfloat16), grads[1], grads[2], grads[3], grads[4], grads[5], grads[6], grads[7], grads[8], grads[9], grads[10], grads[11], grads[12], grads[13], grads[14], grads[15], grads[16])
```

```python
import functools

import jax
import jax.numpy as jnp
from jax import lax
from jax.experimental import pallas as pl
from jax.experimental.pallas import tpu as pltpu
from jax.sharding import PartitionSpec as P

HEADS = 12


EPS = 1e-12
NEG_FILL = -1e30
F32 = jnp.float32
BF16 = jnp.bfloat16
NN = (((1,), (0,)), ((), ()))
NT = (((1,), (1,)), ((), ()))
TN = (((0,), (0,)), ((), ()))


def mm(left, right, dims=NN):
    return lax.dot_general(left, right, dims, preferred_element_type=F32)


def swap(block, axis, mask):
    return lax.ppermute(block, axis, [(i, i ^ mask) for i in range(lax.axis_size(axis))])


def pick(stack, index, axis=0):
    return lax.dynamic_index_in_dim(stack, index, axis, keepdims=False)


def whole_call(kernel, out_shape, n_in, smem_first=True):
    vmem = pl.BlockSpec(memory_space=pltpu.VMEM)
    in_specs = [pl.BlockSpec(memory_space=pltpu.SMEM)] if smem_first else []
    in_specs += [vmem] * (n_in - len(in_specs))
    return pl.pallas_call(
        kernel,
        out_shape=out_shape,
        in_specs=in_specs,
        out_specs=jax.tree.map(lambda _: vmem, out_shape),
        compiler_params=pltpu.CompilerParams(vmem_limit_bytes=56 << 20),
    )


def qkv_kernel(*refs, blocks):
    rows, wt_ref, bias_ref, out_ref = refs[:blocks], refs[blocks], refs[blocks + 1], refs[blocks + 2]
    size = rows[0].shape[0]
    for b in range(blocks):
        out_ref[b * size : (b + 1) * size, :] = (mm(rows[b][...], wt_ref[...], NT) + bias_ref[...]).astype(BF16)


def key_columns(meta_ref, blocks, size, mem):
    total = blocks * size + 2 * mem
    col = lax.broadcasted_iota(jnp.int32, (1, total), 1)
    place = col
    for b in range(blocks):
        inside = (col >= b * size) & (col < (b + 1) * size)
        place = jnp.where(inside, ((meta_ref[0] ^ b) - b) * size + col, place)
    return (place < meta_ref[1]) | (col >= blocks * size)


def attn_fwd_kernel(meta_ref, qkv_ref, mem_ref, wt_ref, bias_ref, *outs, blocks, heads, mem_queries):
    mix_refs, lse_ref, mem_out_ref = outs[:blocks], outs[blocks], outs[blocks + 1]
    size = qkv_ref.shape[0] // blocks
    mem = mem_ref.shape[0]
    width = qkv_ref.shape[1] // 3
    head_dim = width // heads
    mem_out_ref[...] = (mm(mem_ref[...], wt_ref[...], NT) + bias_ref[...]).astype(BF16)
    keep = key_columns(meta_ref, blocks, size, mem)
    for h in range(heads):
        lo, hi = h * head_dim, (h + 1) * head_dim
        mem_key = mem_out_ref[:, width + lo : width + hi]
        mem_value = mem_out_ref[:, 2 * width + lo : 2 * width + hi]
        key = jnp.concatenate([qkv_ref[:, width + lo : width + hi], mem_key, mem_key], axis=0)
        value = jnp.concatenate([qkv_ref[:, 2 * width + lo : 2 * width + hi], mem_value, mem_value], axis=0)

        def one(query):
            scores = jnp.where(keep, mm(query, key, NT) * 0.125, NEG_FILL)
            highest = jnp.max(scores, axis=-1, keepdims=True)
            weights = jnp.exp(scores - highest)
            total = jnp.sum(weights, axis=-1, keepdims=True)
            probs = (weights * (1.0 / total)).astype(BF16)
            return mm(probs, value).astype(BF16), highest + jnp.log(total)

        for b in range(blocks):
            mixed, lse = one(qkv_ref[b * size : (b + 1) * size, lo:hi])
            mix_refs[b][:size, lo:hi] = mixed
            lse_ref[b * size : (b + 1) * size, h : h + 1] = lse
        if mem_queries:
            mixed, lse = one(mem_out_ref[:, lo:hi])
            for b in range(blocks):
                mix_refs[b][size:, lo:hi] = mixed
            lse_ref[blocks * size : blocks * size + mem, h : h + 1] = lse


def attn_bwd_kernel(meta_ref, qkv_ref, mem_ref, lse_ref, *refs, blocks, heads, mem_queries):
    n_grad = blocks + (1 if mem_queries else 0)
    grad_refs, out_refs, mem_out_ref = refs[:n_grad], refs[n_grad : n_grad + blocks], refs[n_grad + blocks]
    size = qkv_ref.shape[0] // blocks
    mem = mem_ref.shape[0]
    width = qkv_ref.shape[1] // 3
    head_dim = width // heads
    keep = key_columns(meta_ref, blocks, size, mem)
    for h in range(heads):
        lo, hi = h * head_dim, (h + 1) * head_dim
        mem_key = mem_ref[:, width + lo : width + hi]
        mem_value = mem_ref[:, 2 * width + lo : 2 * width + hi]
        key = jnp.concatenate([qkv_ref[:, width + lo : width + hi], mem_key, mem_key], axis=0)
        value = jnp.concatenate([qkv_ref[:, 2 * width + lo : 2 * width + hi], mem_value, mem_value], axis=0)

        def one(query, grad, lse):
            scores = jnp.where(keep, mm(query, key, NT) * 0.125, NEG_FILL)
            probs = jnp.exp(scores - lse)
            grad_probs = mm(grad, value, NT)
            inner = jnp.sum(grad_probs * probs, axis=-1, keepdims=True)
            grad_scores = (probs * (grad_probs - inner)).astype(BF16)
            grad_query = (mm(grad_scores, key) * 0.125).astype(BF16)
            return grad_query, mm(grad_scores, query, TN), mm(probs.astype(BF16), grad, TN)

        grad_key = grad_value = None
        for b in range(n_grad):
            if b < blocks:
                query = qkv_ref[b * size : (b + 1) * size, lo:hi]
                lse = lse_ref[b * size : (b + 1) * size, h : h + 1]
            else:
                query = mem_ref[:, lo:hi]
                lse = lse_ref[blocks * size : blocks * size + mem, h : h + 1]
            grad_query, key_part, value_part = one(query, grad_refs[b][:, lo:hi], lse)
            grad_key = key_part if grad_key is None else grad_key + key_part
            grad_value = value_part if grad_value is None else grad_value + value_part
            if b < blocks:
                out_refs[b][:, lo:hi] = grad_query
            else:
                mem_out_ref[:, lo:hi] = grad_query
        if not mem_queries:
            mem_out_ref[:, lo:hi] = jnp.zeros((mem, head_dim), BF16)
        grad_key = (grad_key * 0.125).astype(BF16)
        grad_value = grad_value.astype(BF16)
        for b in range(blocks):
            out_refs[b][:, width + lo : width + hi] = grad_key[b * size : (b + 1) * size]
            out_refs[b][:, 2 * width + lo : 2 * width + hi] = grad_value[b * size : (b + 1) * size]
        mem_out_ref[:, width + lo : width + hi] = grad_key[blocks * size : blocks * size + mem]
        mem_out_ref[:, 2 * width + lo : 2 * width + hi] = grad_value[blocks * size : blocks * size + mem]


def norm_parts(hidden):
    center = hidden - jnp.mean(hidden, axis=-1, keepdims=True)
    inverse = lax.rsqrt(jnp.mean(center * center, axis=-1, keepdims=True) + EPS)
    return center * inverse, inverse


def norm_back(grad, gain, unit, inverse):
    scaled = grad * gain
    mean_scaled = jnp.mean(scaled, axis=-1, keepdims=True)
    mean_product = jnp.mean(scaled * unit, axis=-1, keepdims=True)
    return inverse * (scaled - mean_scaled - unit * mean_product)


def gelu_and_slope(pre):
    cdf = 0.5 * (1.0 + lax.erf(pre * (2.0**-0.5)))
    density = jnp.exp(-0.5 * pre * pre) * 0.3989422804014327
    return pre * cdf, cdf + pre * density


def rows_forward(hidden_in, mixed, w):
    unit_a, inverse_a = norm_parts(hidden_in + (mm(mixed, w["out"]) + w["out_b"]))
    normed = unit_a * w["attn_g"] + w["attn_s"]
    normed_low = normed.astype(BF16)
    active, slope = gelu_and_slope(mm(normed_low, w["exp"]) + w["exp_b"])
    active_low = active.astype(BF16)
    unit_f, inverse_f = norm_parts(normed + (mm(active_low, w["red"]) + w["red_b"]))
    result = unit_f * w["fin_g"] + w["fin_s"]
    return result, (mixed, unit_a, inverse_a, normed_low, slope, active_low, unit_f, inverse_f)


def rows_backward(grad, kept, w):
    mixed, unit_a, inverse_a, normed_low, slope, active_low, unit_f, inverse_f = kept
    grad_sum = norm_back(grad, w["fin_g"], unit_f, inverse_f)
    grad_branch = grad_sum.astype(BF16)
    grad_pre = (mm(grad_branch, w["red"], NT) * slope).astype(BF16)
    grad_normed = grad_sum + mm(grad_pre, w["exp"], NT)
    grad_hidden = norm_back(grad_normed, w["attn_g"], unit_a, inverse_a)
    grad_attn = grad_hidden.astype(BF16)
    grad_mixed = mm(grad_attn, w["out"], NT).astype(BF16)
    small = {
        "fin_g": jnp.sum(grad * unit_f, 0),
        "fin_s": jnp.sum(grad, 0),
        "red_b": jnp.sum(grad_branch.astype(F32), 0),
        "exp_b": jnp.sum(grad_pre.astype(F32), 0),
        "attn_g": jnp.sum(grad_normed * unit_a, 0),
        "attn_s": jnp.sum(grad_normed, 0),
        "out_b": jnp.sum(grad_attn.astype(F32), 0),
    }
    pairs = {"exp": (normed_low, grad_pre), "red": (active_low, grad_branch), "out": (mixed, grad_attn)}
    return grad_hidden, grad_mixed, small, pairs


def shards(
    tokens,
    new_doc,
    valid_len,
    mem_init,
    query_proj,
    query_bias,
    key_proj,
    value_proj,
    value_bias,
    output_proj,
    output_bias,
    attn_gain,
    attn_shift,
    expand_proj,
    expand_bias,
    reduce_proj,
    reduce_bias,
    final_gain,
    final_shift,
    d_out,
):
    slots, size, wide = tokens.shape
    assert slots == 2
    n_seg, n_doc = lax.axis_size("seg"), lax.axis_size("doc")
    n_pair = n_doc // 2
    hidden_units = expand_proj.shape[1]
    mem = mem_init.shape[0]
    width = wide // n_seg
    heads = HEADS // n_seg
    seg, doc = lax.axis_index("seg"), lax.axis_index("doc")
    core, pair = doc & 1, doc >> 1
    owner = (seg == 0).astype(F32)
    others = range(1, n_seg)

    rows = [[tokens[t]] + [swap(tokens[t], "seg", m) for m in others] for t in range(slots)]

    turned = jnp.stack([query_proj.T, key_proj.T, value_proj.T]).reshape(3, n_seg, width, wide)
    head_wt = [pick(turned, seg ^ m, 1).reshape(3 * width, wide) for m in range(n_seg)]
    out_rel = jnp.concatenate([pick(output_proj.reshape(n_seg, width, wide), seg ^ m) for m in range(n_seg)], 0)
    bias_own = jnp.concatenate(
        [
            pick(query_bias.reshape(n_seg, width), seg),
            jnp.zeros((width,), F32),
            pick(value_bias.reshape(n_seg, width), seg),
        ]
    )[None]
    w = {
        "out": out_rel,
        "out_b": output_bias,
        "attn_g": attn_gain,
        "attn_s": attn_shift,
        "exp": expand_proj,
        "exp_b": expand_bias,
        "red": reduce_proj,
        "red_b": reduce_bias,
        "fin_g": final_gain,
        "fin_s": final_shift,
    }
    meta = [jnp.stack([seg, valid_len[t]]).astype(jnp.int32) for t in range(slots)]
    all_rows = n_seg * size

    def project(t):
        return whole_call(
            functools.partial(qkv_kernel, blocks=n_seg),
            jax.ShapeDtypeStruct((all_rows, 3 * width), BF16),
            n_seg + 2,
            False,
        )(*rows[t], head_wt[0], bias_own)

    def attend(t, qkv, memory_low, mem_queries):
        size_out = size + (mem if mem_queries else 0)
        got = whole_call(
            functools.partial(attn_fwd_kernel, blocks=n_seg, heads=heads, mem_queries=mem_queries),
            [jax.ShapeDtypeStruct((size_out, width), BF16)] * n_seg
            + [jax.ShapeDtypeStruct((all_rows + mem, 128), F32), jax.ShapeDtypeStruct((mem, 3 * width), BF16)],
            5,
        )(meta[t], qkv, memory_low, head_wt[0], bias_own)
        return got[:n_seg], got[n_seg], got[n_seg + 1]

    def attend_back(t, qkv, qkv_mem, lse, grads):
        got = whole_call(
            functools.partial(attn_bwd_kernel, blocks=n_seg, heads=heads, mem_queries=len(grads) > n_seg),
            [jax.ShapeDtypeStruct((size, 3 * width), BF16)] * n_seg + [jax.ShapeDtypeStruct((mem, 3 * width), BF16)],
            4 + len(grads),
        )(meta[t], qkv, qkv_mem, lse, *grads)
        return got[:n_seg], got[n_seg]

    def trade(blocks):
        return [blocks[0]] + [swap(blocks[m], "seg", m) for m in others]

    mem_float = mem_init.astype(F32)
    qkv0 = project(0)
    mixed0, lse0, qkv_mem0 = attend(0, qkv0, mem_init, True)
    mixed0 = jnp.concatenate(trade(mixed0), axis=1)
    qkv1 = project(1)
    hidden0 = jnp.concatenate([tokens[0].astype(F32), mem_float], axis=0)
    result0, kept0 = rows_forward(hidden0, mixed0, w)
    memory1 = jnp.where(new_doc[1] == 1, mem_float, result0[size:])
    memory1_low = memory1.astype(BF16)
    mixed1, lse1, qkv_mem1 = attend(1, qkv1, memory1_low, False)
    mixed1 = jnp.concatenate(trade(mixed1), axis=1)
    result1, kept1 = rows_forward(tokens[1].astype(F32), mixed1, w)
    layer_out = jnp.stack([result0[:size], result1]).astype(BF16)

    kept_tok = [jnp.concatenate([a[:size], b], axis=0) for a, b in zip(kept0, kept1)]
    kept_mem = [a[size:] for a in kept0]
    grad_tok = d_out.reshape(slots * size, wide).astype(F32)
    hidden_tok, grad_mixed, small, pairs = rows_backward(grad_tok, kept_tok, w)
    grads = [
        trade([grad_mixed[t * size : (t + 1) * size, m * width : (m + 1) * width] for m in range(n_seg)])
        for t in range(slots)
    ]
    d_qkv1, d_mem1 = attend_back(1, qkv1, qkv_mem1, lse1, grads[1])
    d_mem1_all = trade([d_mem1[:, width:]] * n_seg)
    back_mem1 = sum(mm(d_mem1_all[m], head_wt[m][width:]) for m in range(n_seg))
    memory1_grad = 2.0 * back_mem1
    fresh1 = (new_doc[1] == 1).astype(F32)
    hidden_mem, grad_mixed_mem, small_mem, pairs_mem = rows_backward((1.0 - fresh1) * memory1_grad, kept_mem, w)
    d_qkv0, d_mem0 = attend_back(0, qkv0, qkv_mem0, lse0, list(grads[0]) + [grad_mixed_mem[:, :width]])

    back = [trade(d_qkv0), trade(d_qkv1)]
    grad_rows = [
        hidden_tok[t * size : (t + 1) * size] + sum(mm(back[t][m], head_wt[m]) for m in range(n_seg))
        for t in range(slots)
    ]
    grad_tokens = jnp.stack(grad_rows).astype(BF16)

    twice = jnp.concatenate([jnp.ones((width,), BF16), jnp.full((2 * width,), 2.0, BF16)])
    d_mem0_all = d_mem0 * twice
    d_mem1_all2 = d_mem1 * twice
    grad_mem = mm(d_mem0_all, head_wt[0]) + owner * (hidden_mem + fresh1 * memory1_grad)

    left = jnp.concatenate(rows[0] + rows[1] + [mem_init, memory1_low], axis=0)
    right = jnp.concatenate(list(d_qkv0) + list(d_qkv1) + [d_mem0_all, d_mem1_all2], axis=0)
    grad_heads = mm(left, right, TN).astype(BF16)
    bias_sums = jnp.sum(right.astype(F32), axis=0)

    def core_stage(blocks):
        keep, send = pick(blocks, core, 2), pick(blocks, 1 - core, 2)
        return keep.astype(F32) + swap(send, "doc", 1).astype(F32)

    def seg_stage(blocks):
        total = pick(blocks, seg).astype(F32)
        for m in others:
            total = total + swap(pick(blocks, seg ^ m), "seg", m).astype(F32)
        return total

    def pair_stage(blocks):
        step = n_pair
        while step > 4:
            step //= 2
            halves = blocks.reshape(2, step, *blocks.shape[1:])
            bit = (pair // step) & 1
            blocks = pick(halves, bit).astype(F32) + swap(
                pick(halves, 1 - bit).astype(blocks.dtype), "doc", 2 * step
            ).astype(F32)
            blocks = blocks.astype(halves.dtype)
        mine = pair % step
        total = pick(blocks, mine).astype(F32)
        for m in range(1, step):
            total = total + swap(pick(blocks, mine ^ m), "doc", 2 * m).astype(F32)
        return total

    shares = {}
    for name, (lhs, rhs) in pairs.items():
        full = mm(lhs, rhs, TN).astype(BF16)
        if name == "out":
            full = jnp.concatenate([pick(full.reshape(n_seg, width, wide), seg ^ m) for m in range(n_seg)], 0)
        each = full.shape[0] // (n_seg * n_doc)
        blocks = full.reshape(n_seg, n_pair, 2, each, full.shape[1])
        quarter = seg_stage(core_stage(blocks).astype(BF16))
        lhs_m, rhs_m = pairs_mem[name]
        lhs_m = jnp.concatenate([lhs_m, swap(lhs_m, "doc", 1)], axis=0)
        rhs_m = jnp.concatenate([rhs_m, swap(rhs_m, "doc", 1)], axis=0)
        if name == "out":
            mine = lhs_m.reshape(2 * mem, n_seg, n_pair, 2, each)[:, 0]
        else:
            mine = pick(lhs_m.reshape(2 * mem, n_seg, n_pair, 2, each), seg, 1)
        mine = pick(mine, core, 2).reshape(2 * mem, n_pair * each)
        quarter = quarter + mm(mine, rhs_m, TN).reshape(n_pair, each, -1)
        shares[name] = pair_stage(quarter.astype(BF16))

    each = wide // (n_seg * n_doc)
    halves = core_stage(grad_heads.reshape(n_seg, n_pair, 2, each, 3 * width)).astype(BF16)
    mine = [pick(halves, seg)] + [swap(pick(halves, seg ^ m), "seg", m) for m in others]
    mine = pair_stage(jnp.stack(mine, axis=1))
    mine = jnp.stack([pick(mine, seg ^ a) for a in range(n_seg)]).reshape(n_seg, each, 3, width)
    grad_q, grad_k, grad_v = [
        mine[:, :, i].transpose(1, 0, 2).reshape(each, wide) for i in range(3)
    ]

    sums = {k: small[k] + owner * small_mem[k] for k in small}
    own = lambda v: lax.dynamic_update_slice(jnp.zeros((wide,), F32), v, (seg * width,))
    sums["q_b"] = own(bias_sums[:width])
    sums["v_b"] = own(bias_sums[2 * width :])
    names = ["q_b", "v_b", "out_b", "attn_g", "attn_s", "exp_b", "red_b", "fin_g", "fin_s"]
    parts = [sums[k].reshape(n_seg, n_doc, -1) for k in names]
    parts.append(grad_mem.reshape(mem, n_seg, n_doc, each).transpose(1, 2, 0, 3).reshape(n_seg, n_doc, -1))
    packed = jnp.concatenate(parts, axis=-1)
    used = packed.shape[-1]
    padded = -(-used // 1024) * 1024
    packed = jnp.pad(packed, ((0, 0), (0, 0), (0, padded - used))).reshape(n_seg, n_pair, 2, 8, padded // 8)
    packed = pair_stage(seg_stage(core_stage(packed))).reshape(padded)
    got, at = {}, 0
    for k, part in zip(names + ["mem"], parts):
        got[k] = packed[at : at + part.shape[-1]]
        at += part.shape[-1]

    return (
        layer_out,
        grad_tokens,
        got["mem"].reshape(mem, each),
        grad_q,
        got["q_b"],
        grad_k,
        grad_v,
        got["v_b"],
        shares["out"],
        got["out_b"],
        got["attn_g"],
        got["attn_s"],
        shares["exp"],
        got["exp_b"],
        shares["red"],
        got["red_b"],
        got["fin_g"],
        got["fin_s"],
    )


def solution(mesh):
    both = ("seg", "doc")
    data = P("doc", "seg", None)
    placed = (data, P("doc"), P("doc")) + (P(),) * 16 + (data,)
    vec, mat = P(both), P(both, None)
    return jax.shard_map(
        shards,
        mesh=mesh,
        in_specs=placed,
        out_specs=(
            data,
            data,
            P(None, both),
            mat,
            vec,
            mat,
            mat,
            vec,
            mat,
            vec,
            vec,
            vec,
            mat,
            vec,
            mat,
            vec,
            vec,
            vec,
        ),
        check_vma=False,
    )
```

```python
import functools

import jax
import jax.numpy as jnp
from jax import lax
from jax.experimental import pallas as pl
from jax.experimental.pallas import tpu as pltpu
from jax.sharding import PartitionSpec as P

HEADS = 12


EPS = 1e-12
NEG_FILL = -1e30
F32 = jnp.float32
BF16 = jnp.bfloat16
NN = (((1,), (0,)), ((), ()))
NT = (((1,), (1,)), ((), ()))
TN = (((0,), (0,)), ((), ()))

Q_B, V_B, OUT_B, ATTN_G, ATTN_S, RED_B, FIN_G, FIN_S, EXP_B = range(9)
FRESH, VALID = 1, 2
N_VEC = 16
N_SMALL = 32


def mm(left, right, dims=NN):
    return lax.dot_general(left, right, dims, preferred_element_type=F32)


def swap(block, axis, mask):
    return lax.ppermute(block, axis, [(i, i ^ mask) for i in range(lax.axis_size(axis))])


def seg_here():
    return lax.axis_index("seg")


def core_here():
    return lax.axis_index("doc") & 1


def pair_here():
    return lax.axis_index("doc") >> 1


def shape_of(*dims, dtype=BF16):
    return jax.ShapeDtypeStruct(dims, dtype)


def call(kernel, out_shape, args, micros, far_in=(), far_out=(), scratch=()):
    vmem, far = pl.BlockSpec(memory_space=pltpu.VMEM), pl.BlockSpec(memory_space=pltpu.HBM)
    near = [x if i == 0 or i in far_in else pltpu.with_memory_space_constraint(x, pltpu.VMEM) for i, x in enumerate(args)]
    return pl.pallas_call(
        kernel,
        out_shape=[o if i in far_out else pltpu.VMEM(o.shape, o.dtype) for i, o in enumerate(out_shape)],
        in_specs=[pl.BlockSpec(memory_space=pltpu.SMEM)]
        + [far if i in far_in else vmem for i in range(1, len(args))],
        out_specs=[vmem] * len(out_shape),
        scratch_shapes=scratch,
        compiler_params=pltpu.CompilerParams(vmem_limit_bytes=8 << 20),
        cost_estimate=pl.CostEstimate(flops=0, transcendentals=0, bytes_accessed=int(micros * 3e6)),
    )(*near)


def reorder(x, seg, n_seg):
    width = x.shape[1] // n_seg
    bit = 1
    while bit < n_seg:
        moved = jnp.concatenate([x[:, (b ^ bit) * width : ((b ^ bit) + 1) * width] for b in range(n_seg)], axis=1)
        x = jnp.where((seg & bit) != 0, moved, x)
        bit *= 2
    return x


def own_columns(x, seg, n_seg):
    width = x.shape[1] // n_seg
    out = x[:, :width]
    for b in range(1, n_seg):
        out = jnp.where(seg == b, x[:, b * width : (b + 1) * width], out)
    return out


def prep_kernel(meta_ref, wq_ref, wk_ref, wv_ref, *refs, n_seg, chunks):
    vec_refs, (w_ref, b_ref, out_ref, sems) = refs[: EXP_B + 1], refs[EXP_B + 1 :]
    copies = [pltpu.make_async_copy(r, out_ref.at[i], sems.at[i]) for i, r in enumerate(vec_refs[:EXP_B])]
    copies.append(pltpu.make_async_copy(vec_refs[EXP_B], out_ref.at[EXP_B : EXP_B + chunks], sems.at[EXP_B]))
    for c in copies:
        c.start()
    seg = seg_here()
    w_ref[...] = jnp.concatenate([own_columns(r[...], seg, n_seg) for r in (wq_ref, wk_ref, wv_ref)], axis=1)
    for c in copies:
        c.wait()
    q_b = own_columns(out_ref[Q_B : Q_B + 1], seg, n_seg)
    v_b = own_columns(out_ref[V_B : V_B + 1], seg, n_seg)
    b_ref[...] = jnp.concatenate([q_b, jnp.zeros_like(q_b), v_b], axis=1)


def qkv_kernel(meta_ref, w_ref, b_ref, *refs):
    rows, out_ref = refs[:-1], refs[-1]
    size = rows[0].shape[0]
    for b, r in enumerate(rows):
        out_ref[b * size : (b + 1) * size, :] = (mm(r[...], w_ref[...]) + b_ref[...]).astype(BF16)


def key_columns(meta_ref, slot, blocks, size, mem):
    total = blocks * size + 2 * mem
    col = lax.broadcasted_iota(jnp.int32, (1, total), 1)
    place = col
    for b in range(blocks):
        inside = (col >= b * size) & (col < (b + 1) * size)
        place = jnp.where(inside, ((seg_here() ^ b) - b) * size + col, place)
    return (place < meta_ref[VALID + slot]) | (col >= blocks * size)


def attn_fwd_kernel(meta_ref, qkv_ref, mem_ref, w_ref, b_ref, *outs, slot, blocks, heads, mem_queries):
    if mem_queries:
        memory = mem_ref[...]
    else:
        written_ref, outs = outs[0], outs[1:]
        memory = jnp.where(meta_ref[FRESH] == 1, mem_ref[...], written_ref[...].astype(BF16))
        outs[-1][...] = memory
    mix_refs, lse_ref, mem_out_ref = outs[:blocks], outs[blocks], outs[blocks + 1]
    size = qkv_ref.shape[0] // blocks
    mem = mem_ref.shape[0]
    width = qkv_ref.shape[1] // 3
    head_dim = width // heads
    mem_out_ref[...] = (mm(memory, w_ref[...]) + b_ref[...]).astype(BF16)
    keep = key_columns(meta_ref, slot, blocks, size, mem)
    for h in range(heads):
        lo, hi = h * head_dim, (h + 1) * head_dim
        mem_key = mem_out_ref[:, width + lo : width + hi]
        mem_value = mem_out_ref[:, 2 * width + lo : 2 * width + hi]
        key = jnp.concatenate([qkv_ref[:, width + lo : width + hi], mem_key, mem_key], axis=0)
        value = jnp.concatenate([qkv_ref[:, 2 * width + lo : 2 * width + hi], mem_value, mem_value], axis=0)

        def one(query):
            scores = jnp.where(keep, mm(query, key, NT) * 0.125, NEG_FILL)
            highest = jnp.max(scores, axis=-1, keepdims=True)
            weights = jnp.exp(scores - highest)
            total = jnp.sum(weights, axis=-1, keepdims=True)
            probs = (weights * (1.0 / total)).astype(BF16)
            return mm(probs, value).astype(BF16), highest + jnp.log(total)

        for b in range(blocks):
            mixed, lse = one(qkv_ref[b * size : (b + 1) * size, lo:hi])
            mix_refs[b][:size, lo:hi] = mixed
            lse_ref[b * size : (b + 1) * size, h : h + 1] = lse
        if mem_queries:
            mixed, lse = one(mem_out_ref[:, lo:hi])
            for b in range(blocks):
                mix_refs[b][size:, lo:hi] = mixed
            lse_ref[blocks * size : blocks * size + mem, h : h + 1] = lse


def attn_bwd_kernel(meta_ref, qkv_ref, mem_ref, lse_ref, *refs, slot, blocks, heads, mem_queries):
    n_grad = blocks + (1 if mem_queries else 0)
    grad_refs, refs = refs[:n_grad], refs[n_grad:]
    more_refs, out_refs, mem_out_ref = refs[: -blocks - 1], refs[-blocks - 1 : -1], refs[-1]
    for more_ref, out_ref in zip(more_refs, out_refs):
        out_ref[out_ref.shape[0] - more_ref.shape[0] :, :] = more_ref[...]
    size = qkv_ref.shape[0] // blocks
    first = slot * size
    mem = mem_ref.shape[0]
    width = qkv_ref.shape[1] // 3
    head_dim = width // heads
    keep = key_columns(meta_ref, slot, blocks, size, mem)
    for h in range(heads):
        lo, hi = h * head_dim, (h + 1) * head_dim
        mem_key = mem_ref[:, width + lo : width + hi]
        mem_value = mem_ref[:, 2 * width + lo : 2 * width + hi]
        key = jnp.concatenate([qkv_ref[:, width + lo : width + hi], mem_key, mem_key], axis=0)
        value = jnp.concatenate([qkv_ref[:, 2 * width + lo : 2 * width + hi], mem_value, mem_value], axis=0)

        def one(query, grad, lse):
            scores = jnp.where(keep, mm(query, key, NT) * 0.125, NEG_FILL)
            probs = jnp.exp(scores - lse)
            grad_probs = mm(grad, value, NT)
            inner = jnp.sum(grad_probs * probs, axis=-1, keepdims=True)
            grad_scores = (probs * (grad_probs - inner)).astype(BF16)
            grad_query = (mm(grad_scores, key) * 0.125).astype(BF16)
            return grad_query, mm(grad_scores, query, TN), mm(probs.astype(BF16), grad, TN)

        grad_key = grad_value = None
        for b in range(n_grad):
            if b < blocks:
                query = qkv_ref[b * size : (b + 1) * size, lo:hi]
                lse = lse_ref[b * size : (b + 1) * size, h : h + 1]
            else:
                query = mem_ref[:, lo:hi]
                lse = lse_ref[blocks * size : blocks * size + mem, h : h + 1]
            grad = grad_refs[b][first : first + size, lo:hi] if b < blocks else grad_refs[b][:, lo:hi]
            grad_query, key_part, value_part = one(query, grad, lse)
            grad_key = key_part if grad_key is None else grad_key + key_part
            grad_value = value_part if grad_value is None else grad_value + value_part
            if b < blocks:
                out_refs[b][:size, lo:hi] = grad_query
            else:
                mem_out_ref[:, lo:hi] = grad_query
        if not mem_queries:
            mem_out_ref[:, lo:hi] = jnp.zeros((mem, head_dim), BF16)
        grad_key = (grad_key * 0.125).astype(BF16)
        grad_value = grad_value.astype(BF16)
        for b in range(blocks):
            out_refs[b][:size, width + lo : width + hi] = grad_key[b * size : (b + 1) * size]
            out_refs[b][:size, 2 * width + lo : 2 * width + hi] = grad_value[b * size : (b + 1) * size]
        mem_out_ref[:, width + lo : width + hi] = grad_key[blocks * size : blocks * size + mem]
        mem_out_ref[:, 2 * width + lo : 2 * width + hi] = grad_value[blocks * size : blocks * size + mem]


def norm_parts(hidden):
    center = hidden - jnp.mean(hidden, axis=-1, keepdims=True)
    inverse = lax.rsqrt(jnp.mean(center * center, axis=-1, keepdims=True) + EPS)
    return center * inverse, inverse


def norm_back(grad, gain, unit, inverse):
    scaled = grad * gain
    mean_scaled = jnp.mean(scaled, axis=-1, keepdims=True)
    mean_product = jnp.mean(scaled * unit, axis=-1, keepdims=True)
    return inverse * (scaled - mean_scaled - unit * mean_product)


def gelu_and_slope(pre):
    cdf = 0.5 * (1.0 + lax.erf(pre * (2.0**-0.5)))
    density = jnp.exp(-0.5 * pre * pre) * 0.3989422804014327
    return pre * cdf, cdf + pre * density


N_KEPT = 4


def rows_fwd_kernel(meta_ref, *refs, n_seg, n_pair, n_hidden):
    mix_refs, hid_refs = refs[:n_seg], refs[n_seg : n_seg + n_hidden]
    vec_ref, out_ref, exp_ref, red_ref = refs[n_seg + n_hidden : n_seg + n_hidden + 4]
    outs = refs[n_seg + n_hidden + 4 :]
    unit_a_ref, inv_ref, slope_ref, unit_f_ref = outs[:N_KEPT]
    result_refs, left_refs = outs[N_KEPT : N_KEPT + n_hidden], outs[N_KEPT + n_hidden :]
    wide = out_ref.shape[0]
    size = hid_refs[0].shape[0]

    def vec(i):
        return vec_ref[i : i + 1]

    def keep_left(x, at, first, blocks):
        left_factors(meta_ref, x, left_refs, at, first, blocks, n_seg, n_pair, size)

    each = wide // (n_seg * n_pair * 2)
    mixed = reorder(jnp.concatenate([r[...] for r in mix_refs], axis=1), seg_here(), n_seg)
    hidden = jnp.concatenate([r[...].astype(F32) for r in hid_refs], axis=0)
    unit, inverse = norm_parts(hidden + (mm(mixed, out_ref[...]) + vec(OUT_B)))
    unit_a_ref[...] = unit
    inv_ref[:, 0:1] = inverse
    normed = unit * vec(ATTN_G) + vec(ATTN_S)
    low = normed.astype(BF16)
    chunks = exp_ref.shape[1] // wide
    acc = normed + vec(RED_B)
    for q in range(chunks):
        cols = slice(q * wide, (q + 1) * wide)
        active, slope = gelu_and_slope(mm(low, exp_ref[:, cols]) + vec(EXP_B + q))
        slope_ref[:, cols] = slope
        active = active.astype(BF16)
        acc = acc + mm(active, red_ref[cols])
        keep_left(active, each, q * n_seg // chunks, n_seg // chunks)
    unit, inverse = norm_parts(acc)
    unit_f_ref[...] = unit
    inv_ref[:, 1:2] = inverse
    result = unit * vec(FIN_G) + vec(FIN_S)
    at = 0
    for r in result_refs:
        r[...] = result[at : at + r.shape[0]].astype(r.dtype)
        at += r.shape[0]
    keep_left(low, 0, 0, n_seg)
    keep_left(mixed, (chunks + 1) * each, 0, n_seg)


def left_factors(meta_ref, x, left_refs, at, first, blocks, n_seg, n_pair, size):
    seg, core, pair = seg_here(), core_here(), pair_here()
    rows = x.shape[1] // (blocks * n_pair * 2)
    keep_ref, send_ref = left_refs[:2]
    keep, send = core_halves(x[:size].astype(F32).T, core, n_pair, rows)
    for s in range(blocks):
        for z in range(n_pair):
            keep_ref[(first + s) ^ seg, z ^ pair, at : at + rows] = keep[s * n_pair + z]
            send_ref[(first + s) ^ seg, z ^ pair, at : at + rows] = send[s * n_pair + z]
    if left_refs[2:]:
        keep_ref, send_ref = left_refs[2:]
        mine = x[size:].astype(F32)
        if blocks > 1:
            assert blocks == n_seg
            mine = own_columns(mine, seg, n_seg)
        keep, send = core_halves(mine.T, core, n_pair, rows)

        @pl.when((seg == first) | (blocks > 1))
        def _():
            for z in range(n_pair):
                keep_ref[z ^ pair, at : at + rows] = keep[z]
                send_ref[z ^ pair, at : at + rows] = send[z]


def core_halves(x, core, pairs, rows):
    x = x.reshape(x.shape[0] // (2 * rows), 2, rows, x.shape[1])
    even, odd = x[:, 0], x[:, 1]
    return jnp.where(core == 0, even, odd).astype(BF16), jnp.where(core == 0, odd, even).astype(BF16)


def rows_back(seg, n_seg, grad, kept, vec_ref, out_ref, exp_ref, red_ref, outs):
    right_ref, hidden_ref, small_ref = outs
    wide = hidden_ref.shape[1]
    chunks = exp_ref.shape[1] // wide

    def vec(i):
        return vec_ref[i : i + 1]

    def total(x):
        return jnp.sum(x, axis=0, keepdims=True)

    unit = kept(3)
    grad_sum = norm_back(grad, vec(FIN_G), unit, kept(1)[:, 1:2])
    low = grad_sum.astype(BF16)
    right_ref[:, chunks * wide : (chunks + 1) * wide] = low
    small_ref[...] = jnp.zeros_like(small_ref)
    small_ref[FIN_G : FIN_G + 1] = total(grad * unit)
    small_ref[FIN_S : FIN_S + 1] = total(grad)
    small_ref[RED_B : RED_B + 1] = total(low.astype(F32))
    acc = grad_sum
    for q in range(chunks):
        cols = slice(q * wide, (q + 1) * wide)
        grad_pre = (mm(low, red_ref[cols], NT) * kept(2, cols)).astype(BF16)
        right_ref[:, cols] = grad_pre
        small_ref[EXP_B + q : EXP_B + q + 1] = total(grad_pre.astype(F32))
        acc = acc + mm(grad_pre, exp_ref[:, cols], NT)
    unit = kept(0)
    small_ref[ATTN_G : ATTN_G + 1] = total(acc * unit)
    small_ref[ATTN_S : ATTN_S + 1] = total(acc)
    grad_hidden = norm_back(acc, vec(ATTN_G), unit, kept(1)[:, 0:1])
    hidden_ref[...] = grad_hidden
    low = grad_hidden.astype(BF16)
    right_ref[:, (chunks + 1) * wide :] = low
    small_ref[OUT_B : OUT_B + 1] = total(low.astype(F32))
    return reorder(mm(low, out_ref[...], NT).astype(BF16), seg, n_seg)


def token_rows_back_kernel(meta_ref, grad_ref, *refs, slots, n_seg):
    kept_refs = [refs[t * N_KEPT : (t + 1) * N_KEPT] for t in range(slots)]
    refs = refs[slots * N_KEPT :]
    (vec_ref, out_ref, exp_ref, red_ref), outs, mix_refs = refs[:4], refs[4:7], refs[7:]
    size = grad_ref.shape[1]

    def kept(i, cols=slice(None)):
        return jnp.concatenate([kept_refs[t][i][:size, cols] for t in range(slots)], axis=0)

    grad = jnp.concatenate([grad_ref[t].astype(F32) for t in range(slots)], axis=0)
    mixed = rows_back(seg_here(), n_seg, grad, kept, vec_ref, out_ref, exp_ref, red_ref, outs)
    width = mixed.shape[1] // n_seg
    for m in range(n_seg):
        mix_refs[m][...] = mixed[:, m * width : (m + 1) * width]


def memory_rows_back_kernel(meta_ref, *refs, n_seg, size):
    d_refs, refs = refs[:n_seg], refs[n_seg:]
    (wk_ref, wv_ref), kept_refs, refs = refs[:2], refs[2 : 2 + N_KEPT], refs[2 + N_KEPT :]
    (vec_ref, out_ref, exp_ref, red_ref), outs, (memory_ref, own_ref) = refs[:4], refs[4:7], refs[7:]
    seg = seg_here()
    width = d_refs[0].shape[1] // 2
    d_key = reorder(jnp.concatenate([r[:, :width] for r in d_refs], axis=1), seg, n_seg)
    d_value = reorder(jnp.concatenate([r[:, width:] for r in d_refs], axis=1), seg, n_seg)
    grad = 2.0 * (mm(d_key, wk_ref[...], NT) + mm(d_value, wv_ref[...], NT))
    memory_ref[...] = grad
    grad = jnp.where(meta_ref[FRESH] == 1, jnp.zeros_like(grad), grad)

    def kept(i, cols=slice(None)):
        return kept_refs[i][size:, cols]

    mixed = rows_back(seg, n_seg, grad, kept, vec_ref, out_ref, exp_ref, red_ref, outs)
    own_ref[...] = mixed[:, : own_ref.shape[1]]


def tokens_grad_kernel(meta_ref, hidden_ref, wq_ref, wk_ref, wv_ref, *refs, slots, n_seg):
    d_refs, out_ref = refs[:-1], refs[-1]
    size = out_ref.shape[1]
    width = d_refs[0].shape[1] // 3
    seg = seg_here()
    for t in range(slots):
        grad = hidden_ref[t * size : (t + 1) * size]
        for i, w_ref in enumerate((wq_ref, wk_ref, wv_ref)):
            part = jnp.concatenate([r[t * size : (t + 1) * size, i * width : (i + 1) * width] for r in d_refs], 1)
            grad = grad + mm(reorder(part, seg, n_seg), w_ref[...], NT)
        out_ref[t] = grad.astype(BF16)


def rows_weights_kernel(meta_ref, *refs, n_seg, n_pair):
    left_refs, (right_ref, other_ref), outs = refs[:-6], refs[-6:-4], refs[-4:]
    wide = right_ref.shape[1] - 0
    wide = outs[0].shape[3]
    chunks = right_ref.shape[1] // wide - 2
    each = outs[0].shape[2] // (2 * chunks + 1)
    half = n_pair // 2

    def product(lo, rows, q, row):
        left = jnp.concatenate(
            [r[:, :, lo : lo + rows].reshape(n_seg * n_pair * rows, r.shape[3]) for r in left_refs], axis=1
        )
        right = jnp.concatenate([r[:, q * wide : (q + 1) * wide] for r in (right_ref, other_ref)], axis=0)
        full = mm(left, right).reshape(n_seg, n_pair, rows, wide).astype(BF16)
        for s in range(n_seg):
            low, high = s & 1, s >> 1
            outs[low][high, :, row : row + rows] = full[s, :half]
            outs[2 + high][low, :, row : row + rows] = full[s, half:]

    for q in range(chunks):
        product(0, each, q, q * each)
    product(each, chunks * each, chunks, chunks * each)
    product((chunks + 1) * each, each, chunks + 1, 2 * chunks * each)


def quarter_kernel(meta_ref, left_ref, left2_ref, right_ref, right2_ref, *refs):
    half_refs, outs = (refs[:2], refs[2:4]), refs[4:]
    wide = outs[0].shape[2]
    pairs = left_ref.shape[0]
    chunks = right_ref.shape[1] // wide - 2
    each = left_ref.shape[1] // (chunks + 2)
    half = pairs // 2

    def put(lo, rows, q, row):
        def rows_of(r):
            return jnp.concatenate([r[z].astype(F32)[lo : lo + rows] for z in range(pairs)], axis=0)

        left = jnp.concatenate([rows_of(left_ref), rows_of(left2_ref)], axis=1).astype(BF16)
        right = jnp.concatenate([r[:, q * wide : (q + 1) * wide] for r in (right_ref, right2_ref)], axis=0)
        part = mm(left, right).reshape(pairs, rows, wide)
        for z in range(pairs):
            total = part[z]
            for r in half_refs[z // half]:
                total = total + r[z % half, row : row + rows].astype(F32)
            outs[z & 1][z >> 1, row : row + rows] = total.astype(BF16)

    for q in range(chunks):
        put(0, each, q, q * each)
    put(each, chunks * each, chunks, chunks * each)
    put((chunks + 1) * each, each, chunks + 1, 2 * chunks * each)


def heads_weights_kernel(meta_ref, small_ref, small_m_ref, hid_ref, memory_ref, w_ref, *refs, slots, n_seg):
    rows, refs = refs[: slots * n_seg], refs[slots * n_seg :]
    grads, (mem0_ref, mem1_ref, dm0_ref, dm1_ref, keep_ref, send_ref) = refs[:n_seg], refs[n_seg:]
    seg, core, pair, fresh1 = seg_here(), core_here(), pair_here(), meta_ref[FRESH]
    wide = rows[0].shape[1]
    width = wide // n_seg
    each = keep_ref.shape[2]
    col = lax.broadcasted_iota(jnp.int32, (1, 3 * width), 1)
    twice = jnp.where(col < width, 1.0, 2.0)
    dm0 = (dm0_ref[...].astype(F32) * twice).astype(BF16)
    dm1 = (dm1_ref[...].astype(F32) * twice).astype(BF16)
    full = mm(mem0_ref[...], dm0, TN) + mm(mem1_ref[...], dm1, TN)
    sums = jnp.sum(dm0.astype(F32), axis=0, keepdims=True) + jnp.sum(dm1.astype(F32), axis=0, keepdims=True)
    for m, g in enumerate(grads):
        x = jnp.concatenate([r[...] for r in rows[m::n_seg]], axis=0)
        full = full + mm(x, g[...], TN)
        sums = sums + jnp.sum(g[...].astype(F32), axis=0, keepdims=True)
    grad_mem = mm(dm0, w_ref[...], NT)
    whole = hid_ref[...] + jnp.where(fresh1 == 1, memory_ref[...], 0.0)
    grad_mem = grad_mem + jnp.where(seg == 0, whole, 0.0)

    def placed(v):
        return reorder(jnp.concatenate([v, jnp.zeros((1, wide - width), F32)], axis=1), seg, n_seg)

    n_pair = keep_ref.shape[0]
    chunks = 4
    head = EXP_B + chunks
    given = small_ref[...] + jnp.where(seg == 0, small_m_ref[...], 0.0)
    small = jnp.concatenate(
        [
            placed(sums[:, :width]),
            placed(sums[:, 2 * width :]),
            given[2:head],
            grad_mem,
            jnp.zeros((N_SMALL - head - grad_mem.shape[0], wide), F32),
        ],
        axis=0,
    ).T
    turned = small.reshape(wide // (chunks * each), chunks, each, N_SMALL)
    spread = [
        jnp.concatenate(
            [turned[:, k, :, EXP_B + q : EXP_B + q + 1].reshape(wide // chunks, 1) for k in range(chunks)], axis=1
        )
        for q in range(chunks)
    ]
    small = jnp.concatenate([small[:, :EXP_B], jnp.concatenate(spread, axis=0), small[:, head:]], axis=1)
    high = small.astype(BF16)
    rest = (small - high.astype(F32)).astype(BF16)
    full = jnp.concatenate([full, high.astype(F32), rest.astype(F32)], axis=1)
    keep, send = core_halves(full, core, n_pair, each)
    for s in range(n_seg):
        for z in range(n_pair):
            keep_ref[z ^ pair, s ^ seg] = keep[s * n_pair + z]
            send_ref[z ^ pair, s ^ seg] = send[s * n_pair + z]


def late_sum(*parts, at):
    total = sum(p.astype(F32) for p in parts)
    small = total[..., at : at + N_SMALL] + total[..., at + N_SMALL :]
    high = small.astype(BF16)
    rest = (small - high.astype(F32)).astype(BF16)
    return jnp.concatenate([total[..., :at].astype(BF16), high, rest], axis=-1)


def heads_final_kernel(meta_ref, *refs, n_seg, mem):
    ins, outs = refs[:n_seg], refs[n_seg:]
    seg = seg_here()
    width = outs[0].shape[1] // n_seg
    total = [r[...].astype(F32) for r in ins]
    for i in range(3):
        outs[i][...] = reorder(
            jnp.concatenate([total[m][:, i * width : (i + 1) * width] for m in range(n_seg)], axis=1), seg, n_seg
        )
    at = 3 * width
    small = sum(t[:, at : at + N_SMALL] + t[:, at + N_SMALL : at + 2 * N_SMALL] for t in total).T
    vec_refs, exp_ref, mem_ref = outs[3 : 3 + EXP_B], outs[3 + EXP_B], outs[4 + EXP_B]
    for i, r in enumerate(vec_refs):
        r[...] = small[i : i + 1]
    exp_ref[...] = jnp.concatenate([small[EXP_B + q : EXP_B + q + 1] for q in range(4)], axis=1)
    mem_ref[...] = small[EXP_B + 4 : EXP_B + 4 + mem]


def rows_final_kernel(meta_ref, *refs):
    ins, (exp_ref, red_ref, out_ref) = refs[:-3], refs[-3:]
    each, wide = out_ref.shape
    chunks = exp_ref.shape[1] // wide
    total = ins[0][...].astype(F32)
    for r in ins[1:]:
        total = total + r[...].astype(F32)
    for q in range(chunks):
        exp_ref[:, q * wide : (q + 1) * wide] = total[q * each : (q + 1) * each]
    red_ref[...] = total[chunks * each : 2 * chunks * each]
    out_ref[...] = total[2 * chunks * each :]


def shards(
    tokens,
    new_doc,
    valid_len,
    mem_init,
    query_proj,
    query_bias,
    key_proj,
    value_proj,
    value_bias,
    output_proj,
    output_bias,
    attn_gain,
    attn_shift,
    expand_proj,
    expand_bias,
    reduce_proj,
    reduce_bias,
    final_gain,
    final_shift,
    d_out,
):
    slots, size, wide = tokens.shape
    assert slots == 2
    n_seg, n_doc = lax.axis_size("seg"), lax.axis_size("doc")
    n_pair = n_doc // 2
    hidden_units = expand_proj.shape[1]
    chunks = hidden_units // wide
    assert chunks == 4
    mem = mem_init.shape[0]
    width = wide // n_seg
    heads = HEADS // n_seg
    others = range(1, n_seg)
    all_rows = n_seg * size

    rows0 = [tokens[0]] + [swap(tokens[0], "seg", m) for m in others]
    place = jnp.concatenate([new_doc, valid_len])
    w_own, b_own, vecs = call(
        functools.partial(prep_kernel, n_seg=n_seg, chunks=chunks),
        [shape_of(wide, 3 * width), shape_of(1, 3 * width, dtype=F32), shape_of(N_VEC, wide, dtype=F32)],
        (
            place,
            query_proj,
            key_proj,
            value_proj,
            query_bias,
            value_bias,
            output_bias,
            attn_gain,
            attn_shift,
            reduce_bias,
            final_gain,
            final_shift,
            expand_bias.reshape(chunks, wide),
        ),
        4,
        far_in=range(4, 5 + EXP_B),
        scratch=[pltpu.SemaphoreType.DMA((EXP_B + 1,))],
    )

    second, w_own, *rows0 = lax.optimization_barrier((tokens[1], w_own, *rows0))
    rows = [rows0, [second] + [swap(second, "seg", m) for m in others]]

    def project(t):
        (out,) = call(qkv_kernel, [shape_of(all_rows, 3 * width)], (place, w_own, b_own, *rows[t]), 3)
        return out

    def attend(t, qkv, written=()):
        mem_queries = not written
        got = call(
            functools.partial(attn_fwd_kernel, slot=t, blocks=n_seg, heads=heads, mem_queries=mem_queries),
            [shape_of(size + (mem if mem_queries else 0), width)] * n_seg
            + [shape_of(all_rows + mem, 128, dtype=F32), shape_of(mem, 3 * width)]
            + [shape_of(mem, wide)] * len(written),
            (place, qkv, mem_init, w_own, b_own, *written),
            8,
        )
        return list(got[:n_seg]), *got[n_seg:]

    def attend_back(t, qkv, qkv_mem, lse, grads, more=()):
        got = call(
            functools.partial(attn_bwd_kernel, slot=t, blocks=n_seg, heads=heads, mem_queries=len(grads) > n_seg),
            [shape_of(size * (2 if more else 1), 3 * width)] * n_seg + [shape_of(mem, 3 * width)],
            (place, qkv, qkv_mem, lse, *grads, *more),
            8,
        )
        return got[:n_seg], got[n_seg]

    def trade(blocks):
        return [blocks[0]] + [swap(blocks[m], "seg", m) for m in others]

    weights = (vecs, output_proj, expand_proj, reduce_proj)
    each = wide // (n_seg * n_doc)

    def rows_forward(mixed, hidden, result_shapes):
        n_rows = sum(h.shape[0] for h in hidden)
        left = [shape_of(n_seg, n_pair, (chunks + 2) * each, size)] * 2
        if len(hidden) > 1:
            left += [shape_of(n_pair, (chunks + 2) * each, mem)] * 2
        got = call(
            functools.partial(rows_fwd_kernel, n_seg=n_seg, n_pair=n_pair, n_hidden=len(hidden)),
            [
                shape_of(n_rows, wide, dtype=F32),
                shape_of(n_rows, 128, dtype=F32),
                shape_of(n_rows, hidden_units, dtype=F32),
                shape_of(n_rows, wide, dtype=F32),
                *result_shapes,
                *left,
            ],
            (place, *mixed, *hidden, *weights),
            8,
        )
        return got[:N_KEPT], got[N_KEPT : N_KEPT + len(hidden)], got[N_KEPT + len(hidden) :]

    qkv0 = project(0)
    mixed0, lse0, qkv_mem0 = attend(0, qkv0)
    mixed0[0], *rows[1] = lax.optimization_barrier((mixed0[0], *rows[1]))
    qkv1 = project(1)
    mixed0 = trade(mixed0)
    qkv1, mixed0[0] = lax.optimization_barrier((qkv1, mixed0[0]))
    kept0, (layer0, written), (left0, left0_send, left_m, left_m_send) = rows_forward(
        mixed0, (tokens[0], mem_init), [shape_of(size, wide), shape_of(mem, wide, dtype=F32)]
    )
    mixed1, lse1, qkv_mem1, memory1 = attend(1, qkv1, (written,))
    kept1, (layer1,), (left1, left1_send) = rows_forward(trade(mixed1), (tokens[1],), [shape_of(size, wide)])
    layer_out = jnp.stack([layer0, layer1])

    def back_shapes(n_rows):
        return [
            shape_of(n_rows, hidden_units + 2 * wide),
            shape_of(n_rows, wide, dtype=F32),
            shape_of(N_VEC, wide, dtype=F32),
        ]

    n_rows = slots * size
    got = call(
        functools.partial(token_rows_back_kernel, slots=slots, n_seg=n_seg),
        back_shapes(n_rows) + [shape_of(n_rows, width)] * n_seg,
        (place, d_out, *kept0, *kept1, *weights),
        10,
    )
    right, hidden, small = got[:3]
    grads = trade(got[3:])
    right_other = swap(right, "doc", 1)
    left0_other, left_m_other = swap(left0_send, "doc", 1), swap(left_m_send, "doc", 1)
    left1_other = swap(left1_send, "doc", 1)

    d_qkv1, d_mem1 = attend_back(1, qkv1, qkv_mem1, lse1, grads)
    d_mem1_all = trade([d_mem1[:, width:]] * n_seg)

    right_other, d_mem1_all[0] = lax.optimization_barrier((right_other, d_mem1_all[0]))
    share = (2 * chunks + 1) * each
    keep_a, send_a, keep_b, send_b = call(
        functools.partial(rows_weights_kernel, n_seg=n_seg, n_pair=n_pair),
        [shape_of(n_seg // 2, n_pair // 2, share, wide)] * 4,
        (place, left0, left1, left0_other, left1_other, right, right_other),
        8,
    )
    send_a, send_b, *d_mem1_all = lax.optimization_barrier((send_a, send_b, *d_mem1_all))

    def plain_sum(*parts):
        return sum(p.astype(F32) for p in parts).astype(BF16)

    came_a, came_b = swap(send_a, "seg", 1), swap(send_b, "seg", 2)

    got = call(
        functools.partial(memory_rows_back_kernel, n_seg=n_seg, size=size),
        back_shapes(mem) + [shape_of(mem, wide, dtype=F32), shape_of(mem, width)],
        (place, *d_mem1_all, key_proj, value_proj, *kept0, *weights),
        6,
    )
    right_m, hidden_m, small_m, memory1_grad, mixed_m = got
    right_m_other = swap(right_m, "doc", 1)
    d_qkv, d_mem0 = attend_back(0, qkv0, qkv_mem0, lse0, [*grads, mixed_m], d_qkv1)

    back = trade(d_qkv)
    (grad_tokens,) = call(
        functools.partial(tokens_grad_kernel, slots=slots, n_seg=n_seg),
        [shape_of(slots, size, wide)],
        (place, hidden, query_proj, key_proj, value_proj, *back),
        3,
        far_out=(0,),
    )

    columns = 3 * width + 2 * N_SMALL
    keep, send = call(
        functools.partial(heads_weights_kernel, slots=slots, n_seg=n_seg),
        [shape_of(n_pair, n_seg, each, columns)] * 2,
        (
            place,
            small,
            small_m,
            hidden_m,
            memory1_grad,
            w_own,
            *rows[0],
            *rows[1],
            *d_qkv,
            mem_init,
            memory1,
            d_mem0,
            d_mem1,
        ),
        6,
    )
    came_a, came_b, keep = lax.optimization_barrier((came_a, came_b, keep))
    keep_a, send_a = [plain_sum(keep_a[i], came_a[i]) for i in range(2)]
    keep_b, send_b = [plain_sum(keep_b[i], came_b[i]) for i in range(2)]
    add = functools.partial(late_sum, at=3 * width)
    came = swap(send, "doc", 1)
    came, send_a, send_b = lax.optimization_barrier((came, send_a, send_b))
    came_a, came_b = swap(send_a, "seg", 2), swap(send_b, "seg", 1)
    keep_e, send_e = call(
        quarter_kernel,
        [shape_of(n_pair // 2, share, wide)] * 2,
        (place, left_m, left_m_other, right_m, right_m_other, keep_a, came_a, keep_b, came_b),
        5,
    )

    def pair_sum(keep, send, add):
        bit = 2
        came = swap(send, "doc", bit)
        while keep.shape[0] > 1:
            bit *= 2
            if keep.shape[0] == 2:
                (keep, send) = [add(keep[i : i + 1], came[i : i + 1]) for i in range(2)]
            else:
                both = add(keep, came)
                keep, send = both[0::2], both[1::2]
            came = swap(send, "doc", bit)
        return [keep[0], came[0]]

    grad_exp, grad_red, grad_out = call(
        rows_final_kernel,
        [
            shape_of(each, hidden_units, dtype=F32),
            shape_of(chunks * each, wide, dtype=F32),
            shape_of(each, wide, dtype=F32),
        ],
        (place, *pair_sum(keep_e, send_e, plain_sum)),
        1,
        far_out=range(3),
    )

    mine = add(keep, came)
    mine = add(*pair_sum(mine[0::2], mine[1::2], add))
    parts = trade([mine[m] for m in range(n_seg)])
    got = call(
        functools.partial(heads_final_kernel, n_seg=n_seg, mem=mem),
        [shape_of(each, wide, dtype=F32)] * 3
        + [shape_of(1, each, dtype=F32)] * EXP_B
        + [shape_of(1, chunks * each, dtype=F32), shape_of(mem, each, dtype=F32)],
        (place, *parts),
        1,
        far_out=range(5 + EXP_B),
    )
    grad_q, grad_k, grad_v = got[:3]
    flat = [v.reshape(-1) for v in got[3:-1]]

    return (
        layer_out,
        grad_tokens,
        got[-1],
        grad_q,
        flat[Q_B],
        grad_k,
        grad_v,
        flat[V_B],
        grad_out,
        flat[OUT_B],
        flat[ATTN_G],
        flat[ATTN_S],
        grad_exp,
        flat[EXP_B],
        grad_red,
        flat[RED_B],
        flat[FIN_G],
        flat[FIN_S],
    )


def solution(mesh):
    both = ("seg", "doc")
    data = P("doc", "seg", None)
    placed = (data, P("doc"), P("doc")) + (P(),) * 16 + (data,)
    vec, mat = P(both), P(both, None)
    return jax.shard_map(
        shards,
        mesh=mesh,
        in_specs=placed,
        out_specs=(
            data,
            data,
            P(None, both),
            mat,
            vec,
            mat,
            mat,
            vec,
            mat,
            vec,
            vec,
            vec,
            mat,
            vec,
            mat,
            vec,
            vec,
            vec,
        ),
        check_vma=False,
    )
```

```python
import functools

import jax
import jax.numpy as jnp
from jax import lax
from jax.experimental import pallas as pl
from jax.experimental.pallas import tpu as pltpu
from jax.sharding import PartitionSpec as P

HEADS = 12


EPS = 1e-12
NEG_FILL = -1e30
F32 = jnp.float32
BF16 = jnp.bfloat16
NN = (((1,), (0,)), ((), ()))
NT = (((1,), (1,)), ((), ()))
TN = (((0,), (0,)), ((), ()))

Q_B, V_B, OUT_B, ATTN_G, ATTN_S, RED_B, FIN_G, FIN_S, EXP_B = range(9)
FRESH, VALID = 1, 2
N_VEC = 16
N_SMALL = 32


def mm(left, right, dims=NN):
    return lax.dot_general(left, right, dims, preferred_element_type=F32)


def swap(block, axis, mask):
    return lax.ppermute(block, axis, [(i, i ^ mask) for i in range(lax.axis_size(axis))])


def seg_here():
    return lax.axis_index("seg")


def core_here():
    return lax.axis_index("doc") & 1


def pair_here():
    return lax.axis_index("doc") >> 1


def shape_of(*dims, dtype=BF16):
    return jax.ShapeDtypeStruct(dims, dtype)


def call(kernel, out_shape, args, micros, far_in=(), far_out=(), scratch=()):
    vmem, far = pl.BlockSpec(memory_space=pltpu.VMEM), pl.BlockSpec(memory_space=pltpu.HBM)
    near = [
        x if i == 0 else pltpu.with_memory_space_constraint(x, pltpu.HBM if i in far_in else pltpu.VMEM)
        for i, x in enumerate(args)
    ]
    return pl.pallas_call(
        kernel,
        out_shape=[o if i in far_out else pltpu.VMEM(o.shape, o.dtype) for i, o in enumerate(out_shape)],
        in_specs=[pl.BlockSpec(memory_space=pltpu.SMEM)]
        + [far if i in far_in else vmem for i in range(1, len(args))],
        out_specs=[vmem] * len(out_shape),
        scratch_shapes=scratch,
        compiler_params=pltpu.CompilerParams(vmem_limit_bytes=8 << 20),
        cost_estimate=pl.CostEstimate(flops=0, transcendentals=0, bytes_accessed=int(micros * 3e6)),
    )(*near)


def reorder(x, seg, n_seg):
    width = x.shape[1] // n_seg
    bit = 1
    while bit < n_seg:
        moved = jnp.concatenate([x[:, (b ^ bit) * width : ((b ^ bit) + 1) * width] for b in range(n_seg)], axis=1)
        x = jnp.where((seg & bit) != 0, moved, x)
        bit *= 2
    return x


def own_columns(x, seg, n_seg):
    width = x.shape[1] // n_seg
    out = x[:, :width]
    for b in range(1, n_seg):
        out = jnp.where(seg == b, x[:, b * width : (b + 1) * width], out)
    return out


def prep_kernel(meta_ref, wq_ref, wk_ref, wv_ref, *refs, n_seg, chunks):
    vec_refs, (w_ref, b_ref, out_ref, line_ref, sems) = refs[: EXP_B + 1], refs[EXP_B + 1 :]
    copies = [pltpu.make_async_copy(r, out_ref.at[i], sems.at[i]) for i, r in enumerate(vec_refs[:EXP_B])]
    copies.append(pltpu.make_async_copy(vec_refs[EXP_B], line_ref.at[0], sems.at[EXP_B]))
    for c in copies:
        c.start()
    seg = seg_here()
    w_ref[...] = jnp.concatenate([own_columns(r[...], seg, n_seg) for r in (wq_ref, wk_ref, wv_ref)], axis=1)
    for c in copies:
        c.wait()
    wide = out_ref.shape[1]
    for q in range(chunks):
        out_ref[EXP_B + q : EXP_B + q + 1] = line_ref[:, q * wide : (q + 1) * wide]
    q_b = own_columns(out_ref[Q_B : Q_B + 1], seg, n_seg)
    v_b = own_columns(out_ref[V_B : V_B + 1], seg, n_seg)
    b_ref[...] = jnp.concatenate([q_b, jnp.zeros_like(q_b), v_b], axis=1)


def qkv_kernel(meta_ref, w_ref, b_ref, *refs):
    rows, out_ref = refs[:-1], refs[-1]
    size = rows[0].shape[0]
    for b, r in enumerate(rows):
        out_ref[b * size : (b + 1) * size, :] = (mm(r[...], w_ref[...]) + b_ref[...]).astype(BF16)


def key_columns(meta_ref, slot, blocks, size, mem):
    total = blocks * size + 2 * mem
    col = lax.broadcasted_iota(jnp.int32, (1, total), 1)
    place = col
    for b in range(blocks):
        inside = (col >= b * size) & (col < (b + 1) * size)
        place = jnp.where(inside, ((seg_here() ^ b) - b) * size + col, place)
    return (place < meta_ref[VALID + slot]) | (col >= blocks * size)


def attn_fwd_kernel(meta_ref, qkv_ref, mem_ref, w_ref, b_ref, *outs, slot, blocks, heads, mem_queries):
    if mem_queries:
        memory = mem_ref[...]
    else:
        written_ref, outs = outs[0], outs[1:]
        memory = jnp.where(meta_ref[FRESH] == 1, mem_ref[...], written_ref[...].astype(BF16))
        outs[-1][...] = memory
    mix_refs, lse_ref, mem_out_ref = outs[:blocks], outs[blocks], outs[blocks + 1]
    size = qkv_ref.shape[0] // blocks
    mem = mem_ref.shape[0]
    width = qkv_ref.shape[1] // 3
    head_dim = width // heads
    mem_out_ref[...] = (mm(memory, w_ref[...]) + b_ref[...]).astype(BF16)
    keep = key_columns(meta_ref, slot, blocks, size, mem)
    for h in range(heads):
        lo, hi = h * head_dim, (h + 1) * head_dim
        mem_key = mem_out_ref[:, width + lo : width + hi]
        mem_value = mem_out_ref[:, 2 * width + lo : 2 * width + hi]
        key = jnp.concatenate([qkv_ref[:, width + lo : width + hi], mem_key, mem_key], axis=0)
        value = jnp.concatenate([qkv_ref[:, 2 * width + lo : 2 * width + hi], mem_value, mem_value], axis=0)

        def one(query):
            scores = jnp.where(keep, mm(query, key, NT) * 0.125, NEG_FILL)
            highest = jnp.max(scores, axis=-1, keepdims=True)
            weights = jnp.exp(scores - highest)
            total = jnp.sum(weights, axis=-1, keepdims=True)
            probs = (weights * (1.0 / total)).astype(BF16)
            return mm(probs, value).astype(BF16), highest + jnp.log(total)

        for b in range(blocks):
            mixed, lse = one(qkv_ref[b * size : (b + 1) * size, lo:hi])
            mix_refs[b][:size, lo:hi] = mixed
            lse_ref[b * size : (b + 1) * size, h : h + 1] = lse
        if mem_queries:
            mixed, lse = one(mem_out_ref[:, lo:hi])
            for b in range(blocks):
                mix_refs[b][size:, lo:hi] = mixed
            lse_ref[blocks * size : blocks * size + mem, h : h + 1] = lse


def attn_bwd_kernel(meta_ref, qkv_ref, mem_ref, lse_ref, *refs, slot, blocks, heads, mem_queries):
    n_grad = blocks + (1 if mem_queries else 0)
    grad_refs, refs = refs[:n_grad], refs[n_grad:]
    more_refs, out_refs, mem_out_ref = refs[: -blocks - 1], refs[-blocks - 1 : -1], refs[-1]
    for more_ref, out_ref in zip(more_refs, out_refs):
        out_ref[out_ref.shape[0] - more_ref.shape[0] :, :] = more_ref[...]
    size = qkv_ref.shape[0] // blocks
    first = slot * (qkv_ref.shape[1] // 3)
    mem = mem_ref.shape[0]
    width = qkv_ref.shape[1] // 3
    head_dim = width // heads
    keep = key_columns(meta_ref, slot, blocks, size, mem)
    for h in range(heads):
        lo, hi = h * head_dim, (h + 1) * head_dim
        mem_key = mem_ref[:, width + lo : width + hi]
        mem_value = mem_ref[:, 2 * width + lo : 2 * width + hi]
        key = jnp.concatenate([qkv_ref[:, width + lo : width + hi], mem_key, mem_key], axis=0)
        value = jnp.concatenate([qkv_ref[:, 2 * width + lo : 2 * width + hi], mem_value, mem_value], axis=0)

        def one(query, grad, lse):
            scores = jnp.where(keep, mm(query, key, NT) * 0.125, NEG_FILL)
            probs = jnp.exp(scores - lse)
            grad_probs = mm(grad, value, NT)
            inner = jnp.sum(grad_probs * probs, axis=-1, keepdims=True)
            grad_scores = (probs * (grad_probs - inner)).astype(BF16)
            grad_query = (mm(grad_scores, key) * 0.125).astype(BF16)
            return grad_query, mm(grad_scores, query, TN), mm(probs.astype(BF16), grad, TN)

        grad_key = grad_value = None
        for b in range(n_grad):
            if b < blocks:
                query = qkv_ref[b * size : (b + 1) * size, lo:hi]
                lse = lse_ref[b * size : (b + 1) * size, h : h + 1]
            else:
                query = mem_ref[:, lo:hi]
                lse = lse_ref[blocks * size : blocks * size + mem, h : h + 1]
            grad = grad_refs[b][:, first + lo : first + hi] if b < blocks else grad_refs[b][:, lo:hi]
            grad_query, key_part, value_part = one(query, grad, lse)
            grad_key = key_part if grad_key is None else grad_key + key_part
            grad_value = value_part if grad_value is None else grad_value + value_part
            if b < blocks:
                out_refs[b][:size, lo:hi] = grad_query
            else:
                mem_out_ref[:, lo:hi] = grad_query
        if not mem_queries:
            mem_out_ref[:, lo:hi] = jnp.zeros((mem, head_dim), BF16)
        grad_key = (grad_key * 0.125).astype(BF16)
        grad_value = grad_value.astype(BF16)
        for b in range(blocks):
            out_refs[b][:size, width + lo : width + hi] = grad_key[b * size : (b + 1) * size]
            out_refs[b][:size, 2 * width + lo : 2 * width + hi] = grad_value[b * size : (b + 1) * size]
        mem_out_ref[:, width + lo : width + hi] = grad_key[blocks * size : blocks * size + mem]
        mem_out_ref[:, 2 * width + lo : 2 * width + hi] = grad_value[blocks * size : blocks * size + mem]


def norm_parts(hidden):
    center = hidden - jnp.mean(hidden, axis=-1, keepdims=True)
    inverse = lax.rsqrt(jnp.mean(center * center, axis=-1, keepdims=True) + EPS)
    return center * inverse, inverse


def norm_back(grad, gain, unit, inverse):
    scaled = grad * gain
    mean_scaled = jnp.mean(scaled, axis=-1, keepdims=True)
    mean_product = jnp.mean(scaled * unit, axis=-1, keepdims=True)
    return inverse * (scaled - mean_scaled - unit * mean_product)


def gelu_and_slope(pre):
    cdf = 0.5 * (1.0 + lax.erf(pre * (2.0**-0.5)))
    density = jnp.exp(-0.5 * pre * pre) * 0.3989422804014327
    return pre * cdf, cdf + pre * density


N_KEPT = 4


def rows_fwd_kernel(meta_ref, *refs, n_seg, n_pair, n_hidden):
    mix_refs, hid_refs = refs[:n_seg], refs[n_seg : n_seg + n_hidden]
    vec_ref, out_ref, exp_ref, red_ref = refs[n_seg + n_hidden : n_seg + n_hidden + 4]
    outs = refs[n_seg + n_hidden + 4 :]
    unit_a_ref, inv_ref, slope_ref, unit_f_ref = outs[:N_KEPT]
    result_refs, left_refs = outs[N_KEPT : N_KEPT + n_hidden], outs[N_KEPT + n_hidden :]
    wide = out_ref.shape[0]
    size = hid_refs[0].shape[0]

    def vec(i):
        return vec_ref[i : i + 1]

    def keep_left(x, at, first, blocks):
        left_factors(meta_ref, x, left_refs, at, first, blocks, n_seg, n_pair, size)

    each = wide // (n_seg * n_pair * 2)
    mixed = reorder(jnp.concatenate([r[...] for r in mix_refs], axis=1), seg_here(), n_seg)
    hidden = jnp.concatenate([r[...].astype(F32) for r in hid_refs], axis=0)
    unit, inverse = norm_parts(hidden + (mm(mixed, out_ref[...]) + vec(OUT_B)))
    unit_a_ref[...] = unit
    inv_ref[:, 0:1] = inverse
    normed = unit * vec(ATTN_G) + vec(ATTN_S)
    low = normed.astype(BF16)
    chunks = exp_ref.shape[1] // wide
    acc = normed + vec(RED_B)
    for q in range(chunks):
        cols = slice(q * wide, (q + 1) * wide)
        active, slope = gelu_and_slope(mm(low, exp_ref[:, cols]) + vec(EXP_B + q))
        slope_ref[:, cols] = slope
        active = active.astype(BF16)
        acc = acc + mm(active, red_ref[cols])
        keep_left(active, each, q * n_seg // chunks, n_seg // chunks)
    unit, inverse = norm_parts(acc)
    unit_f_ref[...] = unit
    inv_ref[:, 1:2] = inverse
    result = unit * vec(FIN_G) + vec(FIN_S)
    at = 0
    for r in result_refs:
        r[...] = result[at : at + r.shape[0]].astype(r.dtype)
        at += r.shape[0]
    keep_left(low, 0, 0, n_seg)
    keep_left(mixed, (chunks + 1) * each, 0, n_seg)


def left_factors(meta_ref, x, left_refs, at, first, blocks, n_seg, n_pair, size):
    seg, core, pair = seg_here(), core_here(), pair_here()
    rows = x.shape[1] // (blocks * n_pair * 2)
    keep_ref, send_ref = left_refs[:2]
    keep, send = core_halves(x[:size].astype(F32).T, core, n_pair, rows)
    for s in range(blocks):
        for z in range(n_pair):
            keep_ref[(first + s) ^ seg, z ^ pair, at : at + rows] = keep[s * n_pair + z]
            send_ref[(first + s) ^ seg, z ^ pair, at : at + rows] = send[s * n_pair + z]
    if left_refs[2:]:
        keep_ref, send_ref = left_refs[2:]
        mine = x[size:].astype(F32)
        if blocks > 1:
            assert blocks == n_seg
            mine = own_columns(mine, seg, n_seg)
        keep, send = core_halves(mine.T, core, n_pair, rows)

        @pl.when((seg == first) | (blocks > 1))
        def _():
            for z in range(n_pair):
                keep_ref[z ^ pair, at : at + rows] = keep[z]
                send_ref[z ^ pair, at : at + rows] = send[z]


def core_halves(x, core, pairs, rows):
    x = x.reshape(x.shape[0] // (2 * rows), 2, rows, x.shape[1])
    even, odd = x[:, 0], x[:, 1]
    return jnp.where(core == 0, even, odd).astype(BF16), jnp.where(core == 0, odd, even).astype(BF16)


def rows_back(seg, n_seg, grad, kept, vec_ref, out_ref, exp_ref, red_ref, outs):
    right_ref, hidden_ref, small_ref = outs
    wide = hidden_ref.shape[1]
    chunks = exp_ref.shape[1] // wide

    def vec(i):
        return vec_ref[i : i + 1]

    def total(x):
        return jnp.sum(x, axis=0, keepdims=True)

    unit = kept(3)
    grad_sum = norm_back(grad, vec(FIN_G), unit, kept(1)[:, 1:2])
    low = grad_sum.astype(BF16)
    right_ref[:, chunks * wide : (chunks + 1) * wide] = low
    small_ref[...] = jnp.zeros_like(small_ref)
    small_ref[FIN_G : FIN_G + 1] = total(grad * unit)
    small_ref[FIN_S : FIN_S + 1] = total(grad)
    small_ref[RED_B : RED_B + 1] = total(low.astype(F32))
    acc = grad_sum
    for q in range(chunks):
        cols = slice(q * wide, (q + 1) * wide)
        grad_pre = (mm(low, red_ref[cols], NT) * kept(2, cols)).astype(BF16)
        right_ref[:, cols] = grad_pre
        small_ref[EXP_B + q : EXP_B + q + 1] = total(grad_pre.astype(F32))
        acc = acc + mm(grad_pre, exp_ref[:, cols], NT)
    unit = kept(0)
    small_ref[ATTN_G : ATTN_G + 1] = total(acc * unit)
    small_ref[ATTN_S : ATTN_S + 1] = total(acc)
    grad_hidden = norm_back(acc, vec(ATTN_G), unit, kept(1)[:, 0:1])
    hidden_ref[...] = grad_hidden
    low = grad_hidden.astype(BF16)
    right_ref[:, (chunks + 1) * wide :] = low
    small_ref[OUT_B : OUT_B + 1] = total(low.astype(F32))
    return reorder(mm(low, out_ref[...], NT).astype(BF16), seg, n_seg)


def token_rows_back_kernel(meta_ref, grad_ref, *refs, slots, n_seg):
    kept_refs = [refs[t * N_KEPT : (t + 1) * N_KEPT] for t in range(slots)]
    refs = refs[slots * N_KEPT :]
    (vec_ref, out_ref, exp_ref, red_ref), outs, mix_refs = refs[:4], refs[4:7], refs[7:]
    size = grad_ref.shape[1]

    def kept(i, cols=slice(None)):
        return jnp.concatenate([kept_refs[t][i][:size, cols] for t in range(slots)], axis=0)

    grad = jnp.concatenate([grad_ref[t].astype(F32) for t in range(slots)], axis=0)
    mixed = rows_back(seg_here(), n_seg, grad, kept, vec_ref, out_ref, exp_ref, red_ref, outs)
    width = mixed.shape[1] // n_seg
    for m in range(n_seg):
        for t in range(slots):
            mix_refs[m][:, t * width : (t + 1) * width] = mixed[t * size : (t + 1) * size, m * width : (m + 1) * width]


def memory_rows_back_kernel(meta_ref, *refs, n_seg, size):
    d_refs, refs = refs[:n_seg], refs[n_seg:]
    (wk_ref, wv_ref), kept_refs, refs = refs[:2], refs[2 : 2 + N_KEPT], refs[2 + N_KEPT :]
    (vec_ref, out_ref, exp_ref, red_ref), outs, (memory_ref, own_ref) = refs[:4], refs[4:7], refs[7:]
    seg = seg_here()
    width = d_refs[0].shape[1] // 2
    d_key = reorder(jnp.concatenate([r[:, :width] for r in d_refs], axis=1), seg, n_seg)
    d_value = reorder(jnp.concatenate([r[:, width:] for r in d_refs], axis=1), seg, n_seg)
    grad = 2.0 * (mm(d_key, wk_ref[...], NT) + mm(d_value, wv_ref[...], NT))
    memory_ref[...] = grad
    grad = jnp.where(meta_ref[FRESH] == 1, jnp.zeros_like(grad), grad)

    def kept(i, cols=slice(None)):
        return kept_refs[i][size:, cols]

    mixed = rows_back(seg, n_seg, grad, kept, vec_ref, out_ref, exp_ref, red_ref, outs)
    own_ref[...] = mixed[:, : own_ref.shape[1]]


def tokens_grad_kernel(meta_ref, hidden_ref, wq_ref, wk_ref, wv_ref, *refs, slots, n_seg):
    d_refs, out_ref = refs[:-1], refs[-1]
    size = out_ref.shape[1]
    width = d_refs[0].shape[1] // 3
    seg = seg_here()
    for t in range(slots):
        grad = hidden_ref[t * size : (t + 1) * size]
        for i, w_ref in enumerate((wq_ref, wk_ref, wv_ref)):
            part = jnp.concatenate([r[t * size : (t + 1) * size, i * width : (i + 1) * width] for r in d_refs], 1)
            grad = grad + mm(reorder(part, seg, n_seg), w_ref[...], NT)
        out_ref[t] = grad.astype(BF16)


def row_parts(stream, chunks, each):
    if stream == 0:
        return [(0, each, q, q * each) for q in range(chunks)]
    return [(each, chunks * each, chunks, 0), ((chunks + 1) * each, each, chunks + 1, chunks * each)]


def rows_weights_kernel(meta_ref, *refs, stream, n_seg, n_pair, each):
    left_refs, (right_ref, other_ref), outs = refs[:-6], refs[-6:-4], refs[-4:]
    wide = outs[0].shape[3]
    half = n_pair // 2
    for lo, rows, q, row in row_parts(stream, right_ref.shape[1] // wide - 2, each):
        left = jnp.concatenate(
            [r[:, :, lo : lo + rows].reshape(n_seg * n_pair * rows, r.shape[3]) for r in left_refs], axis=1
        )
        right = jnp.concatenate([r[:, q * wide : (q + 1) * wide] for r in (right_ref, other_ref)], axis=0)
        full = mm(left, right).reshape(n_seg, n_pair, rows, wide).astype(BF16)
        for s in range(n_seg):
            low, high = s & 1, s >> 1
            outs[low][high, :, row : row + rows] = full[s, :half]
            outs[2 + high][low, :, row : row + rows] = full[s, half:]


def quarter_kernel(meta_ref, left_ref, left2_ref, right_ref, right2_ref, *refs, stream, each):
    half_refs, outs = (refs[:2], refs[2:4]), refs[4:]
    wide = outs[0].shape[2]
    pairs = left_ref.shape[0]
    half = pairs // 2
    for lo, rows, q, row in row_parts(stream, right_ref.shape[1] // wide - 2, each):

        def rows_of(r):
            return jnp.concatenate([r[z].astype(F32)[lo : lo + rows] for z in range(pairs)], axis=0)

        left = jnp.concatenate([rows_of(left_ref), rows_of(left2_ref)], axis=1).astype(BF16)
        right = jnp.concatenate([r[:, q * wide : (q + 1) * wide] for r in (right_ref, right2_ref)], axis=0)
        part = mm(left, right).reshape(pairs, rows, wide)
        for z in range(pairs):
            total = part[z]
            for r in half_refs[z // half]:
                total = total + r[z % half, row : row + rows].astype(F32)
            outs[z & 1][z >> 1, row : row + rows] = total.astype(BF16)


def heads_weights_kernel(meta_ref, small_ref, small_m_ref, hid_ref, memory_ref, w_ref, *refs, slots, n_seg):
    rows, refs = refs[: slots * n_seg], refs[slots * n_seg :]
    grads, (mem0_ref, mem1_ref, dm0_ref, dm1_ref, keep_ref, send_ref) = refs[:n_seg], refs[n_seg:]
    seg, core, pair, fresh1 = seg_here(), core_here(), pair_here(), meta_ref[FRESH]
    wide = rows[0].shape[1]
    width = wide // n_seg
    each = keep_ref.shape[2]
    col = lax.broadcasted_iota(jnp.int32, (1, 3 * width), 1)
    twice = jnp.where(col < width, 1.0, 2.0)
    dm0 = (dm0_ref[...].astype(F32) * twice).astype(BF16)
    dm1 = (dm1_ref[...].astype(F32) * twice).astype(BF16)
    full = mm(mem0_ref[...], dm0, TN) + mm(mem1_ref[...], dm1, TN)
    sums = jnp.sum(dm0.astype(F32), axis=0, keepdims=True) + jnp.sum(dm1.astype(F32), axis=0, keepdims=True)
    for m, g in enumerate(grads):
        x = jnp.concatenate([r[...] for r in rows[m::n_seg]], axis=0)
        full = full + mm(x, g[...], TN)
        sums = sums + jnp.sum(g[...].astype(F32), axis=0, keepdims=True)
    grad_mem = mm(dm0, w_ref[...], NT)
    whole = hid_ref[...] + jnp.where(fresh1 == 1, memory_ref[...], 0.0)
    grad_mem = grad_mem + jnp.where(seg == 0, whole, 0.0)

    def placed(v):
        return reorder(jnp.concatenate([v, jnp.zeros((1, wide - width), F32)], axis=1), seg, n_seg)

    n_pair = keep_ref.shape[0]
    chunks = 4
    head = EXP_B + chunks
    given = small_ref[...] + jnp.where(seg == 0, small_m_ref[...], 0.0)
    small = jnp.concatenate(
        [
            placed(sums[:, :width]),
            placed(sums[:, 2 * width :]),
            given[2:head],
            grad_mem,
            jnp.zeros((N_SMALL - head - grad_mem.shape[0], wide), F32),
        ],
        axis=0,
    ).T
    turned = small.reshape(wide // (chunks * each), chunks, each, N_SMALL)
    spread = [
        jnp.concatenate(
            [turned[:, k, :, EXP_B + q : EXP_B + q + 1].reshape(wide // chunks, 1) for k in range(chunks)], axis=1
        )
        for q in range(chunks)
    ]
    small = jnp.concatenate([small[:, :EXP_B], jnp.concatenate(spread, axis=0), small[:, head:]], axis=1)
    high = small.astype(BF16)
    rest = (small - high.astype(F32)).astype(BF16)
    full = jnp.concatenate([full, high.astype(F32), rest.astype(F32)], axis=1)
    keep, send = core_halves(full, core, n_pair, each)
    for s in range(n_seg):
        for z in range(n_pair):
            keep_ref[z ^ pair, s ^ seg] = keep[s * n_pair + z]
            send_ref[z ^ pair, s ^ seg] = send[s * n_pair + z]


def late_sum(*parts, at):
    total = sum(p.astype(F32) for p in parts)
    small = total[..., at : at + N_SMALL] + total[..., at + N_SMALL :]
    high = small.astype(BF16)
    rest = (small - high.astype(F32)).astype(BF16)
    return jnp.concatenate([total[..., :at].astype(BF16), high, rest], axis=-1)


def heads_final_kernel(meta_ref, *refs, n_seg, mem):
    ins, outs = refs[:n_seg], refs[n_seg:]
    seg = seg_here()
    width = outs[0].shape[1] // n_seg
    total = [r[...].astype(F32) for r in ins]
    for i in range(3):
        outs[i][...] = reorder(
            jnp.concatenate([total[m][:, i * width : (i + 1) * width] for m in range(n_seg)], axis=1), seg, n_seg
        )
    at = 3 * width
    small = sum(t[:, at : at + N_SMALL] + t[:, at + N_SMALL : at + 2 * N_SMALL] for t in total).T
    vec_refs, exp_ref, mem_ref = outs[3 : 3 + EXP_B], outs[3 + EXP_B], outs[4 + EXP_B]
    for i, r in enumerate(vec_refs):
        r[...] = small[i : i + 1]
    exp_ref[...] = jnp.concatenate([small[EXP_B + q : EXP_B + q + 1] for q in range(4)], axis=1)
    mem_ref[...] = small[EXP_B + 4 : EXP_B + 4 + mem]


def rows_final_kernel(meta_ref, first_ref, second_ref, *outs):
    total = first_ref[...].astype(F32) + second_ref[...].astype(F32)
    wide = total.shape[1]
    at = 0
    for r in outs:
        for q in range(r.shape[1] // wide):
            r[:, q * wide : (q + 1) * wide] = total[at : at + r.shape[0]]
            at += r.shape[0]


def shards(
    tokens,
    new_doc,
    valid_len,
    mem_init,
    query_proj,
    query_bias,
    key_proj,
    value_proj,
    value_bias,
    output_proj,
    output_bias,
    attn_gain,
    attn_shift,
    expand_proj,
    expand_bias,
    reduce_proj,
    reduce_bias,
    final_gain,
    final_shift,
    d_out,
):
    slots, size, wide = tokens.shape
    assert slots == 2
    n_seg, n_doc = lax.axis_size("seg"), lax.axis_size("doc")
    n_pair = n_doc // 2
    hidden_units = expand_proj.shape[1]
    chunks = hidden_units // wide
    assert chunks == 4
    mem = mem_init.shape[0]
    width = wide // n_seg
    heads = HEADS // n_seg
    others = range(1, n_seg)
    all_rows = n_seg * size

    rows0 = [tokens[0]] + [swap(tokens[0], "seg", m) for m in others]
    place = jnp.concatenate([new_doc, valid_len])
    w_own, b_own, vecs = call(
        functools.partial(prep_kernel, n_seg=n_seg, chunks=chunks),
        [shape_of(wide, 3 * width), shape_of(1, 3 * width, dtype=F32), shape_of(N_VEC, wide, dtype=F32)],
        (
            place,
            query_proj,
            key_proj,
            value_proj,
            query_bias,
            value_bias,
            output_bias,
            attn_gain,
            attn_shift,
            reduce_bias,
            final_gain,
            final_shift,
            expand_bias,
        ),
        4,
        far_in=range(4, 5 + EXP_B),
        scratch=[pltpu.VMEM((1, hidden_units), F32), pltpu.SemaphoreType.DMA((EXP_B + 1,))],
    )

    second, w_own, *rows0 = lax.optimization_barrier((tokens[1], w_own, *rows0))
    rows = [rows0, [second] + [swap(second, "seg", m) for m in others]]

    def project(t):
        (out,) = call(qkv_kernel, [shape_of(all_rows, 3 * width)], (place, w_own, b_own, *rows[t]), 3)
        return out

    def attend(t, qkv, written=()):
        mem_queries = not written
        got = call(
            functools.partial(attn_fwd_kernel, slot=t, blocks=n_seg, heads=heads, mem_queries=mem_queries),
            [shape_of(size + (mem if mem_queries else 0), width)] * n_seg
            + [shape_of(all_rows + mem, 128, dtype=F32), shape_of(mem, 3 * width)]
            + [shape_of(mem, wide)] * len(written),
            (place, qkv, mem_init, w_own, b_own, *written),
            8,
        )
        return list(got[:n_seg]), *got[n_seg:]

    def attend_back(t, qkv, qkv_mem, lse, grads, more=()):
        got = call(
            functools.partial(attn_bwd_kernel, slot=t, blocks=n_seg, heads=heads, mem_queries=len(grads) > n_seg),
            [shape_of(size * (2 if more else 1), 3 * width)] * n_seg + [shape_of(mem, 3 * width)],
            (place, qkv, qkv_mem, lse, *grads, *more),
            8,
        )
        return list(got[:n_seg]), got[n_seg]

    def trade(blocks):
        return [blocks[0]] + [swap(blocks[m], "seg", m) for m in others]

    weights = (vecs, output_proj, expand_proj, reduce_proj)
    each = wide // (n_seg * n_doc)

    def rows_forward(mixed, hidden, result_shapes):
        n_rows = sum(h.shape[0] for h in hidden)
        left = [shape_of(n_seg, n_pair, (chunks + 2) * each, size)] * 2
        if len(hidden) > 1:
            left += [shape_of(n_pair, (chunks + 2) * each, mem)] * 2
        got = call(
            functools.partial(rows_fwd_kernel, n_seg=n_seg, n_pair=n_pair, n_hidden=len(hidden)),
            [
                shape_of(n_rows, wide, dtype=F32),
                shape_of(n_rows, 128, dtype=F32),
                shape_of(n_rows, hidden_units, dtype=F32),
                shape_of(n_rows, wide, dtype=F32),
                *result_shapes,
                *left,
            ],
            (place, *mixed, *hidden, *weights),
            8,
        )
        return got[:N_KEPT], got[N_KEPT : N_KEPT + len(hidden)], got[N_KEPT + len(hidden) :]

    qkv0 = project(0)
    mixed0, lse0, qkv_mem0 = attend(0, qkv0)
    mixed0[0], *rows[1] = lax.optimization_barrier((mixed0[0], *rows[1]))
    qkv1 = project(1)
    mixed0 = trade(mixed0)
    qkv1, mixed0[0] = lax.optimization_barrier((qkv1, mixed0[0]))
    kept0, (layer0, written), (left0, left0_send, left_m, left_m_send) = rows_forward(
        mixed0, (tokens[0], mem_init), [shape_of(size, wide), shape_of(mem, wide, dtype=F32)]
    )
    mixed1, lse1, qkv_mem1, memory1 = attend(1, qkv1, (written,))
    left0_other, left_m_other = swap(left0_send, "doc", 1), swap(left_m_send, "doc", 1)
    mixed1[0], left0_other, left_m_other = lax.optimization_barrier((mixed1[0], left0_other, left_m_other))
    kept1, (layer1,), (left1, left1_send) = rows_forward(trade(mixed1), (tokens[1],), [shape_of(size, wide)])
    left1_other = swap(left1_send, "doc", 1)
    layer_out = jnp.stack([layer0, layer1])

    def back_shapes(n_rows):
        return [
            shape_of(n_rows, hidden_units + 2 * wide),
            shape_of(n_rows, wide, dtype=F32),
            shape_of(N_VEC, wide, dtype=F32),
        ]

    n_rows = slots * size
    got = call(
        functools.partial(token_rows_back_kernel, slots=slots, n_seg=n_seg),
        back_shapes(n_rows) + [shape_of(size, slots * width)] * n_seg,
        (place, d_out, *kept0, *kept1, *weights),
        10,
    )
    right, hidden, small = got[:3]
    grads = trade(got[3:])
    right_other = swap(right, "doc", 1)
    right, left1_other = lax.optimization_barrier((right, left1_other))

    def plain_sum(*parts):
        return sum(p.astype(F32) for p in parts).astype(BF16)

    share = [chunks * each, (chunks + 1) * each]

    def row_weights(stream, right_other):
        return call(
            functools.partial(rows_weights_kernel, stream=stream, n_seg=n_seg, n_pair=n_pair, each=each),
            [shape_of(n_seg // 2, n_pair // 2, share[stream], wide)] * 4,
            (place, left0, left1, left0_other, left1_other, right, right_other),
            2,
        )

    def both_sums(keep_a, came_a, keep_b, came_b):
        return [plain_sum(k[i], c[i]) for k, c in ((keep_a, came_a), (keep_b, came_b)) for i in range(2)]

    keep_a, send_a, keep_b, send_b = row_weights(0, right_other)
    send_a, send_b, *grads = lax.optimization_barrier((send_a, send_b, *grads))
    came_a, came_b = swap(send_a, "seg", 1), swap(send_b, "seg", 2)
    d_qkv1, d_mem1 = attend_back(1, qkv1, qkv_mem1, lse1, grads)
    d_mem1_all = trade([d_mem1[:, width:]] * n_seg)

    right_other, d_mem1_all[0] = lax.optimization_barrier((right_other, d_mem1_all[0]))
    keep_c, send_c, keep_d, send_d = row_weights(1, right_other)
    send_c, send_d, came_a, came_b, *d_mem1_all = lax.optimization_barrier(
        (send_c, send_d, came_a, came_b, *d_mem1_all)
    )
    keep_a, send_a, keep_b, send_b = both_sums(keep_a, came_a, keep_b, came_b)
    send_a, send_b, d_mem1_all[0] = lax.optimization_barrier((send_a, send_b, d_mem1_all[0]))
    came_a, came_b = swap(send_a, "seg", 2), swap(send_b, "seg", 1)

    got = call(
        functools.partial(memory_rows_back_kernel, n_seg=n_seg, size=size),
        back_shapes(mem) + [shape_of(mem, wide, dtype=F32), shape_of(mem, width)],
        (place, *d_mem1_all, key_proj, value_proj, *kept0, *weights),
        6,
    )
    right_m, hidden_m, small_m, memory1_grad, mixed_m = got
    right_m_other = swap(right_m, "doc", 1)
    def pair_sum(keep, came, add):
        bit = 2
        while keep.shape[0] > 1:
            bit *= 2
            if keep.shape[0] == 2:
                (keep, send) = [add(keep[i : i + 1], came[i : i + 1]) for i in range(2)]
            else:
                both = add(keep, came)
                keep, send = both[0::2], both[1::2]
            came = swap(send, "doc", bit)
        return [keep[0], came[0]]

    def quarter(stream, *halves):
        keep, send = call(
            functools.partial(quarter_kernel, stream=stream, each=each),
            [shape_of(n_pair // 2, share[stream], wide)] * 2,
            (place, left_m, left_m_other, right_m, right_m_other, *halves),
            1,
        )
        return keep, send

    right_m, came_a, came_b, send_c, send_d = lax.optimization_barrier((right_m, came_a, came_b, send_c, send_d))
    came_c, came_d = swap(send_c, "seg", 1), swap(send_d, "seg", 2)
    keep_x, send_x = quarter(0, keep_a, came_a, keep_b, came_b)
    send_x, mixed_m = lax.optimization_barrier((send_x, mixed_m))
    came_x = swap(send_x, "doc", 2)
    d_qkv, d_mem0 = attend_back(0, qkv0, qkv_mem0, lse0, [*grads, mixed_m], d_qkv1)

    came_x, d_mem0 = lax.optimization_barrier((came_x, d_mem0))
    parts_exp = pair_sum(keep_x, came_x, plain_sum)

    columns = 3 * width + 2 * N_SMALL
    keep, send = call(
        functools.partial(heads_weights_kernel, slots=slots, n_seg=n_seg),
        [shape_of(n_pair, n_seg, each, columns)] * 2,
        (
            place,
            small,
            small_m,
            hidden_m,
            memory1_grad,
            w_own,
            *rows[0],
            *rows[1],
            *d_qkv,
            mem_init,
            memory1,
            d_mem0,
            d_mem1,
        ),
        6,
    )

    def rows_final(parts, *shapes):
        return call(
            rows_final_kernel,
            [shape_of(*dims, dtype=F32) for dims in shapes],
            (place, *parts),
            1,
            far_out=range(len(shapes)),
        )

    add = functools.partial(late_sum, at=3 * width)
    came_c, came_d, parts_exp[1], keep, send = lax.optimization_barrier((came_c, came_d, parts_exp[1], keep, send))
    keep_c, send_c, keep_d, send_d = both_sums(keep_c, came_c, keep_d, came_d)
    came = swap(send, "doc", 1)
    send_c, send_d, came = lax.optimization_barrier((send_c, send_d, came))
    came_c, came_d = swap(send_c, "seg", 2), swap(send_d, "seg", 1)
    mine = add(keep, came)
    came_l = swap(mine[1::2], "doc", 2)
    came_c, came_d, came_l, *d_qkv = lax.optimization_barrier((came_c, came_d, came_l, *d_qkv))
    late = pair_sum(mine[0::2], came_l, add)
    keep_y, send_y = quarter(1, keep_c, came_c, keep_d, came_d)
    parts_rest = pair_sum(keep_y, swap(send_y, "doc", 2), plain_sum)
    (grad_exp,) = rows_final(parts_exp, (each, hidden_units))

    back = trade(d_qkv)
    (grad_tokens,) = call(
        functools.partial(tokens_grad_kernel, slots=slots, n_seg=n_seg),
        [shape_of(slots, size, wide)],
        (place, hidden, query_proj, key_proj, value_proj, *back),
        3,
        far_out=(0,),
    )

    mine = add(*late)
    parts = trade([mine[m] for m in range(n_seg)])
    got = call(
        functools.partial(heads_final_kernel, n_seg=n_seg, mem=mem),
        [shape_of(each, wide, dtype=F32)] * 3
        + [shape_of(1, each, dtype=F32)] * EXP_B
        + [shape_of(1, chunks * each, dtype=F32), shape_of(mem, each, dtype=F32)],
        (place, *parts),
        1,
        far_out=range(5 + EXP_B),
    )
    parts_rest[1], grad_exp, grad_tokens, layer_out = lax.optimization_barrier(
        (parts_rest[1], grad_exp, grad_tokens, layer_out)
    )
    grad_red, grad_out = rows_final(parts_rest, (chunks * each, wide), (each, wide))
    grad_q, grad_k, grad_v = got[:3]
    flat = [v.reshape(-1) for v in got[3:-1]]

    return (
        layer_out,
        grad_tokens,
        got[-1],
        grad_q,
        flat[Q_B],
        grad_k,
        grad_v,
        flat[V_B],
        grad_out,
        flat[OUT_B],
        flat[ATTN_G],
        flat[ATTN_S],
        grad_exp,
        flat[EXP_B],
        grad_red,
        flat[RED_B],
        flat[FIN_G],
        flat[FIN_S],
    )


def solution(mesh):
    both = ("seg", "doc")
    data = P("doc", "seg", None)
    placed = (data, P("doc"), P("doc")) + (P(),) * 16 + (data,)
    vec, mat = P(both), P(both, None)
    return jax.shard_map(
        shards,
        mesh=mesh,
        in_specs=placed,
        out_specs=(
            data,
            data,
            P(None, both),
            mat,
            vec,
            mat,
            mat,
            vec,
            mat,
            vec,
            vec,
            vec,
            mat,
            vec,
            mat,
            vec,
            vec,
            vec,
        ),
        check_vma=False,
    )
```

```python
import functools

import jax
import jax.numpy as jnp
from jax import lax
from jax.experimental import pallas as pl
from jax.experimental.pallas import tpu as pltpu
from jax.sharding import PartitionSpec as P

HEADS = 12


EPS = 1e-12
NEG_FILL = -1e30
F32 = jnp.float32
BF16 = jnp.bfloat16
NN = (((1,), (0,)), ((), ()))
NT = (((1,), (1,)), ((), ()))
TN = (((0,), (0,)), ((), ()))

Q_B, V_B, OUT_B, ATTN_G, ATTN_S, RED_B, FIN_G, FIN_S, EXP_B = range(9)
FRESH, VALID = 1, 2
N_VEC = 16
N_SMALL = 32


def mm(left, right, dims=NN):
    return lax.dot_general(left, right, dims, preferred_element_type=F32)


def swap(block, axis, mask):
    return lax.ppermute(block, axis, [(i, i ^ mask) for i in range(lax.axis_size(axis))])


def seg_here():
    return lax.axis_index("seg")


def core_here():
    return lax.axis_index("doc") & 1


def pair_here():
    return lax.axis_index("doc") >> 1


def shape_of(*dims, dtype=BF16):
    return jax.ShapeDtypeStruct(dims, dtype)


def call(kernel, out_shape, args, micros, far_in=(), far_out=(), scratch=()):
    vmem, far = pl.BlockSpec(memory_space=pltpu.VMEM), pl.BlockSpec(memory_space=pltpu.HBM)
    near = [
        x if i == 0 else pltpu.with_memory_space_constraint(x, pltpu.HBM if i in far_in else pltpu.VMEM)
        for i, x in enumerate(args)
    ]
    return pl.pallas_call(
        kernel,
        out_shape=[o if i in far_out else pltpu.VMEM(o.shape, o.dtype) for i, o in enumerate(out_shape)],
        in_specs=[pl.BlockSpec(memory_space=pltpu.SMEM)]
        + [far if i in far_in else vmem for i in range(1, len(args))],
        out_specs=[vmem] * len(out_shape),
        scratch_shapes=scratch,
        compiler_params=pltpu.CompilerParams(vmem_limit_bytes=8 << 20),
        cost_estimate=pl.CostEstimate(flops=0, transcendentals=0, bytes_accessed=int(micros * 3e6)),
    )(*near)


def reorder(x, seg, n_seg):
    width = x.shape[1] // n_seg
    bit = 1
    while bit < n_seg:
        moved = jnp.concatenate([x[:, (b ^ bit) * width : ((b ^ bit) + 1) * width] for b in range(n_seg)], axis=1)
        x = jnp.where((seg & bit) != 0, moved, x)
        bit *= 2
    return x


def in_loop(count, together, step):
    def some(j, carry):
        for k in range(together):
            step(j * together + k)
        return carry

    lax.fori_loop(0, count // together, some, 0)


def own_columns(x, seg, n_seg):
    width = x.shape[1] // n_seg
    out = x[:, :width]
    for b in range(1, n_seg):
        out = jnp.where(seg == b, x[:, b * width : (b + 1) * width], out)
    return out


def prep_kernel(meta_ref, wq_ref, wk_ref, wv_ref, *refs, n_seg, chunks):
    vec_refs, (w_ref, b_ref, out_ref, line_ref, sems) = refs[: EXP_B + 1], refs[EXP_B + 1 :]
    copies = [pltpu.make_async_copy(r, out_ref.at[i], sems.at[i]) for i, r in enumerate(vec_refs[:EXP_B])]
    copies.append(pltpu.make_async_copy(vec_refs[EXP_B], line_ref.at[0], sems.at[EXP_B]))
    for c in copies:
        c.start()
    seg = seg_here()
    rows = w_ref.shape[0] // 8

    def some_rows(i):
        these = pl.ds(pl.multiple_of(i * rows, rows), rows)
        w_ref[these] = jnp.concatenate([own_columns(r[these], seg, n_seg) for r in (wq_ref, wk_ref, wv_ref)], axis=1)

    in_loop(8, 1, some_rows)
    for c in copies:
        c.wait()
    wide = out_ref.shape[1]
    for q in range(chunks):
        out_ref[EXP_B + q : EXP_B + q + 1] = line_ref[:, q * wide : (q + 1) * wide]
    q_b = own_columns(out_ref[Q_B : Q_B + 1], seg, n_seg)
    v_b = own_columns(out_ref[V_B : V_B + 1], seg, n_seg)
    b_ref[...] = jnp.concatenate([q_b, jnp.zeros_like(q_b), v_b], axis=1)


def qkv_kernel(meta_ref, w_ref, b_ref, *refs):
    rows, out_ref = refs[:-1], refs[-1]
    size = rows[0].shape[0]
    for b, r in enumerate(rows):
        out_ref[b * size : (b + 1) * size, :] = (mm(r[...], w_ref[...]) + b_ref[...]).astype(BF16)


def mask_block(meta_ref, slot, blocks, size, mem, width):
    total = blocks * size + 2 * mem
    row = lax.broadcasted_iota(jnp.int32, (total, width), 0)
    col = lax.broadcasted_iota(jnp.int32, (total, width), 1)
    place = row
    for b in range(blocks):
        inside = (row >= b * size) & (row < (b + 1) * size)
        place = jnp.where(inside, ((seg_here() ^ b) - b) * size + row, place)
    out = (place >= meta_ref[VALID + slot]) & (row < blocks * size) & (col == 0)
    return jnp.where(out, NEG_FILL, 0.0).astype(BF16)


def ones_block(rows, width):
    col = lax.broadcasted_iota(jnp.int32, (rows, width), 1)
    return jnp.where(col == 0, 1.0, 0.0).astype(BF16)


def with_memory(rows, memory):
    return jnp.concatenate([rows, memory, memory], axis=0)


SCALE = 0.125 * 1.4426950408889634


def attn_fwd_kernel(meta_ref, qkv_ref, mem_ref, w_ref, b_ref, *outs, slot, blocks, heads, mem_queries):
    if mem_queries:
        memory = mem_ref[...]
    else:
        written_ref, outs = outs[0], outs[1:]
        memory = jnp.where(meta_ref[FRESH] == 1, mem_ref[...], written_ref[...].astype(BF16))
        outs[-1][...] = memory
    mix_refs, lse_ref, mem_out_ref = outs[:blocks], outs[blocks], outs[blocks + 1]
    size = qkv_ref.shape[0] // blocks
    mem = mem_ref.shape[0]
    width = qkv_ref.shape[1] // 3
    head_dim = width // heads
    mem_out_ref[...] = (mm(memory, w_ref[...]) + b_ref[...]).astype(BF16)
    mask = mask_block(meta_ref, slot, blocks, size, mem, head_dim)
    ones = ones_block(size, head_dim)
    value_t = with_memory(qkv_ref[:, 2 * width :], mem_out_ref[:, 2 * width :]).T
    keys = []
    for h in range(heads):
        cols = slice(width + h * head_dim, width + (h + 1) * head_dim)
        keys.append(jnp.concatenate([with_memory(qkv_ref[:, cols], mem_out_ref[:, cols]), mask], axis=1))

    def mixed_of(queries, ones, first):
        out = []
        for h in range(heads):
            lo, hi = h * head_dim, (h + 1) * head_dim
            scores = mm(keys[h], jnp.concatenate([queries[:, lo:hi], ones], axis=1), NT)
            highest = jnp.max(scores, axis=0, keepdims=True)
            weights = jnp.exp2((scores - highest) * SCALE)
            total = jnp.sum(weights, axis=0, keepdims=True)
            out.append(mm(value_t[lo:hi], weights.astype(BF16)) * (1.0 / total))
            lse_ref[h : h + 1, first : first + queries.shape[0]] = highest * SCALE + jnp.log(total) * 1.4426950408889634
        return jnp.concatenate(out, axis=0).T.astype(BF16)

    for b in range(blocks):
        mix_refs[b][:size] = mixed_of(qkv_ref[b * size : (b + 1) * size, :width], ones, b * size)
    if mem_queries:
        mixed = mixed_of(mem_out_ref[:, :width], ones[:mem], blocks * size)
        for b in range(blocks):
            mix_refs[b][size:] = mixed


def attn_bwd_kernel(meta_ref, qkv_ref, mem_ref, lse_ref, *refs, slot, blocks, heads, mem_queries):
    n_grad = blocks + (1 if mem_queries else 0)
    grad_refs, refs = refs[:n_grad], refs[n_grad:]
    more_refs, out_refs, mem_out_ref = refs[: -blocks - 1], refs[-blocks - 1 : -1], refs[-1]
    for more_ref, out_ref in zip(more_refs, out_refs):
        out_ref[out_ref.shape[0] - more_ref.shape[0] :, :] = more_ref[...]
    size = qkv_ref.shape[0] // blocks
    mem = mem_ref.shape[0]
    width = qkv_ref.shape[1] // 3
    first = slot * width
    head_dim = width // heads
    own = blocks * size + mem
    mask = mask_block(meta_ref, slot, blocks, size, mem, head_dim)
    ones = ones_block(size, head_dim)
    key_t = with_memory(qkv_ref[:, width : 2 * width], mem_ref[:, width : 2 * width]).T
    grad_q = [[] for _ in range(n_grad)]
    for h in range(heads):
        lo, hi = h * head_dim, (h + 1) * head_dim
        key = with_memory(qkv_ref[:, width + lo : width + hi], mem_ref[:, width + lo : width + hi])
        key = jnp.concatenate([key, mask], axis=1)
        value = with_memory(qkv_ref[:, 2 * width + lo : 2 * width + hi], mem_ref[:, 2 * width + lo : 2 * width + hi])

        def one(query, ones, grad, lse):
            scores = mm(key, jnp.concatenate([query, ones], axis=1), NT)
            probs = jnp.exp2(scores * SCALE - lse)
            grad_probs = mm(value, grad, NT)
            inner = jnp.sum(grad_probs * probs, axis=0, keepdims=True)
            return (probs * (grad_probs - inner)).astype(BF16), probs.astype(BF16)

        queries, grads, scores_g, probs = [], [], [], []
        for b in range(blocks):
            queries.append(qkv_ref[b * size : (b + 1) * size, lo:hi])
            grads.append(grad_refs[b][:, first + lo : first + hi])
            g, p = one(queries[b], ones, grads[b], lse_ref[h : h + 1, b * size : (b + 1) * size])
            scores_g.append(g)
            probs.append(p)
            grad_q[b].append(mm(key_t[lo:hi], g) * 0.125)
        grad_key = mm(jnp.concatenate([g[:own] for g in scores_g], axis=1), jnp.concatenate(queries, axis=0))
        grad_value = mm(jnp.concatenate([p[:own] for p in probs], axis=1), jnp.concatenate(grads, axis=0))
        if mem_queries:
            query, grad = mem_ref[:, lo:hi], grad_refs[blocks][:, lo:hi]
            g, p = one(query, ones[:mem], grad, lse_ref[h : h + 1, blocks * size : own])
            grad_q[blocks].append(mm(key_t[lo:hi], g) * 0.125)
            grad_key = grad_key + mm(g[:own], query)
            grad_value = grad_value + mm(p[:own], grad)
        grad_key = (grad_key * 0.125).astype(BF16)
        grad_value = grad_value.astype(BF16)
        for b in range(blocks):
            out_refs[b][:size, width + lo : width + hi] = grad_key[b * size : (b + 1) * size]
            out_refs[b][:size, 2 * width + lo : 2 * width + hi] = grad_value[b * size : (b + 1) * size]
        mem_out_ref[:, width + lo : width + hi] = grad_key[blocks * size :]
        mem_out_ref[:, 2 * width + lo : 2 * width + hi] = grad_value[blocks * size :]
    for b in range(blocks):
        out_refs[b][:size, :width] = jnp.concatenate(grad_q[b], axis=0).T.astype(BF16)
    if mem_queries:
        mem_out_ref[:, :width] = jnp.concatenate(grad_q[blocks], axis=0).T.astype(BF16)
    else:
        mem_out_ref[:, :width] = jnp.zeros((mem, width), BF16)


def norm_parts(hidden):
    center = hidden - jnp.mean(hidden, axis=-1, keepdims=True)
    inverse = lax.rsqrt(jnp.mean(center * center, axis=-1, keepdims=True) + EPS)
    return center * inverse, inverse


def norm_back(grad, gain, unit, inverse):
    scaled = grad * gain
    mean_scaled = jnp.mean(scaled, axis=-1, keepdims=True)
    mean_product = jnp.mean(scaled * unit, axis=-1, keepdims=True)
    return inverse * (scaled - mean_scaled - unit * mean_product)


def gelu_and_slope(pre):
    cdf = 0.5 * (1.0 + lax.erf(pre * (2.0**-0.5)))
    density = jnp.exp(-0.5 * pre * pre) * 0.3989422804014327
    return pre * cdf, cdf + pre * density


N_KEPT = 4


def rows_fwd_kernel(meta_ref, *refs, n_seg, n_pair, n_hidden):
    mix_refs, hid_refs = refs[:n_seg], refs[n_seg : n_seg + n_hidden]
    vec_ref, out_ref, exp_ref, red_ref = refs[n_seg + n_hidden : n_seg + n_hidden + 4]
    outs = refs[n_seg + n_hidden + 4 :]
    unit_a_ref, inv_ref, slope_ref, unit_f_ref = outs[:N_KEPT]
    result_refs, left_refs, acc_ref = outs[N_KEPT : N_KEPT + n_hidden], outs[N_KEPT + n_hidden : -1], outs[-1]
    wide = out_ref.shape[0]
    size = hid_refs[0].shape[0]

    def vec(i):
        return vec_ref[i : i + 1]

    def keep_left(x, at, first, blocks):
        left_factors(meta_ref, x, left_refs, at, first, blocks, n_seg, n_pair, size)

    each = wide // (n_seg * n_pair * 2)
    mixed = reorder(jnp.concatenate([r[...] for r in mix_refs], axis=1), seg_here(), n_seg)
    hidden = jnp.concatenate([r[...].astype(F32) for r in hid_refs], axis=0)
    unit, inverse = norm_parts(hidden + (mm(mixed, out_ref[...]) + vec(OUT_B)))
    unit_a_ref[...] = unit
    inv_ref[:, 0:1] = inverse
    normed = unit * vec(ATTN_G) + vec(ATTN_S)
    low = normed.astype(BF16)
    chunks = exp_ref.shape[1] // wide
    acc_ref[...] = normed + vec(RED_B)

    def chunk(q):
        cols = pl.ds(pl.multiple_of(q * wide, wide), wide)
        active, slope = gelu_and_slope(mm(low, exp_ref[:, cols]) + vec_ref[pl.ds(EXP_B + q, 1)])
        slope_ref[:, cols] = slope
        active = active.astype(BF16)
        acc_ref[...] += mm(active, red_ref[cols])
        keep_left(active, each, q * (n_seg // chunks), n_seg // chunks)

    in_loop(chunks, 2, chunk)
    unit, inverse = norm_parts(acc_ref[...])
    unit_f_ref[...] = unit
    inv_ref[:, 1:2] = inverse
    result = unit * vec(FIN_G) + vec(FIN_S)
    at = 0
    for r in result_refs:
        r[...] = result[at : at + r.shape[0]].astype(r.dtype)
        at += r.shape[0]
    keep_left(low, 0, 0, n_seg)
    keep_left(mixed, (chunks + 1) * each, 0, n_seg)


def left_factors(meta_ref, x, left_refs, at, first, blocks, n_seg, n_pair, size):
    seg, core, pair = seg_here(), core_here(), pair_here()
    rows = x.shape[1] // (blocks * n_pair * 2)
    keep_ref, send_ref = left_refs[:2]
    keep, send = core_halves(x[:size].astype(F32).T, core, n_pair, rows)
    for s in range(blocks):
        for z in range(n_pair):
            keep_ref[(first + s) ^ seg, z ^ pair, at : at + rows] = keep[s * n_pair + z]
            send_ref[(first + s) ^ seg, z ^ pair, at : at + rows] = send[s * n_pair + z]
    if left_refs[2:]:
        keep_ref, send_ref = left_refs[2:]
        mine = x[size:].astype(F32)
        if blocks > 1:
            assert blocks == n_seg
            mine = own_columns(mine, seg, n_seg)
        keep, send = core_halves(mine.T, core, n_pair, rows)

        @pl.when((seg == first) | (blocks > 1))
        def _():
            for z in range(n_pair):
                keep_ref[z ^ pair, at : at + rows] = keep[z]
                send_ref[z ^ pair, at : at + rows] = send[z]


def core_halves(x, core, pairs, rows):
    x = x.reshape(x.shape[0] // (2 * rows), 2, rows, x.shape[1])
    even, odd = x[:, 0], x[:, 1]
    return jnp.where(core == 0, even, odd).astype(BF16), jnp.where(core == 0, odd, even).astype(BF16)


def rows_back(seg, n_seg, grad, kept, vec_ref, out_ref, exp_ref, red_ref, outs, acc_ref, together):
    right_ref, hidden_ref, small_ref = outs
    wide = hidden_ref.shape[1]
    chunks = exp_ref.shape[1] // wide

    def vec(i):
        return vec_ref[i : i + 1]

    def total(x):
        return jnp.sum(x, axis=0, keepdims=True)

    unit = kept(3)
    grad_sum = norm_back(grad, vec(FIN_G), unit, kept(1)[:, 1:2])
    low = grad_sum.astype(BF16)
    right_ref[:, chunks * wide : (chunks + 1) * wide] = low
    small_ref[...] = jnp.zeros_like(small_ref)
    small_ref[FIN_G : FIN_G + 1] = total(grad * unit)
    small_ref[FIN_S : FIN_S + 1] = total(grad)
    small_ref[RED_B : RED_B + 1] = total(low.astype(F32))
    acc_ref[...] = grad_sum

    def chunk(q):
        cols = pl.ds(pl.multiple_of(q * wide, wide), wide)
        grad_pre = (mm(low, red_ref[cols], NT) * kept(2, cols)).astype(BF16)
        right_ref[:, cols] = grad_pre
        small_ref[pl.ds(EXP_B + q, 1)] = total(grad_pre.astype(F32))
        acc_ref[...] += mm(grad_pre, exp_ref[:, cols], NT)

    in_loop(chunks, together, chunk)
    acc = acc_ref[...]
    unit = kept(0)
    small_ref[ATTN_G : ATTN_G + 1] = total(acc * unit)
    small_ref[ATTN_S : ATTN_S + 1] = total(acc)
    grad_hidden = norm_back(acc, vec(ATTN_G), unit, kept(1)[:, 0:1])
    hidden_ref[...] = grad_hidden
    low = grad_hidden.astype(BF16)
    right_ref[:, (chunks + 1) * wide :] = low
    small_ref[OUT_B : OUT_B + 1] = total(low.astype(F32))
    return reorder(mm(low, out_ref[...], NT).astype(BF16), seg, n_seg)


def token_rows_back_kernel(meta_ref, grad_ref, *refs, slots, n_seg):
    kept_refs = [refs[t * N_KEPT : (t + 1) * N_KEPT] for t in range(slots)]
    refs = refs[slots * N_KEPT :]
    (vec_ref, out_ref, exp_ref, red_ref), outs, mix_refs, acc_ref = refs[:4], refs[4:7], refs[7:-1], refs[-1]
    size = grad_ref.shape[1]

    def kept(i, cols=slice(None)):
        return jnp.concatenate([kept_refs[t][i][:size, cols] for t in range(slots)], axis=0)

    grad = jnp.concatenate([grad_ref[t].astype(F32) for t in range(slots)], axis=0)
    mixed = rows_back(seg_here(), n_seg, grad, kept, vec_ref, out_ref, exp_ref, red_ref, outs, acc_ref, 2)
    width = mixed.shape[1] // n_seg
    for m in range(n_seg):
        for t in range(slots):
            mix_refs[m][:, t * width : (t + 1) * width] = mixed[t * size : (t + 1) * size, m * width : (m + 1) * width]


def memory_rows_back_kernel(meta_ref, *refs, n_seg, size):
    d_refs, refs = refs[:n_seg], refs[n_seg:]
    (wk_ref, wv_ref), kept_refs, refs = refs[:2], refs[2 : 2 + N_KEPT], refs[2 + N_KEPT :]
    (vec_ref, out_ref, exp_ref, red_ref), outs, (memory_ref, own_ref, acc_ref) = refs[:4], refs[4:7], refs[7:]
    seg = seg_here()
    width = d_refs[0].shape[1] // 2
    d_key = reorder(jnp.concatenate([r[:, :width] for r in d_refs], axis=1), seg, n_seg)
    d_value = reorder(jnp.concatenate([r[:, width:] for r in d_refs], axis=1), seg, n_seg)
    grad = 2.0 * (mm(d_key, wk_ref[...], NT) + mm(d_value, wv_ref[...], NT))
    memory_ref[...] = grad
    grad = jnp.where(meta_ref[FRESH] == 1, jnp.zeros_like(grad), grad)

    def kept(i, cols=slice(None)):
        return kept_refs[i][size:, cols]

    mixed = rows_back(seg, n_seg, grad, kept, vec_ref, out_ref, exp_ref, red_ref, outs, acc_ref, 1)
    own_ref[...] = mixed[:, : own_ref.shape[1]]


def tokens_grad_kernel(meta_ref, hidden_ref, wq_ref, wk_ref, wv_ref, *refs, slots, n_seg):
    d_refs, out_ref = refs[:-1], refs[-1]
    size = out_ref.shape[1]
    width = d_refs[0].shape[1] // 3
    seg = seg_here()
    for t in range(slots):
        grad = hidden_ref[t * size : (t + 1) * size]
        for i, w_ref in enumerate((wq_ref, wk_ref, wv_ref)):
            part = jnp.concatenate([r[t * size : (t + 1) * size, i * width : (i + 1) * width] for r in d_refs], 1)
            grad = grad + mm(reorder(part, seg, n_seg), w_ref[...], NT)
        out_ref[t] = grad.astype(BF16)


def row_parts(stream, chunks, each):
    if stream == 0:
        return [(0, each, q, q * each) for q in range(chunks)]
    return [(each, chunks * each, chunks, 0), ((chunks + 1) * each, each, chunks + 1, chunks * each)]


def rows_weights_kernel(meta_ref, *refs, stream, n_seg, n_pair, each):
    left_refs, (right_ref, other_ref), outs = refs[:-6], refs[-6:-4], refs[-4:]
    wide = outs[0].shape[3]
    half = n_pair // 2
    for lo, rows, q, row in row_parts(stream, right_ref.shape[1] // wide - 2, each):
        left = jnp.concatenate(
            [r[:, :, lo : lo + rows].reshape(n_seg * n_pair * rows, r.shape[3]) for r in left_refs], axis=1
        )
        right = jnp.concatenate([r[:, q * wide : (q + 1) * wide] for r in (right_ref, other_ref)], axis=0)
        full = mm(left, right).reshape(n_seg, n_pair, rows, wide).astype(BF16)
        for s in range(n_seg):
            low, high = s & 1, s >> 1
            outs[low][high, :, row : row + rows] = full[s, :half]
            outs[2 + high][low, :, row : row + rows] = full[s, half:]


def quarter_kernel(meta_ref, left_ref, left2_ref, right_ref, right2_ref, *refs, stream, each):
    half_refs, outs = (refs[:2], refs[2:4]), refs[4:]
    wide = outs[0].shape[2]
    pairs = left_ref.shape[0]
    half = pairs // 2
    for lo, rows, q, row in row_parts(stream, right_ref.shape[1] // wide - 2, each):

        def rows_of(r):
            return jnp.concatenate([r[z].astype(F32)[lo : lo + rows] for z in range(pairs)], axis=0)

        left = jnp.concatenate([rows_of(left_ref), rows_of(left2_ref)], axis=1).astype(BF16)
        right = jnp.concatenate([r[:, q * wide : (q + 1) * wide] for r in (right_ref, right2_ref)], axis=0)
        part = mm(left, right).reshape(pairs, rows, wide)
        for z in range(pairs):
            total = part[z]
            for r in half_refs[z // half]:
                total = total + r[z % half, row : row + rows].astype(F32)
            outs[z & 1][z >> 1, row : row + rows] = total.astype(BF16)


def heads_weights_kernel(meta_ref, small_ref, small_m_ref, hid_ref, memory_ref, w_ref, *refs, slots, n_seg):
    rows, refs = refs[: slots * n_seg], refs[slots * n_seg :]
    grads, (mem0_ref, mem1_ref, dm0_ref, dm1_ref, keep_ref, send_ref) = refs[:n_seg], refs[n_seg:]
    seg, core, pair, fresh1 = seg_here(), core_here(), pair_here(), meta_ref[FRESH]
    wide = rows[0].shape[1]
    width = wide // n_seg
    each = keep_ref.shape[2]
    col = lax.broadcasted_iota(jnp.int32, (1, 3 * width), 1)
    twice = jnp.where(col < width, 1.0, 2.0)
    dm0 = (dm0_ref[...].astype(F32) * twice).astype(BF16)
    dm1 = (dm1_ref[...].astype(F32) * twice).astype(BF16)
    full = mm(mem0_ref[...], dm0, TN) + mm(mem1_ref[...], dm1, TN)
    sums = jnp.sum(dm0.astype(F32), axis=0, keepdims=True) + jnp.sum(dm1.astype(F32), axis=0, keepdims=True)
    for m, g in enumerate(grads):
        x = jnp.concatenate([r[...] for r in rows[m::n_seg]], axis=0)
        full = full + mm(x, g[...], TN)
        sums = sums + jnp.sum(g[...].astype(F32), axis=0, keepdims=True)
    grad_mem = mm(dm0, w_ref[...], NT)
    whole = hid_ref[...] + jnp.where(fresh1 == 1, memory_ref[...], 0.0)
    grad_mem = grad_mem + jnp.where(seg == 0, whole, 0.0)

    def placed(v):
        return reorder(jnp.concatenate([v, jnp.zeros((1, wide - width), F32)], axis=1), seg, n_seg)

    n_pair = keep_ref.shape[0]
    chunks = 4
    head = EXP_B + chunks
    given = small_ref[...] + jnp.where(seg == 0, small_m_ref[...], 0.0)
    small = jnp.concatenate(
        [
            placed(sums[:, :width]),
            placed(sums[:, 2 * width :]),
            given[2:head],
            grad_mem,
            jnp.zeros((N_SMALL - head - grad_mem.shape[0], wide), F32),
        ],
        axis=0,
    ).T
    turned = small.reshape(wide // (chunks * each), chunks, each, N_SMALL)
    spread = [
        jnp.concatenate(
            [turned[:, k, :, EXP_B + q : EXP_B + q + 1].reshape(wide // chunks, 1) for k in range(chunks)], axis=1
        )
        for q in range(chunks)
    ]
    small = jnp.concatenate([small[:, :EXP_B], jnp.concatenate(spread, axis=0), small[:, head:]], axis=1)
    high = small.astype(BF16)
    rest = (small - high.astype(F32)).astype(BF16)
    full = jnp.concatenate([full, high.astype(F32), rest.astype(F32)], axis=1)
    keep, send = core_halves(full, core, n_pair, each)
    for s in range(n_seg):
        for z in range(n_pair):
            keep_ref[z ^ pair, s ^ seg] = keep[s * n_pair + z]
            send_ref[z ^ pair, s ^ seg] = send[s * n_pair + z]


def late_sum(*parts, at):
    total = sum(p.astype(F32) for p in parts)
    small = total[..., at : at + N_SMALL] + total[..., at + N_SMALL :]
    high = small.astype(BF16)
    rest = (small - high.astype(F32)).astype(BF16)
    return jnp.concatenate([total[..., :at].astype(BF16), high, rest], axis=-1)


def heads_final_kernel(meta_ref, *refs, n_seg, mem):
    ins, outs = refs[:n_seg], refs[n_seg:]
    seg = seg_here()
    width = outs[0].shape[1] // n_seg
    total = [r[...].astype(F32) for r in ins]
    for i in range(3):
        outs[i][...] = reorder(
            jnp.concatenate([total[m][:, i * width : (i + 1) * width] for m in range(n_seg)], axis=1), seg, n_seg
        )
    at = 3 * width
    small = sum(t[:, at : at + N_SMALL] + t[:, at + N_SMALL : at + 2 * N_SMALL] for t in total).T
    vec_refs, exp_ref, mem_ref = outs[3 : 3 + EXP_B], outs[3 + EXP_B], outs[4 + EXP_B]
    for i, r in enumerate(vec_refs):
        r[...] = small[i : i + 1]
    exp_ref[...] = jnp.concatenate([small[EXP_B + q : EXP_B + q + 1] for q in range(4)], axis=1)
    mem_ref[...] = small[EXP_B + 4 : EXP_B + 4 + mem]


def rows_final_kernel(meta_ref, first_ref, second_ref, *outs):
    total = first_ref[...].astype(F32) + second_ref[...].astype(F32)
    wide = total.shape[1]
    at = 0
    for r in outs:
        for q in range(r.shape[1] // wide):
            r[:, q * wide : (q + 1) * wide] = total[at : at + r.shape[0]]
            at += r.shape[0]


def shards(
    tokens,
    new_doc,
    valid_len,
    mem_init,
    query_proj,
    query_bias,
    key_proj,
    value_proj,
    value_bias,
    output_proj,
    output_bias,
    attn_gain,
    attn_shift,
    expand_proj,
    expand_bias,
    reduce_proj,
    reduce_bias,
    final_gain,
    final_shift,
    d_out,
):
    slots, size, wide = tokens.shape
    assert slots == 2
    n_seg, n_doc = lax.axis_size("seg"), lax.axis_size("doc")
    n_pair = n_doc // 2
    hidden_units = expand_proj.shape[1]
    chunks = hidden_units // wide
    assert chunks == 4
    mem = mem_init.shape[0]
    width = wide // n_seg
    heads = HEADS // n_seg
    others = range(1, n_seg)
    all_rows = n_seg * size

    rows0 = [tokens[0]] + [swap(tokens[0], "seg", m) for m in others]
    place = jnp.concatenate([new_doc, valid_len])
    w_own, b_own, vecs = call(
        functools.partial(prep_kernel, n_seg=n_seg, chunks=chunks),
        [shape_of(wide, 3 * width), shape_of(1, 3 * width, dtype=F32), shape_of(N_VEC, wide, dtype=F32)],
        (
            place,
            query_proj,
            key_proj,
            value_proj,
            query_bias,
            value_bias,
            output_bias,
            attn_gain,
            attn_shift,
            reduce_bias,
            final_gain,
            final_shift,
            expand_bias,
        ),
        4,
        far_in=range(4, 5 + EXP_B),
        scratch=[pltpu.VMEM((1, hidden_units), F32), pltpu.SemaphoreType.DMA((EXP_B + 1,))],
    )

    second, w_own, *rows0 = lax.optimization_barrier((tokens[1], w_own, *rows0))
    rows = [rows0, [second] + [swap(second, "seg", m) for m in others]]

    def project(t):
        (out,) = call(qkv_kernel, [shape_of(all_rows, 3 * width)], (place, w_own, b_own, *rows[t]), 3)
        return out

    def attend(t, qkv, written=()):
        mem_queries = not written
        got = call(
            functools.partial(attn_fwd_kernel, slot=t, blocks=n_seg, heads=heads, mem_queries=mem_queries),
            [shape_of(size + (mem if mem_queries else 0), width)] * n_seg
            + [shape_of(8, all_rows + 128, dtype=F32), shape_of(mem, 3 * width)]
            + [shape_of(mem, wide)] * len(written),
            (place, qkv, mem_init, w_own, b_own, *written),
            8,
        )
        return list(got[:n_seg]), *got[n_seg:]

    def attend_back(t, qkv, qkv_mem, lse, grads, more=()):
        got = call(
            functools.partial(attn_bwd_kernel, slot=t, blocks=n_seg, heads=heads, mem_queries=len(grads) > n_seg),
            [shape_of(size * (2 if more else 1), 3 * width)] * n_seg + [shape_of(mem, 3 * width)],
            (place, qkv, qkv_mem, lse, *grads, *more),
            8,
        )
        return list(got[:n_seg]), got[n_seg]

    def trade(blocks):
        return [blocks[0]] + [swap(blocks[m], "seg", m) for m in others]

    weights = (vecs, output_proj, expand_proj, reduce_proj)
    each = wide // (n_seg * n_doc)

    def rows_forward(mixed, hidden, result_shapes):
        n_rows = sum(h.shape[0] for h in hidden)
        left = [shape_of(n_seg, n_pair, (chunks + 2) * each, size)] * 2
        if len(hidden) > 1:
            left += [shape_of(n_pair, (chunks + 2) * each, mem)] * 2
        got = call(
            functools.partial(rows_fwd_kernel, n_seg=n_seg, n_pair=n_pair, n_hidden=len(hidden)),
            [
                shape_of(n_rows, wide, dtype=F32),
                shape_of(n_rows, 128, dtype=F32),
                shape_of(n_rows, hidden_units, dtype=F32),
                shape_of(n_rows, wide, dtype=F32),
                *result_shapes,
                *left,
            ],
            (place, *mixed, *hidden, *weights),
            8,
            scratch=[pltpu.VMEM((n_rows, wide), F32)],
        )
        return got[:N_KEPT], got[N_KEPT : N_KEPT + len(hidden)], got[N_KEPT + len(hidden) :]

    qkv0 = project(0)
    mixed0, lse0, qkv_mem0 = attend(0, qkv0)
    mixed0[0], *rows[1] = lax.optimization_barrier((mixed0[0], *rows[1]))
    qkv1 = project(1)
    mixed0 = trade(mixed0)
    qkv1, mixed0[0] = lax.optimization_barrier((qkv1, mixed0[0]))
    kept0, (layer0, written), (left0, left0_send, left_m, left_m_send) = rows_forward(
        mixed0, (tokens[0], mem_init), [shape_of(size, wide), shape_of(mem, wide, dtype=F32)]
    )
    mixed1, lse1, qkv_mem1, memory1 = attend(1, qkv1, (written,))
    left0_other, left_m_other = swap(left0_send, "doc", 1), swap(left_m_send, "doc", 1)
    mixed1[0], left0_other, left_m_other = lax.optimization_barrier((mixed1[0], left0_other, left_m_other))
    kept1, (layer1,), (left1, left1_send) = rows_forward(trade(mixed1), (tokens[1],), [shape_of(size, wide)])
    left1_other = swap(left1_send, "doc", 1)
    layer_out = jnp.stack([layer0, layer1])

    def back_shapes(n_rows):
        return [
            shape_of(n_rows, hidden_units + 2 * wide),
            shape_of(n_rows, wide, dtype=F32),
            shape_of(N_VEC, wide, dtype=F32),
        ]

    n_rows = slots * size
    got = call(
        functools.partial(token_rows_back_kernel, slots=slots, n_seg=n_seg),
        back_shapes(n_rows) + [shape_of(size, slots * width)] * n_seg,
        (place, d_out, *kept0, *kept1, *weights),
        10,
        scratch=[pltpu.VMEM((n_rows, wide), F32)],
    )
    right, hidden, small = got[:3]
    grads = trade(got[3:])
    right_other = swap(right, "doc", 1)
    right, left1_other = lax.optimization_barrier((right, left1_other))

    def plain_sum(*parts):
        return sum(p.astype(F32) for p in parts).astype(BF16)

    share = [chunks * each, (chunks + 1) * each]

    def row_weights(stream, right_other):
        return call(
            functools.partial(rows_weights_kernel, stream=stream, n_seg=n_seg, n_pair=n_pair, each=each),
            [shape_of(n_seg // 2, n_pair // 2, share[stream], wide)] * 4,
            (place, left0, left1, left0_other, left1_other, right, right_other),
            2,
        )

    def both_sums(keep_a, came_a, keep_b, came_b):
        return [plain_sum(k[i], c[i]) for k, c in ((keep_a, came_a), (keep_b, came_b)) for i in range(2)]

    keep_a, send_a, keep_b, send_b = row_weights(0, right_other)
    send_a, send_b, *grads = lax.optimization_barrier((send_a, send_b, *grads))
    came_a, came_b = swap(send_a, "seg", 1), swap(send_b, "seg", 2)
    d_qkv1, d_mem1 = attend_back(1, qkv1, qkv_mem1, lse1, grads)
    d_mem1_all = trade([d_mem1[:, width:]] * n_seg)

    right_other, d_mem1_all[0] = lax.optimization_barrier((right_other, d_mem1_all[0]))
    keep_c, send_c, keep_d, send_d = row_weights(1, right_other)
    send_c, send_d, came_a, came_b, *d_mem1_all = lax.optimization_barrier(
        (send_c, send_d, came_a, came_b, *d_mem1_all)
    )
    keep_a, send_a, keep_b, send_b = both_sums(keep_a, came_a, keep_b, came_b)
    send_a, send_b, d_mem1_all[0] = lax.optimization_barrier((send_a, send_b, d_mem1_all[0]))
    came_a, came_b = swap(send_a, "seg", 2), swap(send_b, "seg", 1)

    got = call(
        functools.partial(memory_rows_back_kernel, n_seg=n_seg, size=size),
        back_shapes(mem) + [shape_of(mem, wide, dtype=F32), shape_of(mem, width)],
        (place, *d_mem1_all, key_proj, value_proj, *kept0, *weights),
        6,
        scratch=[pltpu.VMEM((mem, wide), F32)],
    )
    right_m, hidden_m, small_m, memory1_grad, mixed_m = got
    right_m_other = swap(right_m, "doc", 1)
    def pair_sum(keep, came, add):
        bit = 2
        while keep.shape[0] > 1:
            bit *= 2
            if keep.shape[0] == 2:
                (keep, send) = [add(keep[i : i + 1], came[i : i + 1]) for i in range(2)]
            else:
                both = add(keep, came)
                keep, send = both[0::2], both[1::2]
            came = swap(send, "doc", bit)
        return [keep[0], came[0]]

    def quarter(stream, *halves):
        keep, send = call(
            functools.partial(quarter_kernel, stream=stream, each=each),
            [shape_of(n_pair // 2, share[stream], wide)] * 2,
            (place, left_m, left_m_other, right_m, right_m_other, *halves),
            1,
        )
        return keep, send

    right_m, came_a, came_b, send_c, send_d = lax.optimization_barrier((right_m, came_a, came_b, send_c, send_d))
    came_c, came_d = swap(send_c, "seg", 1), swap(send_d, "seg", 2)
    keep_x, send_x = quarter(0, keep_a, came_a, keep_b, came_b)
    send_x, mixed_m = lax.optimization_barrier((send_x, mixed_m))
    came_x = swap(send_x, "doc", 2)
    d_qkv, d_mem0 = attend_back(0, qkv0, qkv_mem0, lse0, [*grads, mixed_m], d_qkv1)

    came_x, d_mem0 = lax.optimization_barrier((came_x, d_mem0))
    parts_exp = pair_sum(keep_x, came_x, plain_sum)

    columns = 3 * width + 2 * N_SMALL
    keep, send = call(
        functools.partial(heads_weights_kernel, slots=slots, n_seg=n_seg),
        [shape_of(n_pair, n_seg, each, columns)] * 2,
        (
            place,
            small,
            small_m,
            hidden_m,
            memory1_grad,
            w_own,
            *rows[0],
            *rows[1],
            *d_qkv,
            mem_init,
            memory1,
            d_mem0,
            d_mem1,
        ),
        6,
    )

    def rows_final(parts, *shapes):
        return call(
            rows_final_kernel,
            [shape_of(*dims, dtype=F32) for dims in shapes],
            (place, *parts),
            1,
            far_out=range(len(shapes)),
        )

    add = functools.partial(late_sum, at=3 * width)
    came = swap(send, "doc", 1)
    came_c, came_d, keep = lax.optimization_barrier((came_c, came_d, keep))
    keep_c, send_c, keep_d, send_d = both_sums(keep_c, came_c, keep_d, came_d)
    came_c, came_d = swap(send_c, "seg", 2), swap(send_d, "seg", 1)
    _, came, parts_exp[1] = lax.optimization_barrier((send_c, came, parts_exp[1]))
    mine = add(keep, came)
    came_l = swap(mine[1::2], "doc", 2)
    keep_y, send_y = quarter(1, keep_c, came_c, keep_d, came_d)
    _, came_l, *d_qkv = lax.optimization_barrier((send_y, came_l, *d_qkv))
    late = pair_sum(mine[0::2], came_l, add)
    parts_rest = pair_sum(keep_y, swap(send_y, "doc", 2), plain_sum)
    (grad_exp,) = rows_final(parts_exp, (each, hidden_units))

    back = trade(d_qkv)
    (grad_tokens,) = call(
        functools.partial(tokens_grad_kernel, slots=slots, n_seg=n_seg),
        [shape_of(slots, size, wide)],
        (place, hidden, query_proj, key_proj, value_proj, *back),
        3,
        far_out=(0,),
    )

    late[1], grad_exp, layer_out = lax.optimization_barrier((late[1], grad_exp, layer_out))
    mine = add(*late)
    parts = trade([mine[m] for m in range(n_seg)])
    grad_tokens, *parts = lax.optimization_barrier((grad_tokens, *parts))
    got = call(
        functools.partial(heads_final_kernel, n_seg=n_seg, mem=mem),
        [shape_of(each, wide, dtype=F32)] * 3
        + [shape_of(1, each, dtype=F32)] * EXP_B
        + [shape_of(1, chunks * each, dtype=F32), shape_of(mem, each, dtype=F32)],
        (place, *parts),
        1,
        far_out=range(5 + EXP_B),
    )
    grad_red, grad_out = rows_final(parts_rest, (chunks * each, wide), (each, wide))
    grad_q, grad_k, grad_v = got[:3]
    flat = [v.reshape(-1) for v in got[3:-1]]

    return (
        layer_out,
        grad_tokens,
        got[-1],
        grad_q,
        flat[Q_B],
        grad_k,
        grad_v,
        flat[V_B],
        grad_out,
        flat[OUT_B],
        flat[ATTN_G],
        flat[ATTN_S],
        grad_exp,
        flat[EXP_B],
        grad_red,
        flat[RED_B],
        flat[FIN_G],
        flat[FIN_S],
    )


def solution(mesh):
    both = ("seg", "doc")
    data = P("doc", "seg", None)
    placed = (data, P("doc"), P("doc")) + (P(),) * 16 + (data,)
    vec, mat = P(both), P(both, None)
    return jax.shard_map(
        shards,
        mesh=mesh,
        in_specs=placed,
        out_specs=(
            data,
            data,
            P(None, both),
            mat,
            vec,
            mat,
            mat,
            vec,
            mat,
            vec,
            vec,
            vec,
            mat,
            vec,
            mat,
            vec,
            vec,
            vec,
        ),
        check_vma=False,
    )
```

```python
import functools

import jax
import jax.numpy as jnp
from jax import lax
from jax.experimental import pallas as pl
from jax.experimental.pallas import tpu as pltpu
from jax.sharding import PartitionSpec as P

HEADS = 12


EPS = 1e-12
NEG_FILL = -1e30
F32 = jnp.float32
BF16 = jnp.bfloat16
NN = (((1,), (0,)), ((), ()))
NT = (((1,), (1,)), ((), ()))
TN = (((0,), (0,)), ((), ()))

Q_B, V_B, OUT_B, ATTN_G, ATTN_S, RED_B, FIN_G, FIN_S, EXP_B = range(9)
N_VEC = 16
N_SMALL = 32


def mm(left, right, dims=NN):
    return lax.dot_general(left, right, dims, preferred_element_type=F32)


def swap(block, axis, mask):
    return lax.ppermute(block, axis, [(i, i ^ mask) for i in range(lax.axis_size(axis))])


FRESH, VALID = 0, 1


def flags_kernel(meta_ref, out_ref):
    new_ref, valid_ref = meta_ref
    out_ref[...] = jnp.zeros_like(out_ref)
    out_ref[FRESH : FRESH + 1] = jnp.full((1, out_ref.shape[1]), new_ref[1], jnp.int32)
    for t in range(2):
        out_ref[VALID + t : VALID + t + 1] = jnp.full((1, out_ref.shape[1]), valid_ref[t], jnp.int32)


def flag(flags_ref, i):
    return flags_ref[i : i + 1, 0:1]


def seg_here():
    return lax.axis_index("seg")


def core_here():
    return lax.axis_index("doc") & 1


def pair_here():
    return lax.axis_index("doc") >> 1


def shape_of(*dims, dtype=BF16):
    return jax.ShapeDtypeStruct(dims, dtype)


def call(kernel, out_shape, args, micros, far_in=(), far_out=(), scratch=()):
    vmem, far = pl.BlockSpec(memory_space=pltpu.VMEM), pl.BlockSpec(memory_space=pltpu.HBM)
    integers, *rest = args
    near = [
        pltpu.with_memory_space_constraint(x, pltpu.HBM if i in far_in else pltpu.VMEM) for i, x in enumerate(rest, 1)
    ]

    def body(*refs):
        kernel(refs[: len(integers)], *refs[len(integers) :])

    return pl.pallas_call(
        body,
        out_shape=[o if i in far_out else pltpu.VMEM(o.shape, o.dtype) for i, o in enumerate(out_shape)],
        in_specs=[pl.BlockSpec(memory_space=pltpu.SMEM)] * len(integers)
        + [far if i in far_in else vmem for i in range(1, len(args))],
        out_specs=[vmem] * len(out_shape),
        scratch_shapes=scratch,
        compiler_params=pltpu.CompilerParams(vmem_limit_bytes=8 << 20),
        cost_estimate=pl.CostEstimate(flops=0, transcendentals=0, bytes_accessed=int(micros * 3e6)),
    )(*integers, *near)


def reorder(x, seg, n_seg):
    width = x.shape[1] // n_seg
    bit = 1
    while bit < n_seg:
        moved = jnp.concatenate([x[:, (b ^ bit) * width : ((b ^ bit) + 1) * width] for b in range(n_seg)], axis=1)
        x = jnp.where((seg & bit) != 0, moved, x)
        bit *= 2
    return x


def in_loop(count, together, step):
    def some(j, carry):
        for k in range(together):
            step(j * together + k)
        return carry

    lax.fori_loop(0, count // together, some, 0)


def own_columns(x, seg, n_seg):
    width = x.shape[1] // n_seg
    out = x[:, :width]
    for b in range(1, n_seg):
        out = jnp.where(seg == b, x[:, b * width : (b + 1) * width], out)
    return out


def prep_kernel(meta_ref, wq_ref, wk_ref, wv_ref, *refs, n_seg, chunks):
    vec_refs, (w_ref, b_ref, out_ref, line_ref, near_ref, sems) = refs[: EXP_B + 1], refs[EXP_B + 1 :]
    weights = [
        pltpu.make_async_copy(r, near_ref.at[i], sems.at[EXP_B + 1 + i]) for i, r in enumerate((wq_ref, wk_ref, wv_ref))
    ]
    for c in weights:
        c.start()
    copies = [pltpu.make_async_copy(r, out_ref.at[i], sems.at[i]) for i, r in enumerate(vec_refs[:EXP_B])]
    copies.append(pltpu.make_async_copy(vec_refs[EXP_B], line_ref.at[0], sems.at[EXP_B]))
    for c in copies:
        c.start()
    seg = seg_here()
    rows = w_ref.shape[0] // 8
    for c in weights:
        c.wait()

    def some_rows(i):
        these = pl.ds(pl.multiple_of(i * rows, rows), rows)
        w_ref[these] = jnp.concatenate([own_columns(near_ref[k, these], seg, n_seg) for k in range(3)], axis=1)

    in_loop(8, 1, some_rows)
    for c in copies:
        c.wait()
    wide = out_ref.shape[1]
    for q in range(chunks):
        out_ref[EXP_B + q : EXP_B + q + 1] = line_ref[:, q * wide : (q + 1) * wide]
    q_b = own_columns(out_ref[Q_B : Q_B + 1], seg, n_seg)
    v_b = own_columns(out_ref[V_B : V_B + 1], seg, n_seg)
    b_ref[...] = jnp.concatenate([q_b, jnp.zeros_like(q_b), v_b], axis=1)


def qkv_kernel(meta_ref, w_ref, b_ref, *refs):
    rows, out_ref = refs[:-1], refs[-1]
    size = rows[0].shape[0]
    for b, r in enumerate(rows):
        out_ref[b * size : (b + 1) * size, :] = (mm(r[...], w_ref[...]) + b_ref[...]).astype(BF16)


def mask_block(meta_ref, slot, blocks, size, mem, width):
    total = blocks * size + 2 * mem
    row = lax.broadcasted_iota(jnp.int32, (total, width), 0)
    col = lax.broadcasted_iota(jnp.int32, (total, width), 1)
    place = row
    for b in range(blocks):
        inside = (row >= b * size) & (row < (b + 1) * size)
        place = jnp.where(inside, ((seg_here() ^ b) - b) * size + row, place)
    out = (place >= flag(meta_ref, VALID + slot)) & (row < blocks * size) & (col == 0)
    return jnp.where(out, NEG_FILL, 0.0).astype(BF16)


def ones_block(rows, width):
    col = lax.broadcasted_iota(jnp.int32, (rows, width), 1)
    return jnp.where(col == 0, 1.0, 0.0).astype(BF16)


def with_memory(rows, memory):
    return jnp.concatenate([rows, memory, memory], axis=0)


SCALE = 0.125 * 1.4426950408889634


def attn_fwd_kernel(_, meta_ref, qkv_ref, mem_ref, w_ref, b_ref, *outs, slot, blocks, heads, mem_queries):
    if mem_queries:
        memory = mem_ref[...]
    else:
        written_ref, outs = outs[0], outs[1:]
        memory = jnp.where(flag(meta_ref, FRESH) == 1, mem_ref[...], written_ref[...].astype(BF16))
        outs[-1][...] = memory
    mix_refs, lse_ref, mem_out_ref = outs[:blocks], outs[blocks], outs[blocks + 1]
    size = qkv_ref.shape[0] // blocks
    mem = mem_ref.shape[0]
    width = qkv_ref.shape[1] // 3
    head_dim = width // heads
    mem_out_ref[...] = (mm(memory, w_ref[...]) + b_ref[...]).astype(BF16)
    mask = mask_block(meta_ref, slot, blocks, size, mem, head_dim)
    ones = ones_block(size, head_dim)
    value_t = with_memory(qkv_ref[:, 2 * width :], mem_out_ref[:, 2 * width :]).T
    keys = []
    for h in range(heads):
        cols = slice(width + h * head_dim, width + (h + 1) * head_dim)
        keys.append(jnp.concatenate([with_memory(qkv_ref[:, cols], mem_out_ref[:, cols]), mask], axis=1))

    def mixed_of(queries, ones, first):
        out = []
        for h in range(heads):
            lo, hi = h * head_dim, (h + 1) * head_dim
            scores = mm(keys[h], jnp.concatenate([queries[:, lo:hi], ones], axis=1), NT)
            highest = jnp.max(scores, axis=0, keepdims=True)
            weights = jnp.exp2((scores - highest) * SCALE)
            total = jnp.sum(weights, axis=0, keepdims=True)
            out.append(mm(value_t[lo:hi], weights.astype(BF16)) * (1.0 / total))
            lse_ref[h : h + 1, first : first + queries.shape[0]] = highest * SCALE + jnp.log(total) * 1.4426950408889634
        return jnp.concatenate(out, axis=0).T.astype(BF16)

    def put(b, row, rows):
        half = mix_refs[b].shape[0]
        cut = max(0, min(rows.shape[0], half - row))
        if cut:
            mix_refs[b][row : row + cut, :width] = rows[:cut]
        if cut < rows.shape[0]:
            mix_refs[b][row + cut - half : row + rows.shape[0] - half, width:] = rows[cut:]

    for b in range(blocks):
        put(b, 0, mixed_of(qkv_ref[b * size : (b + 1) * size, :width], ones, b * size))
    if mem_queries:
        mixed = mixed_of(mem_out_ref[:, :width], ones[:mem], blocks * size)
        for b in range(blocks):
            put(b, size, mixed)


def attn_bwd_kernel(_, meta_ref, qkv_ref, mem_ref, lse_ref, *refs, slot, blocks, heads, mem_queries):
    n_grad = blocks + (1 if mem_queries else 0)
    grad_refs, refs = refs[:n_grad], refs[n_grad:]
    more_refs, out_refs, mem_out_ref = refs[: -blocks - 1], refs[-blocks - 1 : -1], refs[-1]
    for more_ref, out_ref in zip(more_refs, out_refs):
        out_ref[out_ref.shape[0] - more_ref.shape[0] :, :] = more_ref[...]
    size = qkv_ref.shape[0] // blocks
    mem = mem_ref.shape[0]
    width = qkv_ref.shape[1] // 3
    first = slot * width
    head_dim = width // heads
    own = blocks * size + mem
    mask = mask_block(meta_ref, slot, blocks, size, mem, head_dim)
    ones = ones_block(size, head_dim)
    key_t = with_memory(qkv_ref[:, width : 2 * width], mem_ref[:, width : 2 * width]).T
    grad_q = [[] for _ in range(n_grad)]
    for h in range(heads):
        lo, hi = h * head_dim, (h + 1) * head_dim
        key = with_memory(qkv_ref[:, width + lo : width + hi], mem_ref[:, width + lo : width + hi])
        key = jnp.concatenate([key, mask], axis=1)
        value = with_memory(qkv_ref[:, 2 * width + lo : 2 * width + hi], mem_ref[:, 2 * width + lo : 2 * width + hi])

        def one(query, ones, grad, lse):
            scores = mm(key, jnp.concatenate([query, ones], axis=1), NT)
            probs = jnp.exp2(scores * SCALE - lse)
            grad_probs = mm(value, grad, NT)
            inner = jnp.sum(grad_probs * probs, axis=0, keepdims=True)
            return (probs * (grad_probs - inner)).astype(BF16), probs.astype(BF16)

        queries, grads, scores_g, probs = [], [], [], []
        for b in range(blocks):
            queries.append(qkv_ref[b * size : (b + 1) * size, lo:hi])
            grads.append(grad_refs[b][:, first + lo : first + hi])
            g, p = one(queries[b], ones, grads[b], lse_ref[h : h + 1, b * size : (b + 1) * size])
            scores_g.append(g)
            probs.append(p)
            grad_q[b].append(mm(key_t[lo:hi], g) * 0.125)
        grad_key = mm(jnp.concatenate([g[:own] for g in scores_g], axis=1), jnp.concatenate(queries, axis=0))
        grad_value = mm(jnp.concatenate([p[:own] for p in probs], axis=1), jnp.concatenate(grads, axis=0))
        if mem_queries:
            query, grad = mem_ref[:, lo:hi], grad_refs[blocks][:, lo:hi]
            g, p = one(query, ones[:mem], grad, lse_ref[h : h + 1, blocks * size : own])
            grad_q[blocks].append(mm(key_t[lo:hi], g) * 0.125)
            grad_key = grad_key + mm(g[:own], query)
            grad_value = grad_value + mm(p[:own], grad)
        grad_key = (grad_key * 0.125).astype(BF16)
        grad_value = grad_value.astype(BF16)
        for b in range(blocks):
            out_refs[b][:size, width + lo : width + hi] = grad_key[b * size : (b + 1) * size]
            out_refs[b][:size, 2 * width + lo : 2 * width + hi] = grad_value[b * size : (b + 1) * size]
        mem_out_ref[:, width + lo : width + hi] = grad_key[blocks * size :]
        mem_out_ref[:, 2 * width + lo : 2 * width + hi] = grad_value[blocks * size :]
    for b in range(blocks):
        out_refs[b][:size, :width] = jnp.concatenate(grad_q[b], axis=0).T.astype(BF16)
    if mem_queries:
        mem_out_ref[:, :width] = jnp.concatenate(grad_q[blocks], axis=0).T.astype(BF16)
    else:
        mem_out_ref[:, :width] = jnp.zeros((mem, width), BF16)


def norm_parts(hidden):
    center = hidden - jnp.mean(hidden, axis=-1, keepdims=True)
    inverse = lax.rsqrt(jnp.mean(center * center, axis=-1, keepdims=True) + EPS)
    return center * inverse, inverse


def norm_back(grad, gain, unit, inverse):
    scaled = grad * gain
    mean_scaled = jnp.mean(scaled, axis=-1, keepdims=True)
    mean_product = jnp.mean(scaled * unit, axis=-1, keepdims=True)
    return inverse * (scaled - mean_scaled - unit * mean_product)


def gelu_and_slope(pre):
    cdf = 0.5 * (1.0 + lax.erf(pre * (2.0**-0.5)))
    density = jnp.exp(-0.5 * pre * pre) * 0.3989422804014327
    return pre * cdf, cdf + pre * density


N_KEPT = 4


def rows_fwd_kernel(meta_ref, *refs, n_seg, n_pair, n_hidden, together):
    mix_refs, hid_refs = refs[:n_seg], refs[n_seg : n_seg + n_hidden]
    vec_ref, out_ref, exp_ref, red_ref = refs[n_seg + n_hidden : n_seg + n_hidden + 4]
    outs = refs[n_seg + n_hidden + 4 :]
    unit_a_ref, inv_ref, slope_ref, unit_f_ref = outs[:N_KEPT]
    result_refs, left_refs, acc_ref = outs[N_KEPT : N_KEPT + n_hidden], outs[N_KEPT + n_hidden : -1], outs[-1]
    wide = out_ref.shape[0]
    size = hid_refs[0].shape[0]

    def vec(i):
        return vec_ref[i : i + 1]

    def keep_left(x, at, first, blocks):
        left_factors(meta_ref, x, left_refs, at, first, blocks, n_seg, n_pair, size)

    each = wide // (n_seg * n_pair * 2)
    width = mix_refs[0].shape[1] // 2
    halves = [
        jnp.concatenate([r[:, i * width : (i + 1) * width] for r in mix_refs], axis=1).astype(F32) for i in range(2)
    ]
    mixed = reorder(jnp.concatenate(halves, axis=0).astype(BF16), seg_here(), n_seg)
    hidden = jnp.concatenate([r[...].astype(F32) for r in hid_refs], axis=0)
    unit, inverse = norm_parts(hidden + (mm(mixed, out_ref[...]) + vec(OUT_B)))
    unit_a_ref[...] = unit
    inv_ref[:, 0:1] = inverse
    normed = unit * vec(ATTN_G) + vec(ATTN_S)
    low = normed.astype(BF16)
    chunks = exp_ref.shape[1] // wide
    acc_ref[...] = normed + vec(RED_B)

    def chunk(q):
        cols = pl.ds(pl.multiple_of(q * wide, wide), wide)
        active, slope = gelu_and_slope(mm(low, exp_ref[:, cols]) + vec_ref[pl.ds(EXP_B + q, 1)])
        slope_ref[:, cols] = slope
        active = active.astype(BF16)
        acc_ref[...] += mm(active, red_ref[cols])
        keep_left(active, each, q * (n_seg // chunks), n_seg // chunks)

    in_loop(chunks, together, chunk)
    unit, inverse = norm_parts(acc_ref[...])
    unit_f_ref[...] = unit
    inv_ref[:, 1:2] = inverse
    result = unit * vec(FIN_G) + vec(FIN_S)
    at = 0
    for r in result_refs:
        r[...] = result[at : at + r.shape[0]].astype(r.dtype)
        at += r.shape[0]
    keep_left(low, 0, 0, n_seg)
    keep_left(mixed, (chunks + 1) * each, 0, n_seg)


def left_factors(meta_ref, x, left_refs, at, first, blocks, n_seg, n_pair, size):
    seg, core, pair = seg_here(), core_here(), pair_here()
    rows = x.shape[1] // (blocks * n_pair * 2)
    keep_ref, send_ref = left_refs[:2]
    keep, send = core_halves(x[:size].astype(F32).T, core, n_pair, rows)
    for s in range(blocks):
        for z in range(n_pair):
            keep_ref[(first + s) ^ seg, z ^ pair, at : at + rows] = keep[s * n_pair + z]
            send_ref[(first + s) ^ seg, z ^ pair, at : at + rows] = send[s * n_pair + z]
    if left_refs[2:]:
        keep_ref, send_ref = left_refs[2:]
        mine = x[size:].astype(F32)
        if blocks > 1:
            assert blocks == n_seg
            mine = own_columns(mine, seg, n_seg)
        keep, send = core_halves(mine.T, core, n_pair, rows)

        @pl.when((seg == first) | (blocks > 1))
        def _():
            for z in range(n_pair):
                keep_ref[z ^ pair, at : at + rows] = keep[z]
                send_ref[z ^ pair, at : at + rows] = send[z]


def core_halves(x, core, pairs, rows):
    x = x.reshape(x.shape[0] // (2 * rows), 2, rows, x.shape[1])
    even, odd = x[:, 0], x[:, 1]
    return jnp.where(core == 0, even, odd).astype(BF16), jnp.where(core == 0, odd, even).astype(BF16)


def rows_back(seg, n_seg, grad, kept, vec_ref, out_ref, exp_ref, red_ref, outs, acc_ref, together):
    right_ref, hidden_ref, small_ref = outs
    wide = hidden_ref.shape[1]
    chunks = exp_ref.shape[1] // wide

    def vec(i):
        return vec_ref[i : i + 1]

    def total(x):
        return jnp.sum(x, axis=0, keepdims=True)

    unit = kept(3)
    grad_sum = norm_back(grad, vec(FIN_G), unit, kept(1)[:, 1:2])
    low = grad_sum.astype(BF16)
    right_ref[:, chunks * wide : (chunks + 1) * wide] = low
    small_ref[...] = jnp.zeros_like(small_ref)
    small_ref[FIN_G : FIN_G + 1] = total(grad * unit)
    small_ref[FIN_S : FIN_S + 1] = total(grad)
    small_ref[RED_B : RED_B + 1] = total(low.astype(F32))
    acc_ref[...] = grad_sum

    def chunk(q):
        cols = pl.ds(pl.multiple_of(q * wide, wide), wide)
        grad_pre = (mm(low, red_ref[cols], NT) * kept(2, cols)).astype(BF16)
        right_ref[:, cols] = grad_pre
        small_ref[pl.ds(EXP_B + q, 1)] = total(grad_pre.astype(F32))
        acc_ref[...] += mm(grad_pre, exp_ref[:, cols], NT)

    in_loop(chunks, together, chunk)
    acc = acc_ref[...]
    unit = kept(0)
    small_ref[ATTN_G : ATTN_G + 1] = total(acc * unit)
    small_ref[ATTN_S : ATTN_S + 1] = total(acc)
    grad_hidden = norm_back(acc, vec(ATTN_G), unit, kept(1)[:, 0:1])
    hidden_ref[...] = grad_hidden
    low = grad_hidden.astype(BF16)
    right_ref[:, (chunks + 1) * wide :] = low
    small_ref[OUT_B : OUT_B + 1] = total(low.astype(F32))
    return reorder(mm(low, out_ref[...], NT).astype(BF16), seg, n_seg)


def token_rows_back_kernel(meta_ref, grad_ref, *refs, slots, n_seg):
    kept_refs = [refs[t * N_KEPT : (t + 1) * N_KEPT] for t in range(slots)]
    refs = refs[slots * N_KEPT :]
    (vec_ref, out_ref, exp_ref, red_ref), outs, mix_refs, acc_ref = refs[:4], refs[4:7], refs[7:-1], refs[-1]
    size = grad_ref.shape[1]

    def kept(i, cols=slice(None)):
        return jnp.concatenate([kept_refs[t][i][:size, cols] for t in range(slots)], axis=0)

    grad = jnp.concatenate([grad_ref[t].astype(F32) for t in range(slots)], axis=0)
    mixed = rows_back(seg_here(), n_seg, grad, kept, vec_ref, out_ref, exp_ref, red_ref, outs, acc_ref, 4)
    width = mixed.shape[1] // n_seg
    for m in range(n_seg):
        for t in range(slots):
            mix_refs[m][:, t * width : (t + 1) * width] = mixed[t * size : (t + 1) * size, m * width : (m + 1) * width]


def memory_rows_back_kernel(_, meta_ref, *refs, n_seg, size):
    d_refs, refs = refs[:n_seg], refs[n_seg:]
    (wk_ref, wv_ref), kept_refs, refs = refs[:2], refs[2 : 2 + N_KEPT], refs[2 + N_KEPT :]
    (vec_ref, out_ref, exp_ref, red_ref), outs, (memory_ref, own_ref, acc_ref) = refs[:4], refs[4:7], refs[7:]
    seg = seg_here()
    width = d_refs[0].shape[1] // 2
    d_key = reorder(jnp.concatenate([r[:, :width] for r in d_refs], axis=1), seg, n_seg)
    d_value = reorder(jnp.concatenate([r[:, width:] for r in d_refs], axis=1), seg, n_seg)
    grad = 2.0 * (mm(d_key, wk_ref[...], NT) + mm(d_value, wv_ref[...], NT))
    memory_ref[...] = grad
    grad = jnp.where(flag(meta_ref, FRESH) == 1, jnp.zeros_like(grad), grad)

    def kept(i, cols=slice(None)):
        return kept_refs[i][size:, cols]

    mixed = rows_back(seg, n_seg, grad, kept, vec_ref, out_ref, exp_ref, red_ref, outs, acc_ref, 1)
    own_ref[...] = mixed[:, : own_ref.shape[1]]


def tokens_grad_kernel(meta_ref, hidden_ref, wq_ref, wk_ref, wv_ref, *refs, slots, n_seg):
    d_refs, out_ref = refs[:-1], refs[-1]
    size = out_ref.shape[1]
    width = d_refs[0].shape[1] // 3
    seg = seg_here()

    def slot(t):
        these = pl.ds(pl.multiple_of(t * size, size), size)
        grad = hidden_ref[these]
        for i, w_ref in enumerate((wq_ref, wk_ref, wv_ref)):
            part = jnp.concatenate([r[these, i * width : (i + 1) * width] for r in d_refs], 1)
            grad = grad + mm(reorder(part, seg, n_seg), w_ref[...], NT)
        out_ref[t] = grad.astype(BF16)

    in_loop(slots, 1, slot)


def row_parts(stream, chunks, each):
    if stream == 1:
        return [(0, each, q, q * each) for q in range(chunks)]
    return [(each, chunks * each, chunks, 0), ((chunks + 1) * each, each, chunks + 1, chunks * each)]


def rows_weights_kernel(meta_ref, *refs, stream, n_seg, n_pair, each):
    left_refs, (right_ref, other_ref), outs = refs[:-6], refs[-6:-4], refs[-4:]
    wide = outs[0].shape[3]
    half = n_pair // 2
    for lo, rows, q, row in row_parts(stream, right_ref.shape[1] // wide - 2, each):
        left = jnp.concatenate(
            [r[:, :, lo : lo + rows].reshape(n_seg * n_pair * rows, r.shape[3]) for r in left_refs], axis=1
        )
        right = jnp.concatenate([r[:, q * wide : (q + 1) * wide] for r in (right_ref, other_ref)], axis=0)
        full = mm(left, right).reshape(n_seg, n_pair, rows, wide).astype(BF16)
        for s in range(n_seg):
            low, high = s & 1, s >> 1
            outs[low][high, :, row : row + rows] = full[s, :half]
            outs[2 + high][low, :, row : row + rows] = full[s, half:]


def quarter_kernel(meta_ref, left_ref, left2_ref, right_ref, right2_ref, *refs, stream, each):
    half_refs, outs = (refs[:2], refs[2:4]), refs[4:]
    wide = outs[0].shape[2]
    pairs = left_ref.shape[0]
    half = pairs // 2
    for lo, rows, q, row in row_parts(stream, right_ref.shape[1] // wide - 2, each):

        def rows_of(r):
            return jnp.concatenate([r[z].astype(F32)[lo : lo + rows] for z in range(pairs)], axis=0)

        left = jnp.concatenate([rows_of(left_ref), rows_of(left2_ref)], axis=1).astype(BF16)
        right = jnp.concatenate([r[:, q * wide : (q + 1) * wide] for r in (right_ref, right2_ref)], axis=0)
        part = mm(left, right).reshape(pairs, rows, wide)
        for z in range(pairs):
            total = part[z]
            for r in half_refs[z // half]:
                total = total + r[z % half, row : row + rows].astype(F32)
            outs[z & 1][z >> 1, row : row + rows] = total.astype(BF16)


def heads_weights_kernel(_, meta_ref, small_ref, small_m_ref, hid_ref, memory_ref, w_ref, *refs, slots, n_seg):
    rows, refs = refs[: slots * n_seg], refs[slots * n_seg :]
    grads, (mem0_ref, mem1_ref, dm0_ref, dm1_ref, keep_ref, send_ref) = refs[:n_seg], refs[n_seg:]
    seg, core, pair, fresh1 = seg_here(), core_here(), pair_here(), flag(meta_ref, FRESH)
    wide = rows[0].shape[1]
    width = wide // n_seg
    each = keep_ref.shape[2]
    col = lax.broadcasted_iota(jnp.int32, (1, 3 * width), 1)
    twice = jnp.where(col < width, 1.0, 2.0)
    dm0 = (dm0_ref[...].astype(F32) * twice).astype(BF16)
    dm1 = (dm1_ref[...].astype(F32) * twice).astype(BF16)
    full = mm(mem0_ref[...], dm0, TN) + mm(mem1_ref[...], dm1, TN)
    sums = jnp.sum(dm0.astype(F32), axis=0, keepdims=True) + jnp.sum(dm1.astype(F32), axis=0, keepdims=True)
    for m, g in enumerate(grads):
        x = jnp.concatenate([r[...] for r in rows[m::n_seg]], axis=0)
        full = full + mm(x, g[...], TN)
        sums = sums + jnp.sum(g[...].astype(F32), axis=0, keepdims=True)
    grad_mem = mm(dm0, w_ref[...], NT)
    whole = hid_ref[...] + jnp.where(fresh1 == 1, memory_ref[...], 0.0)
    grad_mem = grad_mem + jnp.where(seg == 0, whole, 0.0)

    def placed(v):
        return reorder(jnp.concatenate([v, jnp.zeros((1, wide - width), F32)], axis=1), seg, n_seg)

    n_pair = keep_ref.shape[0]
    chunks = 4
    head = EXP_B + chunks
    given = small_ref[...] + jnp.where(seg == 0, small_m_ref[...], 0.0)
    small = jnp.concatenate(
        [
            placed(sums[:, :width]),
            placed(sums[:, 2 * width :]),
            given[2:head],
            grad_mem,
            jnp.zeros((N_SMALL - head - grad_mem.shape[0], wide), F32),
        ],
        axis=0,
    ).T
    turned = small.reshape(wide // (chunks * each), chunks, each, N_SMALL)
    spread = [
        jnp.concatenate(
            [turned[:, k, :, EXP_B + q : EXP_B + q + 1].reshape(wide // chunks, 1) for k in range(chunks)], axis=1
        )
        for q in range(chunks)
    ]
    small = jnp.concatenate([small[:, :EXP_B], jnp.concatenate(spread, axis=0), small[:, head:]], axis=1)
    high = small.astype(BF16)
    rest = (small - high.astype(F32)).astype(BF16)
    full = jnp.concatenate([full, high.astype(F32), rest.astype(F32)], axis=1)
    keep, send = core_halves(full, core, n_pair, each)
    for s in range(n_seg):
        for z in range(n_pair):
            keep_ref[z ^ pair, s ^ seg] = keep[s * n_pair + z]
            send_ref[z ^ pair, s ^ seg] = send[s * n_pair + z]


def late_sum(*parts, at):
    total = sum(p.astype(F32) for p in parts)
    small = total[..., at : at + N_SMALL] + total[..., at + N_SMALL :]
    high = small.astype(BF16)
    rest = (small - high.astype(F32)).astype(BF16)
    return jnp.concatenate([total[..., :at].astype(BF16), high, rest], axis=-1)


def heads_final_kernel(meta_ref, *refs, n_seg, mem):
    ins, outs = refs[:n_seg], refs[n_seg:]
    seg = seg_here()
    width = outs[0].shape[1] // n_seg
    total = [r[...].astype(F32) for r in ins]
    for i in range(3):
        outs[i][...] = reorder(
            jnp.concatenate([total[m][:, i * width : (i + 1) * width] for m in range(n_seg)], axis=1), seg, n_seg
        )
    at = 3 * width
    small = sum(t[:, at : at + N_SMALL] + t[:, at + N_SMALL : at + 2 * N_SMALL] for t in total).T
    vec_refs, exp_ref, mem_ref = outs[3 : 3 + EXP_B], outs[3 + EXP_B], outs[4 + EXP_B]
    for i, r in enumerate(vec_refs):
        r[...] = small[i : i + 1]
    exp_ref[...] = jnp.concatenate([small[EXP_B + q : EXP_B + q + 1] for q in range(4)], axis=1)
    mem_ref[...] = small[EXP_B + 4 : EXP_B + 4 + mem]


def rows_final_kernel(meta_ref, first_ref, second_ref, *outs):
    total = first_ref[...].astype(F32) + second_ref[...].astype(F32)
    wide = total.shape[1]
    at = 0
    for r in outs:
        for q in range(r.shape[1] // wide):
            r[:, q * wide : (q + 1) * wide] = total[at : at + r.shape[0]]
            at += r.shape[0]


def shards(
    tokens,
    new_doc,
    valid_len,
    mem_init,
    query_proj,
    query_bias,
    key_proj,
    value_proj,
    value_bias,
    output_proj,
    output_bias,
    attn_gain,
    attn_shift,
    expand_proj,
    expand_bias,
    reduce_proj,
    reduce_bias,
    final_gain,
    final_shift,
    d_out,
):
    slots, size, wide = tokens.shape
    assert slots == 2
    n_seg, n_doc = lax.axis_size("seg"), lax.axis_size("doc")
    n_pair = n_doc // 2
    hidden_units = expand_proj.shape[1]
    chunks = hidden_units // wide
    assert chunks == 4
    mem = mem_init.shape[0]
    width = wide // n_seg
    heads = HEADS // n_seg
    others = range(1, n_seg)
    all_rows = n_seg * size

    rows0 = [tokens[0]] + [swap(tokens[0], "seg", m) for m in others]
    (flags,) = call(flags_kernel, [shape_of(8, 128, dtype=jnp.int32)], ((new_doc, valid_len),), 1)
    w_own, b_own, vecs = call(
        functools.partial(prep_kernel, n_seg=n_seg, chunks=chunks),
        [shape_of(wide, 3 * width), shape_of(1, 3 * width, dtype=F32), shape_of(N_VEC, wide, dtype=F32)],
        (
            (),
            query_proj,
            key_proj,
            value_proj,
            query_bias,
            value_bias,
            output_bias,
            attn_gain,
            attn_shift,
            reduce_bias,
            final_gain,
            final_shift,
            expand_bias,
        ),
        4,
        far_in=range(1, 5 + EXP_B),
        scratch=[
            pltpu.VMEM((1, hidden_units), F32),
            pltpu.VMEM((3, wide, wide), BF16),
            pltpu.SemaphoreType.DMA((EXP_B + 4,)),
        ],
    )

    second, w_own, flags = lax.optimization_barrier((tokens[1], w_own, flags))
    rows = [rows0, [second] + [swap(second, "seg", m) for m in others]]

    def project(t):
        (out,) = call(qkv_kernel, [shape_of(all_rows, 3 * width)], ((), w_own, b_own, *rows[t]), 3)
        return out

    def attend(t, qkv, written=()):
        mem_queries = not written
        got = call(
            functools.partial(attn_fwd_kernel, slot=t, blocks=n_seg, heads=heads, mem_queries=mem_queries),
            [shape_of((size + (mem if mem_queries else 0)) // 2, 2 * width)] * n_seg
            + [shape_of(8, all_rows + 128, dtype=F32), shape_of(mem, 3 * width)]
            + [shape_of(mem, wide)] * len(written),
            ((), flags, qkv, mem_init, w_own, b_own, *written),
            8,
        )
        return list(got[:n_seg]), *got[n_seg:]

    def attend_back(t, qkv, qkv_mem, lse, grads, more=()):
        got = call(
            functools.partial(attn_bwd_kernel, slot=t, blocks=n_seg, heads=heads, mem_queries=len(grads) > n_seg),
            [shape_of(size * (2 if more else 1), 3 * width)] * n_seg + [shape_of(mem, 3 * width)],
            ((), flags, qkv, qkv_mem, lse, *grads, *more),
            8,
        )
        return list(got[:n_seg]), got[n_seg]

    def trade(blocks):
        return [blocks[0]] + [swap(blocks[m], "seg", m) for m in others]

    weights = (vecs, output_proj, expand_proj, reduce_proj)
    each = wide // (n_seg * n_doc)

    def rows_forward(mixed, hidden, result_shapes):
        n_rows = sum(h.shape[0] for h in hidden)
        left = [shape_of(n_seg, n_pair, (chunks + 2) * each, size)] * 2
        if len(hidden) > 1:
            left += [shape_of(n_pair, (chunks + 2) * each, mem)] * 2
        got = call(
            functools.partial(
                rows_fwd_kernel, n_seg=n_seg, n_pair=n_pair, n_hidden=len(hidden), together=1 if len(hidden) > 1 else 4
            ),
            [
                shape_of(n_rows, wide, dtype=F32),
                shape_of(n_rows, 128, dtype=F32),
                shape_of(n_rows, hidden_units, dtype=F32),
                shape_of(n_rows, wide, dtype=F32),
                *result_shapes,
                *left,
            ],
            ((), *mixed, *hidden, *weights),
            8,
            scratch=[pltpu.VMEM((n_rows, wide), F32)],
        )
        return got[:N_KEPT], got[N_KEPT : N_KEPT + len(hidden)], got[N_KEPT + len(hidden) :]

    qkv0 = project(0)
    mixed0, lse0, qkv_mem0 = attend(0, qkv0)
    mixed0[0], *rows[1] = lax.optimization_barrier((mixed0[0], *rows[1]))
    qkv1 = project(1)
    mixed0 = trade(mixed0)
    qkv1, mixed0[0] = lax.optimization_barrier((qkv1, mixed0[0]))
    kept0, (layer0, written), (left0, left0_send, left_m, left_m_send) = rows_forward(
        mixed0, (tokens[0], mem_init), [shape_of(size, wide), shape_of(mem, wide, dtype=F32)]
    )
    mixed1, lse1, qkv_mem1, memory1 = attend(1, qkv1, (written,))
    left0_other, left_m_other = swap(left0_send, "doc", 1), swap(left_m_send, "doc", 1)
    mixed1[0], left0_other = lax.optimization_barrier((mixed1[0], left0_other))
    kept1, (layer1,), (left1, left1_send) = rows_forward(trade(mixed1), (tokens[1],), [shape_of(size, wide)])
    left1_other = swap(left1_send, "doc", 1)
    layer_out = jnp.stack([layer0, layer1])

    def back_shapes(n_rows):
        return [
            shape_of(n_rows, hidden_units + 2 * wide),
            shape_of(n_rows, wide, dtype=F32),
            shape_of(N_VEC, wide, dtype=F32),
        ]

    n_rows = slots * size
    got = call(
        functools.partial(token_rows_back_kernel, slots=slots, n_seg=n_seg),
        back_shapes(n_rows) + [shape_of(size, slots * width)] * n_seg,
        ((), d_out, *kept0, *kept1, *weights),
        10,
        scratch=[pltpu.VMEM((n_rows, wide), F32)],
    )
    right, hidden, small = got[:3]
    grads = trade(got[3:])
    right_other = swap(right, "doc", 1)
    right, left1_other = lax.optimization_barrier((right, left1_other))

    def plain_sum(*parts):
        return sum(p.astype(F32) for p in parts).astype(BF16)

    share = [(chunks + 1) * each, chunks * each]

    def row_weights(stream, right_other):
        return call(
            functools.partial(rows_weights_kernel, stream=stream, n_seg=n_seg, n_pair=n_pair, each=each),
            [shape_of(n_seg // 2, n_pair // 2, share[stream], wide)] * 4,
            ((), left0, left1, left0_other, left1_other, right, right_other),
            2,
        )

    def both_sums(keep_a, came_a, keep_b, came_b):
        return [plain_sum(k[i], c[i]) for k, c in ((keep_a, came_a), (keep_b, came_b)) for i in range(2)]

    keep_a, send_a, keep_b, send_b = row_weights(0, right_other)
    send_a, send_b, *grads = lax.optimization_barrier((send_a, send_b, *grads))
    came_a, came_b = swap(send_a, "seg", 1), swap(send_b, "seg", 2)
    d_qkv1, d_mem1 = attend_back(1, qkv1, qkv_mem1, lse1, grads)
    d_mem1_all = trade([d_mem1[:, width:]] * n_seg)

    right_other, d_mem1_all[0] = lax.optimization_barrier((right_other, d_mem1_all[0]))
    keep_c, send_c, keep_d, send_d = row_weights(1, right_other)
    send_c, send_d, came_a, came_b, *d_mem1_all = lax.optimization_barrier(
        (send_c, send_d, came_a, came_b, *d_mem1_all)
    )
    keep_a, send_a, keep_b, send_b = both_sums(keep_a, came_a, keep_b, came_b)
    send_a, send_b, d_mem1_all[0] = lax.optimization_barrier((send_a, send_b, d_mem1_all[0]))
    came_a, came_b = swap(send_a, "seg", 2), swap(send_b, "seg", 1)

    got = call(
        functools.partial(memory_rows_back_kernel, n_seg=n_seg, size=size),
        back_shapes(mem) + [shape_of(mem, wide, dtype=F32), shape_of(mem, width)],
        ((), flags, *d_mem1_all, key_proj, value_proj, *kept0, *weights),
        6,
        scratch=[pltpu.VMEM((mem, wide), F32)],
    )
    right_m, hidden_m, small_m, memory1_grad, mixed_m = got
    right_m_other = swap(right_m, "doc", 1)
    def pair_sum(keep, came, add):
        bit = 2
        while keep.shape[0] > 1:
            bit *= 2
            if keep.shape[0] == 2:
                (keep, send) = [add(keep[i : i + 1], came[i : i + 1]) for i in range(2)]
            else:
                both = add(keep, came)
                keep, send = both[0::2], both[1::2]
            came = swap(send, "doc", bit)
        return [keep[0], came[0]]

    def quarter(stream, *halves):
        keep, send = call(
            functools.partial(quarter_kernel, stream=stream, each=each),
            [shape_of(n_pair // 2, share[stream], wide)] * 2,
            ((), left_m, left_m_other, right_m, right_m_other, *halves),
            1,
        )
        return keep, send

    right_m, came_a, came_b, send_c, send_d = lax.optimization_barrier((right_m, came_a, came_b, send_c, send_d))
    came_c, came_d = swap(send_c, "seg", 1), swap(send_d, "seg", 2)
    keep_x, send_x = quarter(0, keep_a, came_a, keep_b, came_b)
    send_x, mixed_m = lax.optimization_barrier((send_x, mixed_m))
    came_x = swap(send_x, "doc", 2)
    d_qkv, d_mem0 = attend_back(0, qkv0, qkv_mem0, lse0, [*grads, mixed_m], d_qkv1)

    came_x, d_mem0 = lax.optimization_barrier((came_x, d_mem0))
    parts_first = pair_sum(keep_x, came_x, plain_sum)

    columns = 3 * width + 2 * N_SMALL
    keep, send = call(
        functools.partial(heads_weights_kernel, slots=slots, n_seg=n_seg),
        [shape_of(n_pair, n_seg, each, columns)] * 2,
        (
            (),
            flags,
            small,
            small_m,
            hidden_m,
            memory1_grad,
            w_own,
            *rows[0],
            *rows[1],
            *d_qkv,
            mem_init,
            memory1,
            d_mem0,
            d_mem1,
        ),
        6,
    )

    def rows_final(parts, *shapes):
        return call(
            rows_final_kernel,
            [shape_of(*dims, dtype=F32) for dims in shapes],
            ((), *parts),
            1,
            far_out=range(len(shapes)),
        )

    add = functools.partial(late_sum, at=3 * width)
    came = swap(send, "doc", 1)
    came_c, came_d, keep = lax.optimization_barrier((came_c, came_d, keep))
    keep_c, send_c, keep_d, send_d = both_sums(keep_c, came_c, keep_d, came_d)
    came_c, came_d = swap(send_c, "seg", 2), swap(send_d, "seg", 1)
    _, came, parts_first[1] = lax.optimization_barrier((send_c, came, parts_first[1]))
    mine = add(keep, came)
    mine, *d_qkv = lax.optimization_barrier((mine, *d_qkv))
    came_l = swap(mine[1::2], "doc", 2)
    keep_y, send_y = quarter(1, keep_c, came_c, keep_d, came_d)
    _, came_l = lax.optimization_barrier((send_y, came_l))
    late = pair_sum(mine[0::2], came_l, add)
    parts_second = pair_sum(keep_y, swap(send_y, "doc", 2), plain_sum)
    grad_red, grad_out = rows_final(parts_first, (chunks * each, wide), (each, wide))

    back = trade(d_qkv)
    (grad_tokens,) = call(
        functools.partial(tokens_grad_kernel, slots=slots, n_seg=n_seg),
        [shape_of(slots, size, wide)],
        ((), hidden, query_proj, key_proj, value_proj, *back),
        3,
        far_out=(0,),
    )

    late[1], grad_red, grad_out, layer_out = lax.optimization_barrier((late[1], grad_red, grad_out, layer_out))
    mine = add(*late)
    parts = trade([mine[m] for m in range(n_seg)])
    grad_tokens, *parts = lax.optimization_barrier((grad_tokens, *parts))
    got = call(
        functools.partial(heads_final_kernel, n_seg=n_seg, mem=mem),
        [shape_of(each, wide, dtype=F32)] * 3
        + [shape_of(1, each, dtype=F32)] * EXP_B
        + [shape_of(1, chunks * each, dtype=F32), shape_of(mem, each, dtype=F32)],
        ((), *parts),
        1,
        far_out=range(5 + EXP_B),
    )
    (grad_exp,) = rows_final(parts_second, (each, hidden_units))
    grad_q, grad_k, grad_v = got[:3]
    flat = [v.reshape(-1) for v in got[3:-1]]

    return (
        layer_out,
        grad_tokens,
        got[-1],
        grad_q,
        flat[Q_B],
        grad_k,
        grad_v,
        flat[V_B],
        grad_out,
        flat[OUT_B],
        flat[ATTN_G],
        flat[ATTN_S],
        grad_exp,
        flat[EXP_B],
        grad_red,
        flat[RED_B],
        flat[FIN_G],
        flat[FIN_S],
    )


def solution(mesh):
    both = ("seg", "doc")
    data = P("doc", "seg", None)
    placed = (data, P("doc"), P("doc")) + (P(),) * 16 + (data,)
    vec, mat = P(both), P(both, None)
    return jax.shard_map(
        shards,
        mesh=mesh,
        in_specs=placed,
        out_specs=(
            data,
            data,
            P(None, both),
            mat,
            vec,
            mat,
            mat,
            vec,
            mat,
            vec,
            vec,
            vec,
            mat,
            vec,
            mat,
            vec,
            vec,
            vec,
        ),
        check_vma=False,
    )
```

```python
import functools

import jax
import jax.numpy as jnp
from jax import lax
from jax.experimental import pallas as pl
from jax.experimental.pallas import tpu as pltpu
from jax.sharding import PartitionSpec as P

HEADS = 12


EPS = 1e-12
NEG_FILL = -1e30
F32 = jnp.float32
BF16 = jnp.bfloat16
NN = (((1,), (0,)), ((), ()))
NT = (((1,), (1,)), ((), ()))
TN = (((0,), (0,)), ((), ()))

Q_B, V_B, OUT_B, ATTN_G, ATTN_S, RED_B, FIN_G, FIN_S, EXP_B = range(9)
N_VEC = 16
N_SMALL = 32


def mm(left, right, dims=NN):
    return lax.dot_general(left, right, dims, preferred_element_type=F32)


def swap(block, axis, mask):
    return lax.ppermute(block, axis, [(i, i ^ mask) for i in range(lax.axis_size(axis))])


FRESH, VALID = 0, 1


def flags_kernel(meta_ref, out_ref):
    new_ref, valid_ref = meta_ref
    out_ref[...] = jnp.zeros_like(out_ref)
    out_ref[FRESH : FRESH + 1] = jnp.full((1, out_ref.shape[1]), new_ref[1], jnp.int32)
    for t in range(2):
        out_ref[VALID + t : VALID + t + 1] = jnp.full((1, out_ref.shape[1]), valid_ref[t], jnp.int32)


def flag(flags_ref, i):
    return flags_ref[i : i + 1, 0:1]


def seg_here():
    return lax.axis_index("seg")


def core_here():
    return lax.axis_index("doc") & 1


def pair_here():
    return lax.axis_index("doc") >> 1


def shape_of(*dims, dtype=BF16):
    return jax.ShapeDtypeStruct(dims, dtype)


def call(kernel, out_shape, args, micros, far_in=(), far_out=(), scratch=()):
    vmem, far = pl.BlockSpec(memory_space=pltpu.VMEM), pl.BlockSpec(memory_space=pltpu.HBM)
    integers, *rest = args
    near = [
        pltpu.with_memory_space_constraint(x, pltpu.HBM if i in far_in else pltpu.VMEM) for i, x in enumerate(rest, 1)
    ]

    def body(*refs):
        kernel(refs[: len(integers)], *refs[len(integers) :])

    return pl.pallas_call(
        body,
        out_shape=[o if i in far_out else pltpu.VMEM(o.shape, o.dtype) for i, o in enumerate(out_shape)],
        in_specs=[pl.BlockSpec(memory_space=pltpu.SMEM)] * len(integers)
        + [far if i in far_in else vmem for i in range(1, len(args))],
        out_specs=[vmem] * len(out_shape),
        scratch_shapes=scratch,
        compiler_params=pltpu.CompilerParams(vmem_limit_bytes=8 << 20),
        cost_estimate=pl.CostEstimate(flops=0, transcendentals=0, bytes_accessed=int(micros * 3e6)),
    )(*integers, *near)


def reorder(x, seg, n_seg):
    width = x.shape[1] // n_seg
    bit = 1
    while bit < n_seg:
        moved = jnp.concatenate([x[:, (b ^ bit) * width : ((b ^ bit) + 1) * width] for b in range(n_seg)], axis=1)
        x = jnp.where((seg & bit) != 0, moved, x)
        bit *= 2
    return x


def in_loop(count, together, step):
    def some(j, carry):
        for k in range(together):
            step(j * together + k)
        return carry

    lax.fori_loop(0, count // together, some, 0)


def own_columns(x, seg, n_seg):
    width = x.shape[1] // n_seg
    out = x[:, :width]
    for b in range(1, n_seg):
        out = jnp.where(seg == b, x[:, b * width : (b + 1) * width], out)
    return out


def prep_kernel(meta_ref, wq_ref, wk_ref, wv_ref, *refs, n_seg, chunks):
    vec_refs, (w_ref, b_ref, out_ref, line_ref, near_ref, sems) = refs[: EXP_B + 1], refs[EXP_B + 1 :]
    weights = [
        pltpu.make_async_copy(r, near_ref.at[i], sems.at[EXP_B + 1 + i]) for i, r in enumerate((wq_ref, wk_ref, wv_ref))
    ]
    for c in weights:
        c.start()
    copies = [pltpu.make_async_copy(r, out_ref.at[i], sems.at[i]) for i, r in enumerate(vec_refs[:EXP_B])]
    copies.append(pltpu.make_async_copy(vec_refs[EXP_B], line_ref.at[0], sems.at[EXP_B]))
    for c in copies:
        c.start()
    seg = seg_here()
    rows = w_ref.shape[0] // 8
    width = w_ref.shape[1] // 3
    for c in weights:
        c.wait()

    def some_rows(i):
        these = pl.ds(pl.multiple_of(i * rows, rows), rows)
        for b in range(n_seg):

            @pl.when(seg == b)
            def _():
                cols = slice(b * width, (b + 1) * width)
                w_ref[these] = jnp.concatenate([near_ref[k, these, cols] for k in range(3)], axis=1)


    in_loop(8, 1, some_rows)
    for c in copies:
        c.wait()
    wide = out_ref.shape[1]
    for q in range(chunks):
        out_ref[EXP_B + q : EXP_B + q + 1] = line_ref[:, q * wide : (q + 1) * wide]
    q_b = own_columns(out_ref[Q_B : Q_B + 1], seg, n_seg)
    v_b = own_columns(out_ref[V_B : V_B + 1], seg, n_seg)
    b_ref[...] = jnp.concatenate([q_b, jnp.zeros_like(q_b), v_b], axis=1)


def qkv_kernel(meta_ref, w_ref, b_ref, *refs):
    rows, out_ref = refs[:-1], refs[-1]
    size = rows[0].shape[0]
    for b, r in enumerate(rows):
        out_ref[b * size : (b + 1) * size, :] = (mm(r[...], w_ref[...]) + b_ref[...]).astype(BF16)


def mask_block(meta_ref, slot, blocks, size, mem, width):
    total = blocks * size + 2 * mem
    row = lax.broadcasted_iota(jnp.int32, (total, width), 0)
    col = lax.broadcasted_iota(jnp.int32, (total, width), 1)
    place = row
    for b in range(blocks):
        inside = (row >= b * size) & (row < (b + 1) * size)
        place = jnp.where(inside, ((seg_here() ^ b) - b) * size + row, place)
    out = (place >= flag(meta_ref, VALID + slot)) & (row < blocks * size) & (col == 0)
    return jnp.where(out, NEG_FILL, 0.0).astype(BF16)


def ones_block(rows, width):
    col = lax.broadcasted_iota(jnp.int32, (rows, width), 1)
    return jnp.where(col == 0, 1.0, 0.0).astype(BF16)


def with_memory(rows, memory):
    return jnp.concatenate([rows, memory, memory], axis=0)


SCALE = 0.125 * 1.4426950408889634


def attn_fwd_kernel(_, meta_ref, qkv_ref, mem_ref, w_ref, b_ref, *outs, slot, blocks, heads, mem_queries):
    if mem_queries:
        memory = mem_ref[...]
    else:
        written_ref, outs = outs[0], outs[1:]
        memory = jnp.where(flag(meta_ref, FRESH) == 1, mem_ref[...], written_ref[...].astype(BF16))
        outs[-1][...] = memory
    mix_refs, lse_ref, mem_out_ref = outs[:blocks], outs[blocks], outs[blocks + 1]
    size = qkv_ref.shape[0] // blocks
    mem = mem_ref.shape[0]
    width = qkv_ref.shape[1] // 3
    head_dim = width // heads
    mem_out_ref[...] = (mm(memory, w_ref[...]) + b_ref[...]).astype(BF16)
    mask = mask_block(meta_ref, slot, blocks, size, mem, head_dim)
    ones = ones_block(size, head_dim)
    value_t = with_memory(qkv_ref[:, 2 * width :], mem_out_ref[:, 2 * width :]).T
    keys = []
    for h in range(heads):
        cols = slice(width + h * head_dim, width + (h + 1) * head_dim)
        keys.append(jnp.concatenate([with_memory(qkv_ref[:, cols], mem_out_ref[:, cols]), mask], axis=1))

    def mixed_of(queries, ones, first):
        out = []
        for h in range(heads):
            lo, hi = h * head_dim, (h + 1) * head_dim
            scores = mm(keys[h], jnp.concatenate([queries[:, lo:hi], ones], axis=1), NT)
            highest = jnp.max(scores, axis=0, keepdims=True)
            weights = jnp.exp2((scores - highest) * SCALE)
            total = jnp.sum(weights, axis=0, keepdims=True)
            out.append(mm(value_t[lo:hi], weights.astype(BF16)) * (1.0 / total))
            lse_ref[h : h + 1, first : first + queries.shape[0]] = highest * SCALE + jnp.log(total) * 1.4426950408889634
        return jnp.concatenate(out, axis=0).T.astype(BF16)

    def put(b, row, rows):
        half = mix_refs[b].shape[0]
        cut = max(0, min(rows.shape[0], half - row))
        if cut:
            mix_refs[b][row : row + cut, :width] = rows[:cut]
        if cut < rows.shape[0]:
            mix_refs[b][row + cut - half : row + rows.shape[0] - half, width:] = rows[cut:]

    for b in range(blocks):
        put(b, 0, mixed_of(qkv_ref[b * size : (b + 1) * size, :width], ones, b * size))
    if mem_queries:
        mixed = mixed_of(mem_out_ref[:, :width], ones[:mem], blocks * size)
        for b in range(blocks):
            put(b, size, mixed)


def attn_bwd_kernel(_, meta_ref, qkv_ref, mem_ref, lse_ref, *refs, slot, blocks, heads, mem_queries):
    n_grad = blocks + (1 if mem_queries else 0)
    grad_refs, refs = refs[:n_grad], refs[n_grad:]
    more_refs, out_refs, mem_out_ref = refs[: -blocks - 1], refs[-blocks - 1 : -1], refs[-1]
    for more_ref, out_ref in zip(more_refs, out_refs):
        out_ref[out_ref.shape[0] - more_ref.shape[0] :, :] = more_ref[...]
    size = qkv_ref.shape[0] // blocks
    mem = mem_ref.shape[0]
    width = qkv_ref.shape[1] // 3
    first = slot * width
    head_dim = width // heads
    own = blocks * size + mem
    mask = mask_block(meta_ref, slot, blocks, size, mem, head_dim)
    ones = ones_block(size, head_dim)
    key_t = with_memory(qkv_ref[:, width : 2 * width], mem_ref[:, width : 2 * width]).T
    grad_q = [[] for _ in range(n_grad)]
    for h in range(heads):
        lo, hi = h * head_dim, (h + 1) * head_dim
        key = with_memory(qkv_ref[:, width + lo : width + hi], mem_ref[:, width + lo : width + hi])
        key = jnp.concatenate([key, mask], axis=1)
        value = with_memory(qkv_ref[:, 2 * width + lo : 2 * width + hi], mem_ref[:, 2 * width + lo : 2 * width + hi])

        def one(query, ones, grad, lse):
            scores = mm(key, jnp.concatenate([query, ones], axis=1), NT)
            probs = jnp.exp2(scores * SCALE - lse)
            grad_probs = mm(value, grad, NT)
            inner = jnp.sum(grad_probs * probs, axis=0, keepdims=True)
            return (probs * (grad_probs - inner)).astype(BF16), probs.astype(BF16)

        queries, grads, scores_g, probs = [], [], [], []
        for b in range(blocks):
            queries.append(qkv_ref[b * size : (b + 1) * size, lo:hi])
            grads.append(grad_refs[b][:, first + lo : first + hi])
            g, p = one(queries[b], ones, grads[b], lse_ref[h : h + 1, b * size : (b + 1) * size])
            scores_g.append(g)
            probs.append(p)
            grad_q[b].append(mm(key_t[lo:hi], g) * 0.125)
        grad_key = mm(jnp.concatenate([g[:own] for g in scores_g], axis=1), jnp.concatenate(queries, axis=0))
        grad_value = mm(jnp.concatenate([p[:own] for p in probs], axis=1), jnp.concatenate(grads, axis=0))
        if mem_queries:
            query, grad = mem_ref[:, lo:hi], grad_refs[blocks][:, lo:hi]
            g, p = one(query, ones[:mem], grad, lse_ref[h : h + 1, blocks * size : own])
            grad_q[blocks].append(mm(key_t[lo:hi], g) * 0.125)
            grad_key = grad_key + mm(g[:own], query)
            grad_value = grad_value + mm(p[:own], grad)
        grad_key = (grad_key * 0.125).astype(BF16)
        grad_value = grad_value.astype(BF16)
        for b in range(blocks):
            out_refs[b][:size, width + lo : width + hi] = grad_key[b * size : (b + 1) * size]
            out_refs[b][:size, 2 * width + lo : 2 * width + hi] = grad_value[b * size : (b + 1) * size]
        mem_out_ref[:, width + lo : width + hi] = grad_key[blocks * size :]
        mem_out_ref[:, 2 * width + lo : 2 * width + hi] = grad_value[blocks * size :]
    for b in range(blocks):
        out_refs[b][:size, :width] = jnp.concatenate(grad_q[b], axis=0).T.astype(BF16)
    if mem_queries:
        mem_out_ref[:, :width] = jnp.concatenate(grad_q[blocks], axis=0).T.astype(BF16)
    else:
        mem_out_ref[:, :width] = jnp.zeros((mem, width), BF16)


def norm_parts(hidden):
    center = hidden - jnp.mean(hidden, axis=-1, keepdims=True)
    inverse = lax.rsqrt(jnp.mean(center * center, axis=-1, keepdims=True) + EPS)
    return center * inverse, inverse


def norm_back(grad, gain, unit, inverse):
    scaled = grad * gain
    mean_scaled = jnp.mean(scaled, axis=-1, keepdims=True)
    mean_product = jnp.mean(scaled * unit, axis=-1, keepdims=True)
    return inverse * (scaled - mean_scaled - unit * mean_product)


def gelu_and_slope(pre):
    cdf = 0.5 * (1.0 + lax.erf(pre * (2.0**-0.5)))
    density = jnp.exp(-0.5 * pre * pre) * 0.3989422804014327
    return pre * cdf, cdf + pre * density


N_KEPT = 4


def rows_fwd_kernel(meta_ref, *refs, n_seg, n_pair, n_hidden, together):
    mix_refs, hid_refs = refs[:n_seg], refs[n_seg : n_seg + n_hidden]
    vec_ref, out_ref, exp_ref, red_ref = refs[n_seg + n_hidden : n_seg + n_hidden + 4]
    outs = refs[n_seg + n_hidden + 4 :]
    unit_a_ref, inv_ref, slope_ref, unit_f_ref = outs[:N_KEPT]
    result_refs, left_refs, acc_ref = outs[N_KEPT : N_KEPT + n_hidden], outs[N_KEPT + n_hidden : -1], outs[-1]
    wide = out_ref.shape[0]
    size = hid_refs[0].shape[0]

    def vec(i):
        return vec_ref[i : i + 1]

    def keep_left(x, at, first, blocks):
        left_factors(meta_ref, x, left_refs, at, first, blocks, n_seg, n_pair, size)

    each = wide // (n_seg * n_pair * 2)
    width = mix_refs[0].shape[1] // 2
    halves = [
        jnp.concatenate([r[:, i * width : (i + 1) * width] for r in mix_refs], axis=1).astype(F32) for i in range(2)
    ]
    mixed = reorder(jnp.concatenate(halves, axis=0).astype(BF16), seg_here(), n_seg)
    hidden = jnp.concatenate([r[...].astype(F32) for r in hid_refs], axis=0)
    unit, inverse = norm_parts(hidden + (mm(mixed, out_ref[...]) + vec(OUT_B)))
    unit_a_ref[...] = unit
    inv_ref[:, 0:1] = inverse
    normed = unit * vec(ATTN_G) + vec(ATTN_S)
    low = normed.astype(BF16)
    chunks = exp_ref.shape[1] // wide
    acc_ref[...] = normed + vec(RED_B)

    def chunk(q):
        cols = pl.ds(pl.multiple_of(q * wide, wide), wide)
        active, slope = gelu_and_slope(mm(low, exp_ref[:, cols]) + vec_ref[pl.ds(EXP_B + q, 1)])
        slope_ref[:, cols] = slope
        active = active.astype(BF16)
        acc_ref[...] += mm(active, red_ref[cols])
        keep_left(active, each, q * (n_seg // chunks), n_seg // chunks)

    in_loop(chunks, together, chunk)
    unit, inverse = norm_parts(acc_ref[...])
    unit_f_ref[...] = unit
    inv_ref[:, 1:2] = inverse
    result = unit * vec(FIN_G) + vec(FIN_S)
    at = 0
    for r in result_refs:
        r[...] = result[at : at + r.shape[0]].astype(r.dtype)
        at += r.shape[0]
    keep_left(low, 0, 0, n_seg)
    keep_left(mixed, (chunks + 1) * each, 0, n_seg)


def left_factors(meta_ref, x, left_refs, at, first, blocks, n_seg, n_pair, size):
    seg, core, pair = seg_here(), core_here(), pair_here()
    rows = x.shape[1] // (blocks * n_pair * 2)
    keep_ref, send_ref = left_refs[:2]
    keep, send = core_halves(x[:size].astype(F32).T, core, n_pair, rows)
    for s in range(blocks):
        for z in range(n_pair):
            keep_ref[(first + s) ^ seg, z ^ pair, at : at + rows] = keep[s * n_pair + z]
            send_ref[(first + s) ^ seg, z ^ pair, at : at + rows] = send[s * n_pair + z]
    if left_refs[2:]:
        keep_ref, send_ref = left_refs[2:]
        mine = x[size:].astype(F32)
        if blocks > 1:
            assert blocks == n_seg
            mine = own_columns(mine, seg, n_seg)
        keep, send = core_halves(mine.T, core, n_pair, rows)

        @pl.when((seg == first) | (blocks > 1))
        def _():
            for z in range(n_pair):
                keep_ref[z ^ pair, at : at + rows] = keep[z]
                send_ref[z ^ pair, at : at + rows] = send[z]


def core_halves(x, core, pairs, rows):
    x = x.reshape(x.shape[0] // (2 * rows), 2, rows, x.shape[1])
    even, odd = x[:, 0], x[:, 1]
    return jnp.where(core == 0, even, odd).astype(BF16), jnp.where(core == 0, odd, even).astype(BF16)


def rows_back(seg, n_seg, grad, kept, vec_ref, out_ref, exp_ref, red_ref, outs, acc_ref, together):
    right_ref, hidden_ref, small_ref = outs
    wide = hidden_ref.shape[1]
    chunks = exp_ref.shape[1] // wide

    def vec(i):
        return vec_ref[i : i + 1]

    def total(x):
        return jnp.sum(x, axis=0, keepdims=True)

    unit = kept(3)
    grad_sum = norm_back(grad, vec(FIN_G), unit, kept(1)[:, 1:2])
    low = grad_sum.astype(BF16)
    right_ref[:, chunks * wide : (chunks + 1) * wide] = low
    small_ref[...] = jnp.zeros_like(small_ref)
    small_ref[FIN_G : FIN_G + 1] = total(grad * unit)
    small_ref[FIN_S : FIN_S + 1] = total(grad)
    small_ref[RED_B : RED_B + 1] = total(low.astype(F32))
    acc_ref[...] = grad_sum

    def chunk(q):
        cols = pl.ds(pl.multiple_of(q * wide, wide), wide)
        grad_pre = (mm(low, red_ref[cols], NT) * kept(2, cols)).astype(BF16)
        right_ref[:, cols] = grad_pre
        small_ref[pl.ds(EXP_B + q, 1)] = total(grad_pre.astype(F32))
        acc_ref[...] += mm(grad_pre, exp_ref[:, cols], NT)

    in_loop(chunks, together, chunk)
    acc = acc_ref[...]
    unit = kept(0)
    small_ref[ATTN_G : ATTN_G + 1] = total(acc * unit)
    small_ref[ATTN_S : ATTN_S + 1] = total(acc)
    grad_hidden = norm_back(acc, vec(ATTN_G), unit, kept(1)[:, 0:1])
    hidden_ref[...] = grad_hidden
    low = grad_hidden.astype(BF16)
    right_ref[:, (chunks + 1) * wide :] = low
    small_ref[OUT_B : OUT_B + 1] = total(low.astype(F32))
    return reorder(mm(low, out_ref[...], NT).astype(BF16), seg, n_seg)


def token_rows_back_kernel(meta_ref, grad_ref, *refs, slots, n_seg):
    kept_refs = [refs[t * N_KEPT : (t + 1) * N_KEPT] for t in range(slots)]
    refs = refs[slots * N_KEPT :]
    (vec_ref, out_ref, exp_ref, red_ref), outs, mix_refs, acc_ref = refs[:4], refs[4:7], refs[7:-1], refs[-1]
    size = grad_ref.shape[1]

    def kept(i, cols=slice(None)):
        return jnp.concatenate([kept_refs[t][i][:size, cols] for t in range(slots)], axis=0)

    grad = jnp.concatenate([grad_ref[t].astype(F32) for t in range(slots)], axis=0)
    mixed = rows_back(seg_here(), n_seg, grad, kept, vec_ref, out_ref, exp_ref, red_ref, outs, acc_ref, 4)
    width = mixed.shape[1] // n_seg
    for m in range(n_seg):
        for t in range(slots):
            mix_refs[m][:, t * width : (t + 1) * width] = mixed[t * size : (t + 1) * size, m * width : (m + 1) * width]


def memory_rows_back_kernel(_, meta_ref, *refs, n_seg, size):
    d_refs, refs = refs[:n_seg], refs[n_seg:]
    (wk_ref, wv_ref), kept_refs, refs = refs[:2], refs[2 : 2 + N_KEPT], refs[2 + N_KEPT :]
    (vec_ref, out_ref, exp_ref, red_ref), outs, (memory_ref, own_ref, acc_ref) = refs[:4], refs[4:7], refs[7:]
    seg = seg_here()
    width = d_refs[0].shape[1] // 2
    d_key = reorder(jnp.concatenate([r[:, :width] for r in d_refs], axis=1), seg, n_seg)
    d_value = reorder(jnp.concatenate([r[:, width:] for r in d_refs], axis=1), seg, n_seg)
    grad = 2.0 * (mm(d_key, wk_ref[...], NT) + mm(d_value, wv_ref[...], NT))
    memory_ref[...] = grad
    grad = jnp.where(flag(meta_ref, FRESH) == 1, jnp.zeros_like(grad), grad)

    def kept(i, cols=slice(None)):
        return kept_refs[i][size:, cols]

    mixed = rows_back(seg, n_seg, grad, kept, vec_ref, out_ref, exp_ref, red_ref, outs, acc_ref, 1)
    own_ref[...] = mixed[:, : own_ref.shape[1]]


def tokens_grad_kernel(meta_ref, hidden_ref, wq_ref, wk_ref, wv_ref, *refs, slots, n_seg):
    d_refs, out_ref = refs[:-1], refs[-1]
    size = out_ref.shape[1]
    width = d_refs[0].shape[1] // 3
    seg = seg_here()

    def slot(t):
        these = pl.ds(pl.multiple_of(t * size, size), size)
        grad = hidden_ref[these]
        for i, w_ref in enumerate((wq_ref, wk_ref, wv_ref)):
            part = jnp.concatenate([r[these, i * width : (i + 1) * width] for r in d_refs], 1)
            grad = grad + mm(reorder(part, seg, n_seg), w_ref[...], NT)
        out_ref[t] = grad.astype(BF16)

    in_loop(slots, 1, slot)


def row_parts(stream, chunks, each):
    if stream == 1:
        return [(0, each, q, q * each) for q in range(chunks)]
    return [(each, chunks * each, chunks, 0), ((chunks + 1) * each, each, chunks + 1, chunks * each)]


def rows_weights_kernel(meta_ref, *refs, stream, n_seg, n_pair, each):
    left_refs, (right_ref, other_ref), outs = refs[:-6], refs[-6:-4], refs[-4:]
    wide = outs[0].shape[3]
    half = n_pair // 2
    for lo, rows, q, row in row_parts(stream, right_ref.shape[1] // wide - 2, each):
        left = jnp.concatenate(
            [r[:, :, lo : lo + rows].reshape(n_seg * n_pair * rows, r.shape[3]) for r in left_refs], axis=1
        )
        right = jnp.concatenate([r[:, q * wide : (q + 1) * wide] for r in (right_ref, other_ref)], axis=0)
        full = mm(left, right).reshape(n_seg, n_pair, rows, wide).astype(BF16)
        for s in range(n_seg):
            low, high = s & 1, s >> 1
            outs[low][high, :, row : row + rows] = full[s, :half]
            outs[2 + high][low, :, row : row + rows] = full[s, half:]


def quarter_kernel(meta_ref, left_ref, left2_ref, right_ref, right2_ref, *refs, stream, each):
    half_refs, outs = (refs[:2], refs[2:4]), refs[4:]
    wide = outs[0].shape[2]
    pairs = left_ref.shape[0]
    half = pairs // 2
    for lo, rows, q, row in row_parts(stream, right_ref.shape[1] // wide - 2, each):

        def rows_of(r):
            return jnp.concatenate([r[z].astype(F32)[lo : lo + rows] for z in range(pairs)], axis=0)

        left = jnp.concatenate([rows_of(left_ref), rows_of(left2_ref)], axis=1).astype(BF16)
        right = jnp.concatenate([r[:, q * wide : (q + 1) * wide] for r in (right_ref, right2_ref)], axis=0)
        part = mm(left, right).reshape(pairs, rows, wide)
        for z in range(pairs):
            total = part[z]
            for r in half_refs[z // half]:
                total = total + r[z % half, row : row + rows].astype(F32)
            outs[z & 1][z >> 1, row : row + rows] = total.astype(BF16)


def heads_weights_kernel(_, meta_ref, small_ref, small_m_ref, hid_ref, memory_ref, w_ref, *refs, slots, n_seg):
    rows, refs = refs[: slots * n_seg], refs[slots * n_seg :]
    grads, (mem0_ref, mem1_ref, dm0_ref, dm1_ref, keep_ref, send_ref) = refs[:n_seg], refs[n_seg:]
    seg, core, pair, fresh1 = seg_here(), core_here(), pair_here(), flag(meta_ref, FRESH)
    wide = rows[0].shape[1]
    width = wide // n_seg
    each = keep_ref.shape[2]
    col = lax.broadcasted_iota(jnp.int32, (1, 3 * width), 1)
    twice = jnp.where(col < width, 1.0, 2.0)
    dm0 = (dm0_ref[...].astype(F32) * twice).astype(BF16)
    dm1 = (dm1_ref[...].astype(F32) * twice).astype(BF16)
    full = mm(mem0_ref[...], dm0, TN) + mm(mem1_ref[...], dm1, TN)
    sums = jnp.sum(dm0.astype(F32), axis=0, keepdims=True) + jnp.sum(dm1.astype(F32), axis=0, keepdims=True)
    for m, g in enumerate(grads):
        x = jnp.concatenate([r[...] for r in rows[m::n_seg]], axis=0)
        full = full + mm(x, g[...], TN)
        sums = sums + jnp.sum(g[...].astype(F32), axis=0, keepdims=True)
    grad_mem = mm(dm0, w_ref[...], NT)
    whole = hid_ref[...] + jnp.where(fresh1 == 1, memory_ref[...], 0.0)
    grad_mem = grad_mem + jnp.where(seg == 0, whole, 0.0)

    def placed(v):
        return reorder(jnp.concatenate([v, jnp.zeros((1, wide - width), F32)], axis=1), seg, n_seg)

    n_pair = keep_ref.shape[0]
    chunks = 4
    head = EXP_B + chunks
    given = small_ref[...] + jnp.where(seg == 0, small_m_ref[...], 0.0)
    small = jnp.concatenate(
        [
            placed(sums[:, :width]),
            placed(sums[:, 2 * width :]),
            given[2:head],
            grad_mem,
            jnp.zeros((N_SMALL - head - grad_mem.shape[0], wide), F32),
        ],
        axis=0,
    ).T
    turned = small.reshape(wide // (chunks * each), chunks, each, N_SMALL)
    spread = [
        jnp.concatenate(
            [turned[:, k, :, EXP_B + q : EXP_B + q + 1].reshape(wide // chunks, 1) for k in range(chunks)], axis=1
        )
        for q in range(chunks)
    ]
    small = jnp.concatenate([small[:, :EXP_B], jnp.concatenate(spread, axis=0), small[:, head:]], axis=1)
    high = small.astype(BF16)
    rest = (small - high.astype(F32)).astype(BF16)
    full = jnp.concatenate([full, high.astype(F32), rest.astype(F32)], axis=1)
    keep, send = core_halves(full, core, n_pair, each)
    for s in range(n_seg):
        for z in range(n_pair):
            keep_ref[z ^ pair, s ^ seg] = keep[s * n_pair + z]
            send_ref[z ^ pair, s ^ seg] = send[s * n_pair + z]


def late_sum(*parts, at):
    total = sum(p.astype(F32) for p in parts)
    small = total[..., at : at + N_SMALL] + total[..., at + N_SMALL :]
    high = small.astype(BF16)
    rest = (small - high.astype(F32)).astype(BF16)
    return jnp.concatenate([total[..., :at].astype(BF16), high, rest], axis=-1)


def heads_final_kernel(meta_ref, *refs, n_seg, mem):
    ins, outs = refs[:n_seg], refs[n_seg:]
    seg = seg_here()
    width = outs[0].shape[1] // n_seg
    total = [r[...].astype(F32) for r in ins]
    for i in range(3):
        outs[i][...] = reorder(
            jnp.concatenate([total[m][:, i * width : (i + 1) * width] for m in range(n_seg)], axis=1), seg, n_seg
        )
    at = 3 * width
    small = sum(t[:, at : at + N_SMALL] + t[:, at + N_SMALL : at + 2 * N_SMALL] for t in total).T
    vec_refs, exp_ref, mem_ref = outs[3 : 3 + EXP_B], outs[3 + EXP_B], outs[4 + EXP_B]
    for i, r in enumerate(vec_refs):
        r[...] = small[i : i + 1]
    exp_ref[...] = jnp.concatenate([small[EXP_B + q : EXP_B + q + 1] for q in range(4)], axis=1)
    mem_ref[...] = small[EXP_B + 4 : EXP_B + 4 + mem]


def rows_final_kernel(meta_ref, first_ref, second_ref, *outs):
    total = first_ref[...].astype(F32) + second_ref[...].astype(F32)
    wide = total.shape[1]
    at = 0
    for r in outs:
        for q in range(r.shape[1] // wide):
            r[:, q * wide : (q + 1) * wide] = total[at : at + r.shape[0]]
            at += r.shape[0]


def shards(
    tokens,
    new_doc,
    valid_len,
    mem_init,
    query_proj,
    query_bias,
    key_proj,
    value_proj,
    value_bias,
    output_proj,
    output_bias,
    attn_gain,
    attn_shift,
    expand_proj,
    expand_bias,
    reduce_proj,
    reduce_bias,
    final_gain,
    final_shift,
    d_out,
):
    slots, size, wide = tokens.shape
    assert slots == 2
    n_seg, n_doc = lax.axis_size("seg"), lax.axis_size("doc")
    n_pair = n_doc // 2
    hidden_units = expand_proj.shape[1]
    chunks = hidden_units // wide
    assert chunks == 4
    mem = mem_init.shape[0]
    width = wide // n_seg
    heads = HEADS // n_seg
    others = range(1, n_seg)
    all_rows = n_seg * size

    rows0 = [tokens[0]] + [swap(tokens[0], "seg", m) for m in others]
    (flags,) = call(flags_kernel, [shape_of(8, 128, dtype=jnp.int32)], ((new_doc, valid_len),), 1)
    w_own, b_own, vecs = call(
        functools.partial(prep_kernel, n_seg=n_seg, chunks=chunks),
        [shape_of(wide, 3 * width), shape_of(1, 3 * width, dtype=F32), shape_of(N_VEC, wide, dtype=F32)],
        (
            (),
            query_proj,
            key_proj,
            value_proj,
            query_bias,
            value_bias,
            output_bias,
            attn_gain,
            attn_shift,
            reduce_bias,
            final_gain,
            final_shift,
            expand_bias,
        ),
        4,
        far_in=range(1, 5 + EXP_B),
        scratch=[
            pltpu.VMEM((1, hidden_units), F32),
            pltpu.VMEM((3, wide, wide), BF16),
            pltpu.SemaphoreType.DMA((EXP_B + 4,)),
        ],
    )

    second, w_own, flags = lax.optimization_barrier((tokens[1], w_own, flags))
    rows = [rows0, [second] + [swap(second, "seg", m) for m in others]]

    def project(t):
        (out,) = call(qkv_kernel, [shape_of(all_rows, 3 * width)], ((), w_own, b_own, *rows[t]), 3)
        return out

    def attend(t, qkv, written=()):
        mem_queries = not written
        got = call(
            functools.partial(attn_fwd_kernel, slot=t, blocks=n_seg, heads=heads, mem_queries=mem_queries),
            [shape_of((size + (mem if mem_queries else 0)) // 2, 2 * width)] * n_seg
            + [shape_of(8, all_rows + 128, dtype=F32), shape_of(mem, 3 * width)]
            + [shape_of(mem, wide)] * len(written),
            ((), flags, qkv, mem_init, w_own, b_own, *written),
            8,
        )
        return list(got[:n_seg]), *got[n_seg:]

    def attend_back(t, qkv, qkv_mem, lse, grads, more=()):
        got = call(
            functools.partial(attn_bwd_kernel, slot=t, blocks=n_seg, heads=heads, mem_queries=len(grads) > n_seg),
            [shape_of(size * (2 if more else 1), 3 * width)] * n_seg + [shape_of(mem, 3 * width)],
            ((), flags, qkv, qkv_mem, lse, *grads, *more),
            8,
        )
        return list(got[:n_seg]), got[n_seg]

    def trade(blocks):
        return [blocks[0]] + [swap(blocks[m], "seg", m) for m in others]

    weights = (vecs, output_proj, expand_proj, reduce_proj)
    each = wide // (n_seg * n_doc)

    def rows_forward(mixed, hidden, result_shapes):
        n_rows = sum(h.shape[0] for h in hidden)
        left = [shape_of(n_seg, n_pair, (chunks + 2) * each, size)] * 2
        if len(hidden) > 1:
            left += [shape_of(n_pair, (chunks + 2) * each, mem)] * 2
        got = call(
            functools.partial(
                rows_fwd_kernel, n_seg=n_seg, n_pair=n_pair, n_hidden=len(hidden), together=1 if len(hidden) > 1 else 4
            ),
            [
                shape_of(n_rows, wide, dtype=F32),
                shape_of(n_rows, 128, dtype=F32),
                shape_of(n_rows, hidden_units, dtype=F32),
                shape_of(n_rows, wide, dtype=F32),
                *result_shapes,
                *left,
            ],
            ((), *mixed, *hidden, *weights),
            8,
            scratch=[pltpu.VMEM((n_rows, wide), F32)],
        )
        return got[:N_KEPT], got[N_KEPT : N_KEPT + len(hidden)], got[N_KEPT + len(hidden) :]

    qkv0 = project(0)
    mixed0, lse0, qkv_mem0 = attend(0, qkv0)
    mixed0[0], *rows[1] = lax.optimization_barrier((mixed0[0], *rows[1]))
    qkv1 = project(1)
    mixed0 = trade(mixed0)
    qkv1, mixed0[0] = lax.optimization_barrier((qkv1, mixed0[0]))
    kept0, (layer0, written), (left0, left0_send, left_m, left_m_send) = rows_forward(
        mixed0, (tokens[0], mem_init), [shape_of(size, wide), shape_of(mem, wide, dtype=F32)]
    )
    mixed1, lse1, qkv_mem1, memory1 = attend(1, qkv1, (written,))
    left0_other, left_m_other = swap(left0_send, "doc", 1), swap(left_m_send, "doc", 1)
    mixed1[0], left0_other = lax.optimization_barrier((mixed1[0], left0_other))
    kept1, (layer1,), (left1, left1_send) = rows_forward(trade(mixed1), (tokens[1],), [shape_of(size, wide)])
    left1_other = swap(left1_send, "doc", 1)
    layer_out = jnp.stack([layer0, layer1])

    def back_shapes(n_rows):
        return [
            shape_of(n_rows, hidden_units + 2 * wide),
            shape_of(n_rows, wide, dtype=F32),
            shape_of(N_VEC, wide, dtype=F32),
        ]

    n_rows = slots * size
    got = call(
        functools.partial(token_rows_back_kernel, slots=slots, n_seg=n_seg),
        back_shapes(n_rows) + [shape_of(size, slots * width)] * n_seg,
        ((), d_out, *kept0, *kept1, *weights),
        10,
        scratch=[pltpu.VMEM((n_rows, wide), F32)],
    )
    right, hidden, small = got[:3]
    grads = trade(got[3:])
    right_other = swap(right, "doc", 1)
    right, left1_other = lax.optimization_barrier((right, left1_other))

    def plain_sum(*parts):
        return sum(p.astype(F32) for p in parts).astype(BF16)

    share = [(chunks + 1) * each, chunks * each]

    def row_weights(stream, right_other):
        return call(
            functools.partial(rows_weights_kernel, stream=stream, n_seg=n_seg, n_pair=n_pair, each=each),
            [shape_of(n_seg // 2, n_pair // 2, share[stream], wide)] * 4,
            ((), left0, left1, left0_other, left1_other, right, right_other),
            2,
        )

    def both_sums(keep_a, came_a, keep_b, came_b):
        return [plain_sum(k[i], c[i]) for k, c in ((keep_a, came_a), (keep_b, came_b)) for i in range(2)]

    keep_a, send_a, keep_b, send_b = row_weights(0, right_other)
    send_a, send_b, *grads = lax.optimization_barrier((send_a, send_b, *grads))
    came_a, came_b = swap(send_a, "seg", 1), swap(send_b, "seg", 2)
    d_qkv1, d_mem1 = attend_back(1, qkv1, qkv_mem1, lse1, grads)
    d_mem1_all = trade([d_mem1[:, width:]] * n_seg)

    right_other, d_mem1_all[0] = lax.optimization_barrier((right_other, d_mem1_all[0]))
    keep_c, send_c, keep_d, send_d = row_weights(1, right_other)
    send_c, send_d, came_a, came_b, *d_mem1_all = lax.optimization_barrier(
        (send_c, send_d, came_a, came_b, *d_mem1_all)
    )
    keep_a, send_a, keep_b, send_b = both_sums(keep_a, came_a, keep_b, came_b)
    send_a, send_b, d_mem1_all[0] = lax.optimization_barrier((send_a, send_b, d_mem1_all[0]))
    came_a, came_b = swap(send_a, "seg", 2), swap(send_b, "seg", 1)

    got = call(
        functools.partial(memory_rows_back_kernel, n_seg=n_seg, size=size),
        back_shapes(mem) + [shape_of(mem, wide, dtype=F32), shape_of(mem, width)],
        ((), flags, *d_mem1_all, key_proj, value_proj, *kept0, *weights),
        6,
        scratch=[pltpu.VMEM((mem, wide), F32)],
    )
    right_m, hidden_m, small_m, memory1_grad, mixed_m = got
    right_m_other = swap(right_m, "doc", 1)
    def pair_sum(keep, came, add):
        bit = 2
        while keep.shape[0] > 1:
            bit *= 2
            if keep.shape[0] == 2:
                (keep, send) = [add(keep[i : i + 1], came[i : i + 1]) for i in range(2)]
            else:
                both = add(keep, came)
                keep, send = both[0::2], both[1::2]
            came = swap(send, "doc", bit)
        return [keep[0], came[0]]

    def quarter(stream, *halves):
        keep, send = call(
            functools.partial(quarter_kernel, stream=stream, each=each),
            [shape_of(n_pair // 2, share[stream], wide)] * 2,
            ((), left_m, left_m_other, right_m, right_m_other, *halves),
            1,
        )
        return keep, send

    right_m, came_a, came_b, send_c, send_d = lax.optimization_barrier((right_m, came_a, came_b, send_c, send_d))
    came_c, came_d = swap(send_c, "seg", 1), swap(send_d, "seg", 2)
    keep_x, send_x = quarter(0, keep_a, came_a, keep_b, came_b)
    send_x, mixed_m = lax.optimization_barrier((send_x, mixed_m))
    came_x = swap(send_x, "doc", 2)
    d_qkv, d_mem0 = attend_back(0, qkv0, qkv_mem0, lse0, [*grads, mixed_m], d_qkv1)

    came_x, d_mem0 = lax.optimization_barrier((came_x, d_mem0))
    parts_first = pair_sum(keep_x, came_x, plain_sum)

    columns = 3 * width + 2 * N_SMALL
    keep, send = call(
        functools.partial(heads_weights_kernel, slots=slots, n_seg=n_seg),
        [shape_of(n_pair, n_seg, each, columns)] * 2,
        (
            (),
            flags,
            small,
            small_m,
            hidden_m,
            memory1_grad,
            w_own,
            *rows[0],
            *rows[1],
            *d_qkv,
            mem_init,
            memory1,
            d_mem0,
            d_mem1,
        ),
        6,
    )

    def rows_final(parts, *shapes):
        return call(
            rows_final_kernel,
            [shape_of(*dims, dtype=F32) for dims in shapes],
            ((), *parts),
            1,
            far_out=range(len(shapes)),
        )

    add = functools.partial(late_sum, at=3 * width)
    came = swap(send, "doc", 1)
    came_c, came_d, keep = lax.optimization_barrier((came_c, came_d, keep))
    keep_c, send_c, keep_d, send_d = both_sums(keep_c, came_c, keep_d, came_d)
    came_c, came_d = swap(send_c, "seg", 2), swap(send_d, "seg", 1)
    _, came, parts_first[1] = lax.optimization_barrier((send_c, came, parts_first[1]))
    mine = add(keep, came)
    mine, *d_qkv = lax.optimization_barrier((mine, *d_qkv))
    came_l = swap(mine[1::2], "doc", 2)
    keep_y, send_y = quarter(1, keep_c, came_c, keep_d, came_d)
    _, came_l = lax.optimization_barrier((send_y, came_l))
    late = pair_sum(mine[0::2], came_l, add)
    parts_second = pair_sum(keep_y, swap(send_y, "doc", 2), plain_sum)
    grad_red, grad_out = rows_final(parts_first, (chunks * each, wide), (each, wide))

    back = trade(d_qkv)
    (grad_tokens,) = call(
        functools.partial(tokens_grad_kernel, slots=slots, n_seg=n_seg),
        [shape_of(slots, size, wide)],
        ((), hidden, query_proj, key_proj, value_proj, *back),
        3,
        far_out=(0,),
    )

    late[1], grad_red, grad_out, layer_out = lax.optimization_barrier((late[1], grad_red, grad_out, layer_out))
    mine = add(*late)
    parts = trade([mine[m] for m in range(n_seg)])
    grad_tokens, *parts = lax.optimization_barrier((grad_tokens, *parts))
    got = call(
        functools.partial(heads_final_kernel, n_seg=n_seg, mem=mem),
        [shape_of(each, wide, dtype=F32)] * 3
        + [shape_of(1, each, dtype=F32)] * EXP_B
        + [shape_of(1, chunks * each, dtype=F32), shape_of(mem, each, dtype=F32)],
        ((), *parts),
        1,
        far_out=range(5 + EXP_B),
    )
    (grad_exp,) = rows_final(parts_second, (each, hidden_units))
    grad_q, grad_k, grad_v = got[:3]
    flat = [v.reshape(-1) for v in got[3:-1]]

    return (
        layer_out,
        grad_tokens,
        got[-1],
        grad_q,
        flat[Q_B],
        grad_k,
        grad_v,
        flat[V_B],
        grad_out,
        flat[OUT_B],
        flat[ATTN_G],
        flat[ATTN_S],
        grad_exp,
        flat[EXP_B],
        grad_red,
        flat[RED_B],
        flat[FIN_G],
        flat[FIN_S],
    )


def solution(mesh):
    both = ("seg", "doc")
    data = P("doc", "seg", None)
    placed = (data, P("doc"), P("doc")) + (P(),) * 16 + (data,)
    vec, mat = P(both), P(both, None)
    return jax.shard_map(
        shards,
        mesh=mesh,
        in_specs=placed,
        out_specs=(
            data,
            data,
            P(None, both),
            mat,
            vec,
            mat,
            mat,
            vec,
            mat,
            vec,
            vec,
            vec,
            mat,
            vec,
            mat,
            vec,
            vec,
            vec,
        ),
        check_vma=False,
    )
```

```python
import functools

import jax
import jax.numpy as jnp
from jax import lax
from jax.experimental import pallas as pl
from jax.experimental.pallas import tpu as pltpu
from jax.sharding import PartitionSpec as P

HEADS = 12


EPS = 1e-12
NEG_FILL = -1e30
F32 = jnp.float32
BF16 = jnp.bfloat16
NN = (((1,), (0,)), ((), ()))
NT = (((1,), (1,)), ((), ()))
TN = (((0,), (0,)), ((), ()))

Q_B, V_B, OUT_B, ATTN_G, ATTN_S, RED_B, FIN_G, FIN_S, EXP_B = range(9)
N_VEC = 16
N_SMALL = 32


def mm(left, right, dims=NN):
    return lax.dot_general(left, right, dims, preferred_element_type=F32)


def swap(block, axis, mask):
    return lax.ppermute(block, axis, [(i, i ^ mask) for i in range(lax.axis_size(axis))])


FRESH, VALID = 0, 1


def flags_kernel(meta_ref, out_ref):
    new_ref, valid_ref = meta_ref
    out_ref[...] = jnp.zeros_like(out_ref)
    out_ref[FRESH : FRESH + 1] = jnp.full((1, out_ref.shape[1]), new_ref[1], jnp.int32)
    for t in range(2):
        out_ref[VALID + t : VALID + t + 1] = jnp.full((1, out_ref.shape[1]), valid_ref[t], jnp.int32)


def flag(flags_ref, i):
    return flags_ref[i : i + 1, 0:1]


def seg_here():
    return lax.axis_index("seg")


def core_here():
    return lax.axis_index("doc") & 1


def pair_here():
    return lax.axis_index("doc") >> 1


def shape_of(*dims, dtype=BF16):
    return jax.ShapeDtypeStruct(dims, dtype)


def call(kernel, out_shape, args, micros, far_in=(), far_out=(), scratch=()):
    vmem, far = pl.BlockSpec(memory_space=pltpu.VMEM), pl.BlockSpec(memory_space=pltpu.HBM)
    integers, *rest = args
    near = [
        pltpu.with_memory_space_constraint(x, pltpu.HBM if i in far_in else pltpu.VMEM) for i, x in enumerate(rest, 1)
    ]

    def body(*refs):
        kernel(refs[: len(integers)], *refs[len(integers) :])

    return pl.pallas_call(
        body,
        out_shape=[o if i in far_out else pltpu.VMEM(o.shape, o.dtype) for i, o in enumerate(out_shape)],
        in_specs=[pl.BlockSpec(memory_space=pltpu.SMEM)] * len(integers)
        + [far if i in far_in else vmem for i in range(1, len(args))],
        out_specs=[vmem] * len(out_shape),
        scratch_shapes=scratch,
        compiler_params=pltpu.CompilerParams(vmem_limit_bytes=8 << 20),
        cost_estimate=pl.CostEstimate(flops=0, transcendentals=0, bytes_accessed=int(micros * 3e6)),
    )(*integers, *near)


def reorder(x, seg, n_seg):
    width = x.shape[1] // n_seg
    bit = 1
    while bit < n_seg:
        moved = jnp.concatenate([x[:, (b ^ bit) * width : ((b ^ bit) + 1) * width] for b in range(n_seg)], axis=1)
        x = jnp.where((seg & bit) != 0, moved, x)
        bit *= 2
    return x


def in_loop(count, together, step):
    def some(j, carry):
        for k in range(together):
            step(j * together + k)
        return carry

    lax.fori_loop(0, count // together, some, 0)


def own_columns(x, seg, n_seg):
    width = x.shape[1] // n_seg
    out = x[:, :width]
    for b in range(1, n_seg):
        out = jnp.where(seg == b, x[:, b * width : (b + 1) * width], out)
    return out


def prep_kernel(meta_ref, wq_ref, wk_ref, wv_ref, *refs, n_seg, chunks):
    vec_refs, (w_ref, b_ref, out_ref, line_ref, near_ref, sems) = refs[: EXP_B + 1], refs[EXP_B + 1 :]
    weights = [
        pltpu.make_async_copy(r, near_ref.at[i], sems.at[EXP_B + 1 + i]) for i, r in enumerate((wq_ref, wk_ref, wv_ref))
    ]
    for c in weights:
        c.start()
    copies = [pltpu.make_async_copy(r, out_ref.at[i], sems.at[i]) for i, r in enumerate(vec_refs[:EXP_B])]
    copies.append(pltpu.make_async_copy(vec_refs[EXP_B], line_ref.at[0], sems.at[EXP_B]))
    for c in copies:
        c.start()
    seg = seg_here()
    rows = w_ref.shape[0] // 8
    width = w_ref.shape[1] // 3
    for c in weights:
        c.wait()

    def some_rows(i):
        these = pl.ds(pl.multiple_of(i * rows, rows), rows)
        for b in range(n_seg):

            @pl.when(seg == b)
            def _():
                cols = slice(b * width, (b + 1) * width)
                w_ref[these] = jnp.concatenate([near_ref[k, these, cols] for k in range(3)], axis=1)


    in_loop(8, 1, some_rows)
    for c in copies:
        c.wait()
    wide = out_ref.shape[1]
    for q in range(chunks):
        out_ref[EXP_B + q : EXP_B + q + 1] = line_ref[:, q * wide : (q + 1) * wide]
    q_b = own_columns(out_ref[Q_B : Q_B + 1], seg, n_seg)
    v_b = own_columns(out_ref[V_B : V_B + 1], seg, n_seg)
    b_ref[...] = jnp.concatenate([q_b, jnp.zeros_like(q_b), v_b], axis=1)


def qkv_kernel(meta_ref, w_ref, b_ref, *refs):
    rows, out_ref = refs[:-1], refs[-1]
    size = rows[0].shape[0]
    for b, r in enumerate(rows):
        out_ref[b * size : (b + 1) * size, :] = (mm(r[...], w_ref[...]) + b_ref[...]).astype(BF16)


def mask_block(meta_ref, slot, blocks, size, mem, width):
    total = blocks * size + 2 * mem
    row = lax.broadcasted_iota(jnp.int32, (total, width), 0)
    col = lax.broadcasted_iota(jnp.int32, (total, width), 1)
    place = row
    for b in range(blocks):
        inside = (row >= b * size) & (row < (b + 1) * size)
        place = jnp.where(inside, ((seg_here() ^ b) - b) * size + row, place)
    out = (place >= flag(meta_ref, VALID + slot)) & (row < blocks * size) & (col == 0)
    return jnp.where(out, NEG_FILL, 0.0).astype(BF16)


def ones_block(rows, width):
    col = lax.broadcasted_iota(jnp.int32, (rows, width), 1)
    return jnp.where(col == 0, 1.0, 0.0).astype(BF16)


def with_memory(rows, memory):
    return jnp.concatenate([rows, memory, memory], axis=0)


SCALE = 0.125 * 1.4426950408889634


def attn_fwd_kernel(_, meta_ref, qkv_ref, mem_ref, w_ref, b_ref, *outs, slot, blocks, heads, mem_queries):
    if mem_queries:
        memory = mem_ref[...]
    else:
        written_ref, outs = outs[0], outs[1:]
        memory = jnp.where(flag(meta_ref, FRESH) == 1, mem_ref[...], written_ref[...].astype(BF16))
        outs[-1][...] = memory
    mix_refs, lse_ref, mem_out_ref = outs[:blocks], outs[blocks], outs[blocks + 1]
    size = qkv_ref.shape[0] // blocks
    mem = mem_ref.shape[0]
    width = qkv_ref.shape[1] // 3
    head_dim = width // heads
    mem_out_ref[...] = (mm(memory, w_ref[...]) + b_ref[...]).astype(BF16)
    mask = mask_block(meta_ref, slot, blocks, size, mem, head_dim)
    ones = ones_block(size, head_dim)
    value_t = with_memory(qkv_ref[:, 2 * width :], mem_out_ref[:, 2 * width :]).T
    keys = []
    for h in range(heads):
        cols = slice(width + h * head_dim, width + (h + 1) * head_dim)
        keys.append(jnp.concatenate([with_memory(qkv_ref[:, cols], mem_out_ref[:, cols]), mask], axis=1))

    def mixed_of(queries, ones, first):
        out = []
        for h in range(heads):
            lo, hi = h * head_dim, (h + 1) * head_dim
            scores = mm(keys[h], jnp.concatenate([queries[:, lo:hi], ones], axis=1), NT)
            highest = jnp.max(scores, axis=0, keepdims=True)
            weights = jnp.exp2((scores - highest) * SCALE)
            total = jnp.sum(weights, axis=0, keepdims=True)
            out.append(mm(value_t[lo:hi], weights.astype(BF16)) * (1.0 / total))
            lse_ref[h : h + 1, first : first + queries.shape[0]] = highest * SCALE + jnp.log(total) * 1.4426950408889634
        return jnp.concatenate(out, axis=0).T.astype(BF16)

    def put(b, row, rows):
        half = mix_refs[b].shape[0]
        cut = max(0, min(rows.shape[0], half - row))
        if cut:
            mix_refs[b][row : row + cut, :width] = rows[:cut]
        if cut < rows.shape[0]:
            mix_refs[b][row + cut - half : row + rows.shape[0] - half, width:] = rows[cut:]

    for b in range(blocks):
        put(b, 0, mixed_of(qkv_ref[b * size : (b + 1) * size, :width], ones, b * size))
    if mem_queries:
        mixed = mixed_of(mem_out_ref[:, :width], ones[:mem], blocks * size)
        for b in range(blocks):
            put(b, size, mixed)


def attn_bwd_kernel(_, meta_ref, qkv_ref, mem_ref, lse_ref, *refs, slot, blocks, heads, mem_queries):
    n_grad = blocks + (1 if mem_queries else 0)
    grad_refs, refs = refs[:n_grad], refs[n_grad:]
    more_refs, out_refs, mem_out_ref = refs[: -blocks - 1], refs[-blocks - 1 : -1], refs[-1]
    for more_ref, out_ref in zip(more_refs, out_refs):
        out_ref[out_ref.shape[0] - more_ref.shape[0] :, :] = more_ref[...]
    size = qkv_ref.shape[0] // blocks
    mem = mem_ref.shape[0]
    width = qkv_ref.shape[1] // 3
    first = slot * width
    head_dim = width // heads
    own = blocks * size + mem
    mask = mask_block(meta_ref, slot, blocks, size, mem, head_dim)
    ones = ones_block(size, head_dim)
    key_t = with_memory(qkv_ref[:, width : 2 * width], mem_ref[:, width : 2 * width]).T
    grad_q = [[] for _ in range(n_grad)]
    for h in range(heads):
        lo, hi = h * head_dim, (h + 1) * head_dim
        key = with_memory(qkv_ref[:, width + lo : width + hi], mem_ref[:, width + lo : width + hi])
        key = jnp.concatenate([key, mask], axis=1)
        value = with_memory(qkv_ref[:, 2 * width + lo : 2 * width + hi], mem_ref[:, 2 * width + lo : 2 * width + hi])

        def one(query, ones, grad, lse):
            scores = mm(key, jnp.concatenate([query, ones], axis=1), NT)
            probs = jnp.exp2(scores * SCALE - lse)
            grad_probs = mm(value, grad, NT)
            inner = jnp.sum(grad_probs * probs, axis=0, keepdims=True)
            return (probs * (grad_probs - inner)).astype(BF16), probs.astype(BF16)

        queries, grads, scores_g, probs = [], [], [], []
        for b in range(blocks):
            queries.append(qkv_ref[b * size : (b + 1) * size, lo:hi])
            grads.append(grad_refs[b][:, first + lo : first + hi])
            g, p = one(queries[b], ones, grads[b], lse_ref[h : h + 1, b * size : (b + 1) * size])
            scores_g.append(g)
            probs.append(p)
            grad_q[b].append(mm(key_t[lo:hi], g) * 0.125)
        grad_key = mm(jnp.concatenate([g[:own] for g in scores_g], axis=1), jnp.concatenate(queries, axis=0))
        grad_value = mm(jnp.concatenate([p[:own] for p in probs], axis=1), jnp.concatenate(grads, axis=0))
        if mem_queries:
            query, grad = mem_ref[:, lo:hi], grad_refs[blocks][:, lo:hi]
            g, p = one(query, ones[:mem], grad, lse_ref[h : h + 1, blocks * size : own])
            grad_q[blocks].append(mm(key_t[lo:hi], g) * 0.125)
            grad_key = grad_key + mm(g[:own], query)
            grad_value = grad_value + mm(p[:own], grad)
        grad_key = (grad_key * 0.125).astype(BF16)
        grad_value = grad_value.astype(BF16)
        for b in range(blocks):
            out_refs[b][:size, width + lo : width + hi] = grad_key[b * size : (b + 1) * size]
            out_refs[b][:size, 2 * width + lo : 2 * width + hi] = grad_value[b * size : (b + 1) * size]
        mem_out_ref[:, width + lo : width + hi] = grad_key[blocks * size :]
        mem_out_ref[:, 2 * width + lo : 2 * width + hi] = grad_value[blocks * size :]
    for b in range(blocks):
        out_refs[b][:size, :width] = jnp.concatenate(grad_q[b], axis=0).T.astype(BF16)
    if mem_queries:
        mem_out_ref[:, :width] = jnp.concatenate(grad_q[blocks], axis=0).T.astype(BF16)
    else:
        mem_out_ref[:, :width] = jnp.zeros((mem, width), BF16)


def norm_parts(hidden):
    center = hidden - jnp.mean(hidden, axis=-1, keepdims=True)
    inverse = lax.rsqrt(jnp.mean(center * center, axis=-1, keepdims=True) + EPS)
    return center * inverse, inverse


def norm_back(grad, gain, unit, inverse):
    scaled = grad * gain
    mean_scaled = jnp.mean(scaled, axis=-1, keepdims=True)
    mean_product = jnp.mean(scaled * unit, axis=-1, keepdims=True)
    return inverse * (scaled - mean_scaled - unit * mean_product)


def gelu_and_slope(pre):
    cdf = 0.5 * (1.0 + lax.erf(pre * (2.0**-0.5)))
    density = jnp.exp(-0.5 * pre * pre) * 0.3989422804014327
    return pre * cdf, cdf + pre * density


N_KEPT = 4


def rows_fwd_kernel(meta_ref, *refs, n_seg, n_pair, n_hidden, together):
    mix_refs, hid_refs = refs[:n_seg], refs[n_seg : n_seg + n_hidden]
    vec_ref, out_ref, exp_ref, red_ref = refs[n_seg + n_hidden : n_seg + n_hidden + 4]
    outs = refs[n_seg + n_hidden + 4 :]
    unit_a_ref, inv_ref, slope_ref, unit_f_ref = outs[:N_KEPT]
    result_refs, left_refs, acc_ref = outs[N_KEPT : N_KEPT + n_hidden], outs[N_KEPT + n_hidden : -1], outs[-1]
    wide = out_ref.shape[0]
    size = hid_refs[0].shape[0]

    def vec(i):
        return vec_ref[i : i + 1]

    def keep_left(x, at, first, blocks):
        left_factors(meta_ref, x, left_refs, at, first, blocks, n_seg, n_pair, size)

    each = wide // (n_seg * n_pair * 2)
    width = mix_refs[0].shape[1] // 2
    halves = [
        jnp.concatenate([r[:, i * width : (i + 1) * width] for r in mix_refs], axis=1).astype(F32) for i in range(2)
    ]
    mixed = reorder(jnp.concatenate(halves, axis=0).astype(BF16), seg_here(), n_seg)
    hidden = jnp.concatenate([r[...].astype(F32) for r in hid_refs], axis=0)
    unit, inverse = norm_parts(hidden + (mm(mixed, out_ref[...]) + vec(OUT_B)))
    unit_a_ref[...] = unit
    inv_ref[:, 0:1] = inverse
    normed = unit * vec(ATTN_G) + vec(ATTN_S)
    low = normed.astype(BF16)
    chunks = exp_ref.shape[1] // wide
    acc_ref[...] = normed + vec(RED_B)

    def chunk(q):
        cols = pl.ds(pl.multiple_of(q * wide, wide), wide)
        active, slope = gelu_and_slope(mm(low, exp_ref[:, cols]) + vec_ref[pl.ds(EXP_B + q, 1)])
        slope_ref[:, cols] = slope
        active = active.astype(BF16)
        acc_ref[...] += mm(active, red_ref[cols])
        keep_left(active, each, q * (n_seg // chunks), n_seg // chunks)

    in_loop(chunks, together, chunk)
    unit, inverse = norm_parts(acc_ref[...])
    unit_f_ref[...] = unit
    inv_ref[:, 1:2] = inverse
    result = unit * vec(FIN_G) + vec(FIN_S)
    at = 0
    for r in result_refs:
        r[...] = result[at : at + r.shape[0]].astype(r.dtype)
        at += r.shape[0]
    keep_left(low, 0, 0, n_seg)
    keep_left(mixed, (chunks + 1) * each, 0, n_seg)


def left_factors(meta_ref, x, left_refs, at, first, blocks, n_seg, n_pair, size):
    seg, core, pair = seg_here(), core_here(), pair_here()
    rows = x.shape[1] // (blocks * n_pair * 2)
    keep_ref, send_ref = left_refs[:2]
    keep, send = core_halves(x[:size].astype(F32).T, core, n_pair, rows)
    for s in range(blocks):
        for z in range(n_pair):
            keep_ref[(first + s) ^ seg, z ^ pair, at : at + rows] = keep[s * n_pair + z]
            send_ref[(first + s) ^ seg, z ^ pair, at : at + rows] = send[s * n_pair + z]
    if left_refs[2:]:
        keep_ref, send_ref = left_refs[2:]
        mine = x[size:].astype(F32)
        if blocks > 1:
            assert blocks == n_seg
            mine = own_columns(mine, seg, n_seg)
        keep, send = core_halves(mine.T, core, n_pair, rows)

        @pl.when((seg == first) | (blocks > 1))
        def _():
            for z in range(n_pair):
                keep_ref[z ^ pair, at : at + rows] = keep[z]
                send_ref[z ^ pair, at : at + rows] = send[z]


def core_halves(x, core, pairs, rows):
    x = x.reshape(x.shape[0] // (2 * rows), 2, rows, x.shape[1])
    even, odd = x[:, 0], x[:, 1]
    return jnp.where(core == 0, even, odd).astype(BF16), jnp.where(core == 0, odd, even).astype(BF16)


def rows_back(seg, n_seg, grad, kept, vec_ref, out_ref, exp_ref, red_ref, outs, acc_ref, together):
    right_ref, hidden_ref, small_ref = outs
    wide = hidden_ref.shape[1]
    chunks = exp_ref.shape[1] // wide

    def vec(i):
        return vec_ref[i : i + 1]

    def total(x):
        return jnp.sum(x, axis=0, keepdims=True)

    unit = kept(3)
    grad_sum = norm_back(grad, vec(FIN_G), unit, kept(1)[:, 1:2])
    low = grad_sum.astype(BF16)
    right_ref[:, chunks * wide : (chunks + 1) * wide] = low
    small_ref[...] = jnp.zeros_like(small_ref)
    small_ref[FIN_G : FIN_G + 1] = total(grad * unit)
    small_ref[FIN_S : FIN_S + 1] = total(grad)
    small_ref[RED_B : RED_B + 1] = total(low.astype(F32))
    acc_ref[...] = grad_sum

    def chunk(q):
        cols = pl.ds(pl.multiple_of(q * wide, wide), wide)
        grad_pre = (mm(low, red_ref[cols], NT) * kept(2, cols)).astype(BF16)
        right_ref[:, cols] = grad_pre
        small_ref[pl.ds(EXP_B + q, 1)] = total(grad_pre.astype(F32))
        acc_ref[...] += mm(grad_pre, exp_ref[:, cols], NT)

    in_loop(chunks, together, chunk)
    acc = acc_ref[...]
    unit = kept(0)
    small_ref[ATTN_G : ATTN_G + 1] = total(acc * unit)
    small_ref[ATTN_S : ATTN_S + 1] = total(acc)
    grad_hidden = norm_back(acc, vec(ATTN_G), unit, kept(1)[:, 0:1])
    hidden_ref[...] = grad_hidden
    low = grad_hidden.astype(BF16)
    right_ref[:, (chunks + 1) * wide :] = low
    small_ref[OUT_B : OUT_B + 1] = total(low.astype(F32))
    return reorder(mm(low, out_ref[...], NT).astype(BF16), seg, n_seg)


def token_rows_back_kernel(meta_ref, grad_ref, *refs, slots, n_seg):
    kept_refs = [refs[t * N_KEPT : (t + 1) * N_KEPT] for t in range(slots)]
    refs = refs[slots * N_KEPT :]
    (vec_ref, out_ref, exp_ref, red_ref), outs, mix_refs, acc_ref = refs[:4], refs[4:7], refs[7:-1], refs[-1]
    size = grad_ref.shape[1]

    def kept(i, cols=slice(None)):
        return jnp.concatenate([kept_refs[t][i][:size, cols] for t in range(slots)], axis=0)

    grad = jnp.concatenate([grad_ref[t].astype(F32) for t in range(slots)], axis=0)
    mixed = rows_back(seg_here(), n_seg, grad, kept, vec_ref, out_ref, exp_ref, red_ref, outs, acc_ref, 4)
    width = mixed.shape[1] // n_seg
    for m in range(n_seg):
        for t in range(slots):
            mix_refs[m][:, t * width : (t + 1) * width] = mixed[t * size : (t + 1) * size, m * width : (m + 1) * width]


def memory_rows_back_kernel(_, meta_ref, *refs, n_seg, size):
    d_refs, refs = refs[:n_seg], refs[n_seg:]
    (wk_ref, wv_ref), kept_refs, refs = refs[:2], refs[2 : 2 + N_KEPT], refs[2 + N_KEPT :]
    (vec_ref, out_ref, exp_ref, red_ref), outs, (memory_ref, own_ref, acc_ref) = refs[:4], refs[4:7], refs[7:]
    seg = seg_here()
    width = d_refs[0].shape[1] // 2
    d_key = reorder(jnp.concatenate([r[:, :width] for r in d_refs], axis=1), seg, n_seg)
    d_value = reorder(jnp.concatenate([r[:, width:] for r in d_refs], axis=1), seg, n_seg)
    grad = 2.0 * (mm(d_key, wk_ref[...], NT) + mm(d_value, wv_ref[...], NT))
    memory_ref[...] = grad
    grad = jnp.where(flag(meta_ref, FRESH) == 1, jnp.zeros_like(grad), grad)

    def kept(i, cols=slice(None)):
        return kept_refs[i][size:, cols]

    mixed = rows_back(seg, n_seg, grad, kept, vec_ref, out_ref, exp_ref, red_ref, outs, acc_ref, 1)
    own_ref[...] = mixed[:, : own_ref.shape[1]]


def tokens_grad_kernel(meta_ref, hidden_ref, wq_ref, wk_ref, wv_ref, *refs, slots, n_seg):
    d_refs, out_ref = refs[:-1], refs[-1]
    size = out_ref.shape[1]
    width = d_refs[0].shape[1] // 3
    seg = seg_here()

    def slot(t):
        these = pl.ds(pl.multiple_of(t * size, size), size)
        grad = hidden_ref[these]
        for i, w_ref in enumerate((wq_ref, wk_ref, wv_ref)):
            part = jnp.concatenate([r[these, i * width : (i + 1) * width] for r in d_refs], 1)
            grad = grad + mm(reorder(part, seg, n_seg), w_ref[...], NT)
        out_ref[t] = grad.astype(BF16)

    in_loop(slots, 1, slot)


def row_parts(stream, chunks, each):
    if stream == 1:
        return [(0, each, q, q * each) for q in range(chunks)]
    return [(each, chunks * each, chunks, 0), ((chunks + 1) * each, each, chunks + 1, chunks * each)]


def rows_weights_kernel(meta_ref, *refs, stream, n_seg, n_pair, each):
    left_refs, (right_ref, other_ref), outs = refs[:-6], refs[-6:-4], refs[-4:]
    wide = outs[0].shape[3]
    half = n_pair // 2
    for lo, rows, q, row in row_parts(stream, right_ref.shape[1] // wide - 2, each):
        left = jnp.concatenate(
            [r[:, :, lo : lo + rows].reshape(n_seg * n_pair * rows, r.shape[3]) for r in left_refs], axis=1
        )
        right = jnp.concatenate([r[:, q * wide : (q + 1) * wide] for r in (right_ref, other_ref)], axis=0)
        full = mm(left, right).reshape(n_seg, n_pair, rows, wide).astype(BF16)
        for s in range(n_seg):
            low, high = s & 1, s >> 1
            outs[low][high, :, row : row + rows] = full[s, :half]
            outs[2 + high][low, :, row : row + rows] = full[s, half:]


def quarter_kernel(meta_ref, left_ref, left2_ref, right_ref, right2_ref, *refs, stream, each):
    half_refs, outs = (refs[:2], refs[2:4]), refs[4:]
    wide = outs[0].shape[2]
    pairs = left_ref.shape[0]
    half = pairs // 2
    for lo, rows, q, row in row_parts(stream, right_ref.shape[1] // wide - 2, each):

        def rows_of(r):
            return jnp.concatenate([r[z].astype(F32)[lo : lo + rows] for z in range(pairs)], axis=0)

        left = jnp.concatenate([rows_of(left_ref), rows_of(left2_ref)], axis=1).astype(BF16)
        right = jnp.concatenate([r[:, q * wide : (q + 1) * wide] for r in (right_ref, right2_ref)], axis=0)
        part = mm(left, right).reshape(pairs, rows, wide)
        for z in range(pairs):
            total = part[z]
            for r in half_refs[z // half]:
                total = total + r[z % half, row : row + rows].astype(F32)
            outs[z & 1][z >> 1, row : row + rows] = total.astype(BF16)


def heads_weights_kernel(_, meta_ref, small_ref, small_m_ref, hid_ref, memory_ref, w_ref, *refs, slots, n_seg):
    rows, refs = refs[: slots * n_seg], refs[slots * n_seg :]
    grads, (mem0_ref, mem1_ref, dm0_ref, dm1_ref, keep_ref, send_ref) = refs[:n_seg], refs[n_seg:]
    seg, core, pair, fresh1 = seg_here(), core_here(), pair_here(), flag(meta_ref, FRESH)
    wide = rows[0].shape[1]
    width = wide // n_seg
    each = keep_ref.shape[2]
    col = lax.broadcasted_iota(jnp.int32, (1, 3 * width), 1)
    twice = jnp.where(col < width, 1.0, 2.0)
    dm0 = (dm0_ref[...].astype(F32) * twice).astype(BF16)
    dm1 = (dm1_ref[...].astype(F32) * twice).astype(BF16)
    full = mm(mem0_ref[...], dm0, TN) + mm(mem1_ref[...], dm1, TN)
    sums = jnp.sum(dm0.astype(F32), axis=0, keepdims=True) + jnp.sum(dm1.astype(F32), axis=0, keepdims=True)
    for m, g in enumerate(grads):
        x = jnp.concatenate([r[...] for r in rows[m::n_seg]], axis=0)
        full = full + mm(x, g[...], TN)
        sums = sums + jnp.sum(g[...].astype(F32), axis=0, keepdims=True)
    grad_mem = mm(dm0, w_ref[...], NT)
    whole = hid_ref[...] + jnp.where(fresh1 == 1, memory_ref[...], 0.0)
    grad_mem = grad_mem + jnp.where(seg == 0, whole, 0.0)

    def placed(v):
        return reorder(jnp.concatenate([v, jnp.zeros((1, wide - width), F32)], axis=1), seg, n_seg)

    n_pair = keep_ref.shape[0]
    chunks = 4
    head = EXP_B + chunks
    given = small_ref[...] + jnp.where(seg == 0, small_m_ref[...], 0.0)
    small = jnp.concatenate(
        [
            placed(sums[:, :width]),
            placed(sums[:, 2 * width :]),
            given[2:head],
            grad_mem,
            jnp.zeros((N_SMALL - head - grad_mem.shape[0], wide), F32),
        ],
        axis=0,
    ).T
    turned = small.reshape(wide // (chunks * each), chunks, each, N_SMALL)
    spread = [
        jnp.concatenate(
            [turned[:, k, :, EXP_B + q : EXP_B + q + 1].reshape(wide // chunks, 1) for k in range(chunks)], axis=1
        )
        for q in range(chunks)
    ]
    small = jnp.concatenate([small[:, :EXP_B], jnp.concatenate(spread, axis=0), small[:, head:]], axis=1)
    high = small.astype(BF16)
    rest = (small - high.astype(F32)).astype(BF16)
    full = jnp.concatenate([full, high.astype(F32), rest.astype(F32)], axis=1)
    keep, send = core_halves(full, core, n_pair, each)
    for s in range(n_seg):
        for z in range(n_pair):
            keep_ref[z ^ pair, s ^ seg] = keep[s * n_pair + z]
            send_ref[z ^ pair, s ^ seg] = send[s * n_pair + z]


def late_sum(*parts, at):
    total = sum(p.astype(F32) for p in parts)
    small = total[..., at : at + N_SMALL] + total[..., at + N_SMALL :]
    high = small.astype(BF16)
    rest = (small - high.astype(F32)).astype(BF16)
    return jnp.concatenate([total[..., :at].astype(BF16), high, rest], axis=-1)


def heads_final_kernel(meta_ref, *refs, n_seg, mem):
    ins, outs = refs[:n_seg], refs[n_seg:]
    seg = seg_here()
    width = outs[0].shape[1] // n_seg
    total = [r[...].astype(F32) for r in ins]
    for i in range(3):
        outs[i][...] = reorder(
            jnp.concatenate([total[m][:, i * width : (i + 1) * width] for m in range(n_seg)], axis=1), seg, n_seg
        )
    at = 3 * width
    small = sum(t[:, at : at + N_SMALL] + t[:, at + N_SMALL : at + 2 * N_SMALL] for t in total).T
    vec_refs, exp_ref, mem_ref = outs[3 : 3 + EXP_B], outs[3 + EXP_B], outs[4 + EXP_B]
    for i, r in enumerate(vec_refs):
        r[...] = small[i : i + 1]
    exp_ref[...] = jnp.concatenate([small[EXP_B + q : EXP_B + q + 1] for q in range(4)], axis=1)
    mem_ref[...] = small[EXP_B + 4 : EXP_B + 4 + mem]


def rows_final_kernel(meta_ref, first_ref, second_ref, *outs):
    total = first_ref[...].astype(F32) + second_ref[...].astype(F32)
    wide = total.shape[1]
    at = 0
    for r in outs:
        for q in range(r.shape[1] // wide):
            r[:, q * wide : (q + 1) * wide] = total[at : at + r.shape[0]]
            at += r.shape[0]


def shards(
    tokens,
    new_doc,
    valid_len,
    mem_init,
    query_proj,
    query_bias,
    key_proj,
    value_proj,
    value_bias,
    output_proj,
    output_bias,
    attn_gain,
    attn_shift,
    expand_proj,
    expand_bias,
    reduce_proj,
    reduce_bias,
    final_gain,
    final_shift,
    d_out,
):
    slots, size, wide = tokens.shape
    assert slots == 2
    n_seg, n_doc = lax.axis_size("seg"), lax.axis_size("doc")
    n_pair = n_doc // 2
    hidden_units = expand_proj.shape[1]
    chunks = hidden_units // wide
    assert chunks == 4
    mem = mem_init.shape[0]
    width = wide // n_seg
    heads = HEADS // n_seg
    others = range(1, n_seg)
    all_rows = n_seg * size

    rows0 = [tokens[0]] + [swap(tokens[0], "seg", m) for m in others]
    (flags,) = call(flags_kernel, [shape_of(8, 128, dtype=jnp.int32)], ((new_doc, valid_len),), 1)
    w_own, b_own, vecs = call(
        functools.partial(prep_kernel, n_seg=n_seg, chunks=chunks),
        [shape_of(wide, 3 * width), shape_of(1, 3 * width, dtype=F32), shape_of(N_VEC, wide, dtype=F32)],
        (
            (),
            query_proj,
            key_proj,
            value_proj,
            query_bias,
            value_bias,
            output_bias,
            attn_gain,
            attn_shift,
            reduce_bias,
            final_gain,
            final_shift,
            expand_bias,
        ),
        4,
        far_in=range(1, 5 + EXP_B),
        scratch=[
            pltpu.VMEM((1, hidden_units), F32),
            pltpu.VMEM((3, wide, wide), BF16),
            pltpu.SemaphoreType.DMA((EXP_B + 4,)),
        ],
    )

    second, w_own, flags = lax.optimization_barrier((tokens[1], w_own, flags))
    rows = [rows0, [second] + [swap(second, "seg", m) for m in others]]

    def project(t):
        (out,) = call(qkv_kernel, [shape_of(all_rows, 3 * width)], ((), w_own, b_own, *rows[t]), 3)
        return out

    def attend(t, qkv, written=()):
        mem_queries = not written
        got = call(
            functools.partial(attn_fwd_kernel, slot=t, blocks=n_seg, heads=heads, mem_queries=mem_queries),
            [shape_of((size + (mem if mem_queries else 0)) // 2, 2 * width)] * n_seg
            + [shape_of(8, all_rows + 128, dtype=F32), shape_of(mem, 3 * width)]
            + [shape_of(mem, wide)] * len(written),
            ((), flags, qkv, mem_init, w_own, b_own, *written),
            8,
        )
        return list(got[:n_seg]), *got[n_seg:]

    def attend_back(t, qkv, qkv_mem, lse, grads, more=()):
        got = call(
            functools.partial(attn_bwd_kernel, slot=t, blocks=n_seg, heads=heads, mem_queries=len(grads) > n_seg),
            [shape_of(size * (2 if more else 1), 3 * width)] * n_seg + [shape_of(mem, 3 * width)],
            ((), flags, qkv, qkv_mem, lse, *grads, *more),
            8,
        )
        return list(got[:n_seg]), got[n_seg]

    def trade(blocks):
        came = {m: swap(blocks[m], "seg", m) for m in reversed(others)}
        return [blocks[0]] + [came[m] for m in others]

    weights = (vecs, output_proj, expand_proj, reduce_proj)
    each = wide // (n_seg * n_doc)

    def rows_forward(mixed, hidden, result_shapes):
        n_rows = sum(h.shape[0] for h in hidden)
        left = [shape_of(n_seg, n_pair, (chunks + 2) * each, size)] * 2
        if len(hidden) > 1:
            left += [shape_of(n_pair, (chunks + 2) * each, mem)] * 2
        got = call(
            functools.partial(
                rows_fwd_kernel, n_seg=n_seg, n_pair=n_pair, n_hidden=len(hidden), together=1 if len(hidden) > 1 else 4
            ),
            [
                shape_of(n_rows, wide, dtype=F32),
                shape_of(n_rows, 128, dtype=F32),
                shape_of(n_rows, hidden_units, dtype=F32),
                shape_of(n_rows, wide, dtype=F32),
                *result_shapes,
                *left,
            ],
            ((), *mixed, *hidden, *weights),
            8,
            scratch=[pltpu.VMEM((n_rows, wide), F32)],
        )
        return got[:N_KEPT], got[N_KEPT : N_KEPT + len(hidden)], got[N_KEPT + len(hidden) :]

    qkv0 = project(0)
    mixed0, lse0, qkv_mem0 = attend(0, qkv0)
    mixed0[0], *rows[1] = lax.optimization_barrier((mixed0[0], *rows[1]))
    qkv1 = project(1)
    mixed0 = trade(mixed0)
    qkv1, mixed0[0] = lax.optimization_barrier((qkv1, mixed0[0]))
    kept0, (layer0, written), (left0, left0_send, left_m, left_m_send) = rows_forward(
        mixed0, (tokens[0], mem_init), [shape_of(size, wide), shape_of(mem, wide, dtype=F32)]
    )
    mixed1, lse1, qkv_mem1, memory1 = attend(1, qkv1, (written,))
    left0_other, left_m_other = swap(left0_send, "doc", 1), swap(left_m_send, "doc", 1)
    mixed1[0], left0_other = lax.optimization_barrier((mixed1[0], left0_other))
    kept1, (layer1,), (left1, left1_send) = rows_forward(trade(mixed1), (tokens[1],), [shape_of(size, wide)])
    left1_other = swap(left1_send, "doc", 1)
    layer_out = jnp.stack([layer0, layer1])

    def back_shapes(n_rows):
        return [
            shape_of(n_rows, hidden_units + 2 * wide),
            shape_of(n_rows, wide, dtype=F32),
            shape_of(N_VEC, wide, dtype=F32),
        ]

    n_rows = slots * size
    got = call(
        functools.partial(token_rows_back_kernel, slots=slots, n_seg=n_seg),
        back_shapes(n_rows) + [shape_of(size, slots * width)] * n_seg,
        ((), d_out, *kept0, *kept1, *weights),
        10,
        scratch=[pltpu.VMEM((n_rows, wide), F32)],
    )
    right, hidden, small = got[:3]
    grads = trade(got[3:])
    right_other = swap(right, "doc", 1)
    right, left1_other = lax.optimization_barrier((right, left1_other))

    def plain_sum(*parts):
        return sum(p.astype(F32) for p in parts).astype(BF16)

    share = [(chunks + 1) * each, chunks * each]

    def row_weights(stream, right_other):
        return call(
            functools.partial(rows_weights_kernel, stream=stream, n_seg=n_seg, n_pair=n_pair, each=each),
            [shape_of(n_seg // 2, n_pair // 2, share[stream], wide)] * 4,
            ((), left0, left1, left0_other, left1_other, right, right_other),
            2,
        )

    def both_sums(keep_a, came_a, keep_b, came_b):
        return [plain_sum(k[i], c[i]) for k, c in ((keep_a, came_a), (keep_b, came_b)) for i in range(2)]

    keep_a, send_a, keep_b, send_b = row_weights(0, right_other)
    send_a, send_b, *grads = lax.optimization_barrier((send_a, send_b, *grads))
    came_a, came_b = swap(send_a, "seg", 1), swap(send_b, "seg", 2)
    d_qkv1, d_mem1 = attend_back(1, qkv1, qkv_mem1, lse1, grads)
    d_mem1_all = trade([d_mem1[:, width:]] * n_seg)

    right_other, d_mem1_all[0] = lax.optimization_barrier((right_other, d_mem1_all[0]))
    keep_c, send_c, keep_d, send_d = row_weights(1, right_other)
    send_c, send_d, came_a, came_b, *d_mem1_all = lax.optimization_barrier(
        (send_c, send_d, came_a, came_b, *d_mem1_all)
    )
    keep_a, send_a, keep_b, send_b = both_sums(keep_a, came_a, keep_b, came_b)
    send_a, send_b, d_mem1_all[0] = lax.optimization_barrier((send_a, send_b, d_mem1_all[0]))
    came_a, came_b = swap(send_a, "seg", 2), swap(send_b, "seg", 1)

    got = call(
        functools.partial(memory_rows_back_kernel, n_seg=n_seg, size=size),
        back_shapes(mem) + [shape_of(mem, wide, dtype=F32), shape_of(mem, width)],
        ((), flags, *d_mem1_all, key_proj, value_proj, *kept0, *weights),
        6,
        scratch=[pltpu.VMEM((mem, wide), F32)],
    )
    right_m, hidden_m, small_m, memory1_grad, mixed_m = got
    right_m_other = swap(right_m, "doc", 1)
    def pair_sum(keep, came, add):
        bit = 2
        while keep.shape[0] > 1:
            bit *= 2
            if keep.shape[0] == 2:
                (keep, send) = [add(keep[i : i + 1], came[i : i + 1]) for i in range(2)]
            else:
                both = add(keep, came)
                keep, send = both[0::2], both[1::2]
            came = swap(send, "doc", bit)
        return [keep[0], came[0]]

    def quarter(stream, *halves):
        keep, send = call(
            functools.partial(quarter_kernel, stream=stream, each=each),
            [shape_of(n_pair // 2, share[stream], wide)] * 2,
            ((), left_m, left_m_other, right_m, right_m_other, *halves),
            1,
        )
        return keep, send

    right_m, came_a, came_b, send_c, send_d = lax.optimization_barrier((right_m, came_a, came_b, send_c, send_d))
    came_c, came_d = swap(send_c, "seg", 1), swap(send_d, "seg", 2)
    keep_x, send_x = quarter(0, keep_a, came_a, keep_b, came_b)
    send_x, mixed_m = lax.optimization_barrier((send_x, mixed_m))
    came_x = swap(send_x, "doc", 2)
    d_qkv, d_mem0 = attend_back(0, qkv0, qkv_mem0, lse0, [*grads, mixed_m], d_qkv1)

    came_x, d_mem0 = lax.optimization_barrier((came_x, d_mem0))
    parts_first = pair_sum(keep_x, came_x, plain_sum)

    columns = 3 * width + 2 * N_SMALL
    keep, send = call(
        functools.partial(heads_weights_kernel, slots=slots, n_seg=n_seg),
        [shape_of(n_pair, n_seg, each, columns)] * 2,
        (
            (),
            flags,
            small,
            small_m,
            hidden_m,
            memory1_grad,
            w_own,
            *rows[0],
            *rows[1],
            *d_qkv,
            mem_init,
            memory1,
            d_mem0,
            d_mem1,
        ),
        6,
    )

    def rows_final(parts, *shapes):
        return call(
            rows_final_kernel,
            [shape_of(*dims, dtype=F32) for dims in shapes],
            ((), *parts),
            1,
            far_out=range(len(shapes)),
        )

    add = functools.partial(late_sum, at=3 * width)
    came = swap(send, "doc", 1)
    came_c, came_d, keep = lax.optimization_barrier((came_c, came_d, keep))
    keep_c, send_c, keep_d, send_d = both_sums(keep_c, came_c, keep_d, came_d)
    came_c, came_d = swap(send_c, "seg", 2), swap(send_d, "seg", 1)
    _, came, parts_first[1] = lax.optimization_barrier((send_c, came, parts_first[1]))
    mine = add(keep, came)
    mine, *d_qkv = lax.optimization_barrier((mine, *d_qkv))
    came_l = swap(mine[1::2], "doc", 2)
    keep_y, send_y = quarter(1, keep_c, came_c, keep_d, came_d)
    _, came_l = lax.optimization_barrier((send_y, came_l))
    late = pair_sum(mine[0::2], came_l, add)
    parts_second = pair_sum(keep_y, swap(send_y, "doc", 2), plain_sum)
    grad_red, grad_out = rows_final(parts_first, (chunks * each, wide), (each, wide))

    back = trade(d_qkv)
    (grad_tokens,) = call(
        functools.partial(tokens_grad_kernel, slots=slots, n_seg=n_seg),
        [shape_of(slots, size, wide)],
        ((), hidden, query_proj, key_proj, value_proj, *back),
        3,
        far_out=(0,),
    )

    late[1], grad_red, grad_out, layer_out = lax.optimization_barrier((late[1], grad_red, grad_out, layer_out))
    mine = add(*late)
    parts = trade([mine[m] for m in range(n_seg)])
    grad_tokens, *parts = lax.optimization_barrier((grad_tokens, *parts))
    got = call(
        functools.partial(heads_final_kernel, n_seg=n_seg, mem=mem),
        [shape_of(each, wide, dtype=F32)] * 3
        + [shape_of(1, each, dtype=F32)] * EXP_B
        + [shape_of(1, chunks * each, dtype=F32), shape_of(mem, each, dtype=F32)],
        ((), *parts),
        1,
        far_out=range(5 + EXP_B),
    )
    (grad_exp,) = rows_final(parts_second, (each, hidden_units))
    grad_q, grad_k, grad_v = got[:3]
    flat = [v.reshape(-1) for v in got[3:-1]]

    return (
        layer_out,
        grad_tokens,
        got[-1],
        grad_q,
        flat[Q_B],
        grad_k,
        grad_v,
        flat[V_B],
        grad_out,
        flat[OUT_B],
        flat[ATTN_G],
        flat[ATTN_S],
        grad_exp,
        flat[EXP_B],
        grad_red,
        flat[RED_B],
        flat[FIN_G],
        flat[FIN_S],
    )


def solution(mesh):
    both = ("seg", "doc")
    data = P("doc", "seg", None)
    placed = (data, P("doc"), P("doc")) + (P(),) * 16 + (data,)
    vec, mat = P(both), P(both, None)
    return jax.shard_map(
        shards,
        mesh=mesh,
        in_specs=placed,
        out_specs=(
            data,
            data,
            P(None, both),
            mat,
            vec,
            mat,
            mat,
            vec,
            mat,
            vec,
            vec,
            vec,
            mat,
            vec,
            mat,
            vec,
            vec,
            vec,
        ),
        check_vma=False,
    )
```
